256 devices in a mesh: gx: 4 (over x), gy: 4 (over z_lo, core), gz: 16 (over z_hi, y).
Axes of the slice: x: 4, y: 4, z: 8 (z_hi: 4, z_lo: 2; z = z_hi * 2 + z_lo), core: 2. Of those that a mesh axis runs over, the one named last changes fastest.
Arguments:
- flow_adjoint: float32 [19, 64, 64, 2048], P(None, 'gx', 'gy', 'gz'), may hold values from -6 to 6
- solute_adjoint: float32 [7, 64, 64, 2048], P(None, 'gx', 'gy', 'gz'), may hold values from -6 to 6
- flow_density: bfloat16 [4, 64, 64, 2048], P(None, 'gx', 'gy', 'gz'), may hold values from 0.796875 to 1.25
- flow_velocity: bfloat16 [4, 3, 64, 64, 2048], P(None, None, 'gx', 'gy', 'gz'), may hold values from -0.119628906 to 0.119628906
- solute_level: bfloat16 [4, 64, 64, 2048], P(None, 'gx', 'gy', 'gz'), may hold values from 0.099609375 to 3
- solid: int32 [64, 64, 2048], P('gx', 'gy', 'gz'), may hold values 0 or 1
- owner: int32 [64], replicated, may hold values from 0 to 15, as said below
Outputs:
- flow_result: float32 [19, 64, 64, 2048], P(None, 'gx', 'gy', 'gz')
- solute_result: float32 [7, 64, 64, 2048], P(None, 'gx', 'gy', 'gz')
The draws below stay inside these ranges and needn't reach their ends.
Inputs may be any that keep to these rules, and one draw needn't show every extreme that they name: owner never falls along the list; every gz device holds 1 to 7 blocks.
All inputs are finite; a program needn't handle non-finite values. No bound on the sum of `solid` on one device may be relied on, other than what follows from the above.
Results may differ from the reference program's by a relative error of at most 0.0003.
Values sent between devices are 32-bit elements; how exact they have to be, the bound alone decides.
A program may use at most 128 MiB of HBM per device.

```python
import math
import jax
import jax.numpy as jnp

BZC = 16
SLOTS = 8
STEPS = 4
LBLK = 64
NX = 64
NY = 64
NZ = 2048
N_GZ = 16


def draw_owner(key, part):
    first_key, second_key = jax.random.split(jax.random.fold_in(key, 7))
    order = jax.random.permutation(first_key, N_GZ)
    moves = jax.random.randint(second_key, (N_GZ // 2,), 1, SLOTS).astype(jnp.int32)
    counts = jnp.zeros((N_GZ,), jnp.int32)
    counts = counts.at[order[0::2]].set(moves)
    counts = counts.at[order[1::2]].set(SLOTS - moves)
    ends = jnp.cumsum(counts)
    positions = jnp.arange(LBLK, dtype=jnp.int32)
    return jnp.sum((positions[:, None] >= ends[None, :]).astype(jnp.int32), axis=1).astype(jnp.int32)


def with_ends(result, own_key, smallest, top_value):
    longest = result.shape.index(max(result.shape))
    spots = []
    for shift in (0, 1):
        where = [jax.random.randint(jax.random.fold_in(own_key, axis), (), 0, length) for axis, length in enumerate(result.shape)]
        where[longest] = (where[longest] + shift) % result.shape[longest]
        spots.append(tuple(where))
    return result.at[spots[0]].set(smallest).at[spots[1]].set(top_value)


def block_scale(own_key, extent, cuts, least, top_value):
    level = 1.0
    for axis_at, blocks in cuts:
        steps = jax.random.uniform(jax.random.fold_in(jax.random.fold_in(own_key, 6), axis_at), (blocks,), jnp.float32, least / len(cuts), top_value / len(cuts))
        level = level * jnp.repeat(jnp.exp(steps), extent[axis_at] // blocks).reshape((-1,) + (1,) * (len(extent) - 1 - axis_at))
    return level


def bell_draw(key, dims, scale, most, cuts=(), kind=jnp.bfloat16):
    entries = scale * jax.random.normal(key, dims, jnp.float32)
    if cuts:
        entries = entries * block_scale(key, dims, cuts, -0.22, 0.18)
    return jnp.clip(entries, -most, most).astype(kind)


def setup_inputs(seed: int = 0) -> dict:
    key_list = jax.random.split(jax.random.key(seed), 8)
    flow_adjoint = bell_draw(key_list[0], (19, NX, NY, NZ), 1.0, 6.0, ((1, 4), (2, 4), (3, 16)), jnp.float32)
    solute_adjoint = bell_draw(key_list[1], (7, NX, NY, NZ), 1.0, 6.0, ((1, 4), (2, 4), (3, 16)), jnp.float32)
    flow_density = jnp.clip(0.796875 + 0.453125 * jax.random.uniform(key_list[2], (STEPS, NX, NY, NZ), jnp.float32) ** block_scale(key_list[2], (STEPS, NX, NY, NZ), ((1, 4), (2, 4), (3, 16)), -0.2, 0.2), 0.796875, 1.25).astype(jnp.bfloat16)
    flow_velocity = jnp.clip(jax.random.uniform(key_list[3], (STEPS, 3, NX, NY, NZ), jnp.float32, -0.119628906, 0.119628906) * block_scale(key_list[3], (STEPS, 3, NX, NY, NZ), ((2, 4), (3, 4), (4, 16)), -0.4, 0.0), -0.119628906, 0.119628906).astype(jnp.bfloat16)
    solute_level = jnp.clip(jnp.exp(math.log(3.0) - 3.4051113 * jax.random.uniform(key_list[4], (STEPS, NX, NY, NZ), jnp.float32) ** block_scale(key_list[4], (STEPS, NX, NY, NZ), ((1, 4), (2, 4), (3, 16)), -0.2, 0.2)), 0.099609375, 3.0).astype(jnp.bfloat16)
    solid = with_ends((jax.random.randint(key_list[5], (NX, NY, NZ), 0, 4) < 1).astype(jnp.int32), jax.random.fold_in(key_list[5], 1), 0, 1)
    owner = draw_owner(jax.random.fold_in(key_list[7], 71), 0)
    return dict(flow_adjoint=flow_adjoint, solute_adjoint=solute_adjoint, flow_density=flow_density, flow_velocity=flow_velocity, solute_level=solute_level, solid=solid, owner=owner)


FLOW_DIRS = [(0, 0, 0), (1, 0, 0), (-1, 0, 0), (0, 1, 0), (0, -1, 0), (0, 0, 1), (0, 0, -1),
             (1, 1, 0), (-1, -1, 0), (1, -1, 0), (-1, 1, 0), (1, 0, 1), (-1, 0, -1),
             (1, 0, -1), (-1, 0, 1), (0, 1, 1), (0, -1, -1), (0, 1, -1), (0, -1, 1)]
FLOW_WEIGHTS = [1.0 / 3.0] + [1.0 / 18.0] * 6 + [1.0 / 36.0] * 12
SOLUTE_DIRS = FLOW_DIRS[:7]
SOLUTE_WEIGHTS = [0.25] + [0.125] * 6
flow_omega = 1.25
solute_omega = 1.6
langmuir_rate = 0.05


def opposite(table):
    return [table.index((-entry[0], -entry[1], -entry[2])) for entry in table]


def reverse_stream(field, solid_pad, table):
    reverse = opposite(table)
    width_x, width_y, width_z = field.shape[1], field.shape[2], field.shape[3]
    padded = jnp.pad(field, ((0, 0), (1, 1), (1, 1), (1, 1)))
    result_rows = []
    for number, (step_x, step_y, step_z) in enumerate(table):
        near = padded[number, 1 + step_x:1 + step_x + width_x, 1 + step_y:1 + step_y + width_y, 1 + step_z:1 + step_z + width_z]
        blocked = solid_pad[1 + step_x:1 + step_x + width_x, 1 + step_y:1 + step_y + width_y, 1 + step_z:1 + step_z + width_z]
        result_rows.append(jnp.where(blocked == 0, near, field[reverse[number]]))
    return jnp.stack(result_rows)


def solute_update(read, level, velocity):
    vel_x = velocity[0].astype(jnp.float32)
    vel_y = velocity[1].astype(jnp.float32)
    vel_z = velocity[2].astype(jnp.float32)
    level = level.astype(jnp.float32)
    moment_zero = 0.0
    moment_x = 0.0
    moment_y = 0.0
    moment_z = 0.0
    for number, (step_x, step_y, step_z) in enumerate(SOLUTE_DIRS):
        weighted = SOLUTE_WEIGHTS[number] * read[number]
        moment_zero = moment_zero + weighted
        moment_x = moment_x + step_x * weighted
        moment_y = moment_y + step_y * weighted
        moment_z = moment_z + step_z * weighted
    uptake = langmuir_rate / ((1.0 + level) * (1.0 + level))
    common = solute_omega * (moment_zero + 4.0 * (moment_x * vel_x + moment_y * vel_y + moment_z * vel_z)) - uptake * moment_zero
    updated = jnp.stack([(1.0 - solute_omega) * read[number] + common for number in range(len(SOLUTE_DIRS))])
    factor = 4.0 * solute_omega * level
    pull = jnp.stack([factor * moment_x, factor * moment_y, factor * moment_z])
    return updated, pull


def flow_update(read, density, velocity, pull):
    vel_x = velocity[0].astype(jnp.float32)
    vel_y = velocity[1].astype(jnp.float32)
    vel_z = velocity[2].astype(jnp.float32)
    speed_sq = vel_x * vel_x + vel_y * vel_y + vel_z * vel_z
    moment_zero = 0.0
    moment_x = 0.0
    moment_y = 0.0
    moment_z = 0.0
    for number, (step_x, step_y, step_z) in enumerate(FLOW_DIRS):
        weighted = FLOW_WEIGHTS[number] * read[number]
        along = step_x * vel_x + step_y * vel_y + step_z * vel_z
        moment_zero = moment_zero + weighted * (1.0 - 4.5 * along * along + 1.5 * speed_sq)
        shared = 9.0 * weighted * along
        moment_x = moment_x + weighted * (3.0 * step_x - 3.0 * vel_x) + shared * step_x
        moment_y = moment_y + weighted * (3.0 * step_y - 3.0 * vel_y) + shared * step_y
        moment_z = moment_z + weighted * (3.0 * step_z - 3.0 * vel_z) + shared * step_z
    inverse_density = 1.0 / density.astype(jnp.float32)
    result_rows = []
    for number, (step_x, step_y, step_z) in enumerate(FLOW_DIRS):
        relax = moment_zero + step_x * moment_x + step_y * moment_y + step_z * moment_z
        source = (pull[0] * (step_x - vel_x) + pull[1] * (step_y - vel_y) + pull[2] * (step_z - vel_z)) * inverse_density
        result_rows.append((1.0 - flow_omega) * read[number] + flow_omega * relax + source)
    return jnp.stack(result_rows)


def reference(flow_adjoint, solute_adjoint, flow_density, flow_velocity, solute_level, solid, owner):
    blocks = owner.shape[0]
    slot_start = jnp.sum((owner[None, :] < owner[:, None]).astype(jnp.int32), axis=1)
    slot_number = jnp.arange(blocks, dtype=jnp.int32) - slot_start
    offsets = (owner * SLOTS + slot_number) * BZC
    zmap = (offsets[:, None] + jnp.arange(BZC, dtype=jnp.int32)[None, :]).reshape(-1).astype(jnp.int32)
    flow = jnp.take(flow_adjoint, zmap, axis=-1)
    solute = jnp.take(solute_adjoint, zmap, axis=-1)
    density = jnp.take(flow_density, zmap, axis=-1)
    velocity = jnp.take(flow_velocity, zmap, axis=-1)
    level = jnp.take(solute_level, zmap, axis=-1)
    solid_column = jnp.take(solid, zmap, axis=-1)
    valid = jnp.where(solid_column == 0, 1.0, 0.0).astype(jnp.float32)
    solid_pad = jnp.pad(solid_column, 1)
    pulls = [None] * STEPS
    for step in reversed(range(STEPS)):
        read = reverse_stream(solute, solid_pad, SOLUTE_DIRS)
        solute, pulls[step] = solute_update(read, level[step], velocity[step])
        solute = solute * valid
    for step in reversed(range(STEPS)):
        read = reverse_stream(flow, solid_pad, FLOW_DIRS)
        flow = flow_update(read, density[step], velocity[step], pulls[step]) * valid
    flow_result = jnp.zeros(flow_adjoint.shape, jnp.float32).at[..., zmap].set(flow)
    solute_result = jnp.zeros(solute_adjoint.shape, jnp.float32).at[..., zmap].set(solute)
    return flow_result, solute_result
```

```python
import functools

import jax
import jax.numpy as jnp
from jax import lax
from jax.experimental import pallas as pl
from jax.experimental.pallas import tpu as pltpu
from jax.sharding import PartitionSpec as P

MESH = pl.DeviceIdType.MESH
BZC = 16

FLOW_DIRS = [
    (0, 0, 0),
    (1, 0, 0),
    (-1, 0, 0),
    (0, 1, 0),
    (0, -1, 0),
    (0, 0, 1),
    (0, 0, -1),
    (1, 1, 0),
    (-1, -1, 0),
    (1, -1, 0),
    (-1, 1, 0),
    (1, 0, 1),
    (-1, 0, -1),
    (1, 0, -1),
    (-1, 0, 1),
    (0, 1, 1),
    (0, -1, -1),
    (0, 1, -1),
    (0, -1, 1),
]
NF = 19
DIRS = FLOW_DIRS + FLOW_DIRS[:7]
NP = len(DIRS)
OPP = [FLOW_DIRS.index((-c[0], -c[1], -c[2])) for c in FLOW_DIRS]
OPP = OPP + [NF + o for o in OPP[:7]]
flow_omega = 1.25
solute_omega = 1.6
langmuir_rate = 0.05

FACE = [[[p for p in range(NP) if DIRS[p][a] == s] for s in (1, -1)] for a in range(3)]
NQ = 6
SPAN = 18
NBR = [c for c in FLOW_DIRS[1:] if c[2] and c[0]]
NBR += [c for c in FLOW_DIRS[1:] if c[2] and c[1]]
NBR += [c for c in FLOW_DIRS[1:] if c[2] and not c[0] and not c[1]]
NBR += [c for c in FLOW_DIRS[1:] if not c[2] and not (c[0] and c[1])]
NBR += [c for c in FLOW_DIRS[1:] if c[0] and c[1]]
XY = [c for c in NBR if c[0] and c[1]]
XZ = [c for c in NBR if c[0] and c[2]]
YZ = [c for c in NBR if c[1] and c[2]]
Y0 = 8


def side(step):
    return 0 if step > 0 else 1


def kernel(
    sizes,
    steps,
    owner_ref,
    flow_hbm,
    sol_hbm,
    rho_hbm,
    vel_hbm,
    lev_hbm,
    solid_hbm,
    oflow,
    osol,
    A,
    S,
    Zh,
    rho,
    vel,
    lev,
    solid,
    sx,
    sy,
    sz,
    sxy,
    syz,
    rx,
    ry,
    rz,
    rxy,
    rxz,
    ryz,
    in_sem,
    send_sem,
    recv_sem,
):
    WX, WY, D = solid.shape
    H = WY // 8
    names = ("gx", "gy", "gz")
    me = tuple(lax.axis_index(a) for a in names)

    copies = [
        pltpu.make_async_copy(
            flow_hbm, A.at[0, pl.ds(0, NF), pl.ds(1, WX), pl.ds(Y0, WY), :], in_sem.at[0]
        ),
        pltpu.make_async_copy(
            sol_hbm, A.at[0, pl.ds(NF, NP - NF), pl.ds(1, WX), pl.ds(Y0, WY), :], in_sem.at[1]
        ),
        pltpu.make_async_copy(solid_hbm, solid, in_sem.at[2]),
        pltpu.make_async_copy(rho_hbm, rho, in_sem.at[3]),
        pltpu.make_async_copy(vel_hbm, vel, in_sem.at[4]),
        pltpu.make_async_copy(lev_hbm, lev, in_sem.at[5]),
    ]
    for c in copies:
        c.start()

    def exists(c):
        ok = None
        for a in range(3):
            if c[a] > 0:
                t = me[a] < sizes[a] - 1
            elif c[a] < 0:
                t = me[a] > 0
            else:
                continue
            ok = t if ok is None else jnp.logical_and(ok, t)
        return ok

    def device(c):
        return tuple(me[a] + c[a] for a in range(3))

    def neg(c):
        return (-c[0], -c[1], -c[2])

    def clear(ref):
        ref[...] = jnp.zeros(ref.shape, ref.dtype)

    for s in range(steps):
        for ref in (rx, ry, rz, rxy, rxz, ryz):
            clear(ref.at[s])

    barrier = pltpu.get_barrier_semaphore()
    for c in NBR:

        @pl.when(exists(c))
        def _(c=c):
            pl.semaphore_signal(barrier, inc=1, device_id=device(c), device_id_type=MESH)

    n = [
        (me[a] > 0).astype(jnp.int32) + (me[a] < sizes[a] - 1).astype(jnp.int32) for a in range(3)
    ]
    pl.semaphore_wait(
        barrier, n[0] + n[1] + n[2] + n[0] * n[1] + n[0] * n[2] + n[1] * n[2]
    )

    count = jnp.int32(0)
    for i in range(owner_ref.shape[0]):
        count = count + (owner_ref[i] == me[2]).astype(jnp.int32)
    top = count * BZC - 1

    lane = lax.broadcasted_iota(jnp.int32, (8, D), 1)
    group = lane // SPAN
    within = lane - group * SPAN
    is_top = lane == top
    is_bottom = lane == 0

    def message(c, slot, first):
        nq = NQ + 1 if first else NQ
        i = NBR.index(c)
        if c in XY:
            d = XY.index(c)
            src, dst = sxy.at[slot, d, pl.ds(0, nq - NQ + 1)], rxy.at[slot, d, pl.ds(0, nq - NQ + 1)]
        elif c in XZ:
            src, dst = sz.at[slot, side(c[2])], rxz.at[slot, XZ.index(c)]
        elif c in YZ:
            d = YZ.index(c)
            src, dst = syz.at[slot, d], ryz.at[slot, d]
        elif c[0]:
            s = side(c[0])
            src, dst = sx.at[slot, s, pl.ds(0, nq)], rx.at[slot, s, pl.ds(0, nq)]
        elif c[1]:
            s = side(c[1])
            src, dst = sy.at[slot, s, pl.ds(0, nq)], ry.at[slot, s, pl.ds(0, nq)]
        else:
            s = side(c[2])
            src, dst = sz.at[slot, s], rz.at[slot, s]
        return pltpu.make_async_remote_copy(
            src_ref=src,
            dst_ref=dst,
            send_sem=send_sem.at[slot, i],
            recv_sem=recv_sem.at[slot, i],
            device_id=device(neg(c)),
            device_id_type=MESH,
        )

    def send(slot, first):
        for c in NBR:

            @pl.when(exists(neg(c)))
            def _(c=c):
                message(c, slot, first).start()

    def wait_recv(slot, first):
        for c in NBR:

            @pl.when(exists(c))
            def _(c=c):
                message(c, slot, first).wait_recv()

    def wait_send(slot, first):
        for c in NBR:

            @pl.when(exists(neg(c)))
            def _(c=c):
                message(c, slot, first).wait_send()

    def stage_rows(slot, x, q, s, value):
        row = value[0:1] if s == 0 else value[7:8]
        sy[slot, s, q, x] = row

    def pack(slot, x, s, h, values):
        acc = sz[slot, s, pl.ds(8 * h, 8), :]
        source = jnp.int32(0) if s == 0 else top
        put = acc
        for q, value in enumerate(values):
            moved = pltpu.roll(value, (q * SPAN + x + 1 - source + D) % D, 1)
            put = jnp.where((group == q) & (within == x + 1), moved, put)
        sz[slot, s, pl.ds(8 * h, 8), :] = put

    def stage_rest(slot, first, cur):
        for s in (0, 1):
            x = 1 if s == 0 else WX
            for q, p in enumerate(FACE[0][s]):
                sx[slot, s, q] = A[cur, p, x, pl.ds(Y0, WY), :]
            if first:
                sx[slot, s, NQ] = S[0, x, pl.ds(Y0, WY), :]
        for d, c in enumerate(XY):
            q = FACE[1][side(c[1])].index(FLOW_DIRS.index(c))
            x = 0 if c[0] > 0 else WX - 1
            sxy[slot, d, 0] = sy[slot, side(c[1]), q, x]
            if first:
                sxy[slot, d, 1] = sy[slot, side(c[1]), NQ, x]
        for d, c in enumerate(YZ):
            y = 0 if c[1] > 0 else WY - 1
            syz[slot, d] = sz[slot, side(c[2]), pl.ds(y, 1), :]

    def merge(slot, first, cur):
        for s in (0, 1):
            x = WX + 1 if s == 0 else 0
            for q, p in enumerate(FACE[0][s]):
                A[cur, p, x, pl.ds(Y0, WY), :] = rx[slot, s, q]
            if first:
                S[0, x, pl.ds(Y0, WY), :] = rx[slot, s, NQ]

        def rows(x, carry):
            for s in (0, 1):
                y = Y0 + WY if s == 0 else Y0 - 1
                for q, p in enumerate(FACE[1][s]):
                    A[cur, p, x + 1, pl.ds(y, 1), :] = ry[slot, s, q, x]
                if first:
                    S[0, x + 1, pl.ds(y, 1), :] = ry[slot, s, NQ, x]
            return carry

        lax.fori_loop(0, WX, rows, 0)
        for d, c in enumerate(XY):
            x = WX + 1 if c[0] > 0 else 0
            y = Y0 + WY if c[1] > 0 else Y0 - 1
            p = FLOW_DIRS.index(c)
            A[cur, p, x, pl.ds(y, 1), :] = rxy[slot, d, 0]
            if first:
                S[0, x, pl.ds(y, 1), :] = rxy[slot, d, 1]
        for s in (0, 1):
            zc = 1 if s == 0 else -1
            for h in range(H):
                part = pl.ds(8 * h, 8)
                v = rz[slot, s, part, :]
                up = pltpu.roll(rxz[slot, XZ.index((1, 0, zc)), part, :], SPAN - 2, 1)
                down = pltpu.roll(rxz[slot, XZ.index((-1, 0, zc)), part, :], D - (SPAN - 2), 1)
                v = jnp.where(within == SPAN - 1, up, v)
                v = jnp.where(within == 0, down, v)
                Zh[s, pl.ds(Y0 + 8 * h, 8), :] = v
            Zh[s, pl.ds(Y0 + WY, 1), :] = ryz[slot, YZ.index((0, 1, zc))]
            Zh[s, pl.ds(Y0 - 1, 1), :] = ryz[slot, YZ.index((0, -1, zc))]

    def halo_lane(s, q, x, start):
        target = top if s == 0 else jnp.int32(0)
        return pltpu.roll(
            Zh[s, pl.ds(start, 8), :], (target - (q * SPAN + x) + 2 * D) % D, 1
        )

    def along_z(value, s, q, x, start):
        moved = pltpu.roll(value, D - 1 if s == 0 else 1, 1)
        return jnp.where(is_top if s == 0 else is_bottom, halo_lane(s, q, x, start), moved)

    for c in copies[:3]:
        c.wait()

    clear(Zh)
    for part in (0, Y0 + WY):
        for x in range(WX + 2):
            S[0, x, pl.ds(part, 8), :] = jnp.zeros((8, D), jnp.float32)

    sz[...] = jnp.zeros(sz.shape, jnp.float32)

    def first_stage(x, carry):
        flags = solid[x].astype(jnp.float32)
        S[0, x + 1, pl.ds(Y0, WY), :] = flags
        for h in range(H):
            part = pl.ds(Y0 + 8 * h, 8)
            flag = flags[8 * h : 8 * h + 8]
            for s in (0, 1):
                if h == (0 if s == 0 else H - 1):
                    for q, p in enumerate(FACE[1][s]):
                        stage_rows(0, x, q, s, A[0, p, x + 1, part, :])
                    stage_rows(0, x, NQ, s, flag)
                pack(0, x, s, h, [A[0, p, x + 1, part, :] for p in FACE[2][s]] + [flag])
        return carry

    lax.fori_loop(0, WX, first_stage, 0)
    stage_rest(0, True, 0)
    send(0, True)
    for c in copies[3:]:
        c.wait()
    wait_recv(0, True)
    merge(0, True, 0)

    def flags_z(x, carry):
        for s in (0, 1):
            for start in (Y0 - 8, Y0, Y0 + 8, Y0 + WY):
                part = pl.ds(start, 8)
                S[1 + s, x, part, :] = along_z(S[0, x, part, :], s, NQ, x, start)
        return carry

    lax.fori_loop(0, WX + 2, flags_z, 0)

    def cell(k, cur, x, h, start, u, level, density):
        t = steps - 1 - k

        def read(p):
            c = DIRS[p]
            here = A[cur, p, x + 1 + c[0], pl.ds(start + c[1], 8), :]
            if c == (0, 0, 0):
                return here
            if c[2]:
                s = side(c[2])
                here = along_z(here, s, FACE[2][s].index(p), x + 1 + c[0], start + c[1])
                flag = S[1 + s, x + 1 + c[0], pl.ds(start + c[1], 8), :]
            else:
                flag = S[0, x + 1 + c[0], pl.ds(start + c[1], 8), :]
            back = A[cur, OPP[p], x + 1, pl.ds(start, 8), :]
            return jnp.where(flag > 0.5, back, here)

        ux, uy, uz = u
        new = [None] * NP
        h0 = read(NF)
        hs = [read(NF + p) for p in range(1, 7)]
        mx, my, mz = hs[0] - hs[1], hs[2] - hs[3], hs[4] - hs[5]
        m0 = 0.25 * h0 + 0.125 * ((hs[0] + hs[1]) + (hs[2] + hs[3]) + (hs[4] + hs[5]))
        along = mx * ux + my * uy + mz * uz
        one = 1.0 + level
        common = (solute_omega - langmuir_rate / (one * one)) * m0 + (
            solute_omega * 0.5
        ) * along
        for p, v in enumerate([h0] + hs):
            new[NF + p] = (1.0 - solute_omega) * v + common
        inverse = 1.0 / density
        factor = (0.5 * solute_omega) * level * inverse
        g = [read(p) for p in range(NF)]
        a = [g[p] + g[p + 1] for p in range(1, NF, 2)]
        d = [g[p] - g[p + 1] for p in range(1, NF, 2)]
        ax, ay, az = 2.0 * a[0], 2.0 * a[1], 2.0 * a[2]
        sxy_, sxz_, syz_ = a[3] + a[4], a[5] + a[6], a[7] + a[8]
        qxy, qxz, qyz = a[3] - a[4], a[5] - a[6], a[7] - a[8]
        qxx, qyy, qzz = ax + sxy_ + sxz_, ay + sxy_ + syz_, az + sxz_ + syz_
        total = 12.0 * g[0] + (qxx + ay + az) + syz_
        jx = 2.0 * d[0] + (d[3] + d[4]) + (d[5] + d[6])
        jy = 2.0 * d[1] + (d[3] - d[4]) + (d[7] + d[8])
        jz = 2.0 * d[2] + (d[5] - d[6]) + (d[7] - d[8])
        vx = qxx * ux + qxy * uy + qxz * uz
        vy = qxy * ux + qyy * uy + qyz * uz
        vz = qxz * ux + qyz * uy + qzz * uz
        quad = vx * ux + vy * uy + vz * uz
        speed = ux * ux + uy * uy + uz * uz
        w = flow_omega / 36.0
        scalar = w * (total * (1.0 + 1.5 * speed) - 4.5 * quad) - factor * along
        tx = (3.0 * w) * (jx + 3.0 * vx - ux * total) + factor * mx
        ty = (3.0 * w) * (jy + 3.0 * vy - uy * total) + factor * my
        tz = (3.0 * w) * (jz + 3.0 * vz - uz * total) + factor * mz
        rest = 1.0 - flow_omega
        new[0] = rest * g[0] + scalar
        pairs = [tx, ty, tz, tx + ty, tx - ty, tx + tz, tx - tz, ty + tz, ty - tz]
        for i, v in enumerate(pairs):
            p = 1 + 2 * i
            new[p] = rest * g[p] + (scalar + v)
            new[p + 1] = rest * g[p + 1] + (scalar - v)
        return new

    def slab(k, cur, x):
        t = steps - 1 - k
        level = lev[t, x].astype(jnp.float32)
        density = rho[t, x].astype(jnp.float32)
        u = [vel[t, i, x].astype(jnp.float32) for i in range(3)]
        for h in range(H):
            cut = slice(8 * h, 8 * h + 8)
            yield h, cell(
                k, cur, x, h, Y0 + 8 * h, [v[cut] for v in u], level[cut], density[cut]
            )

    def step(k, carry):
        cur = lax.rem(k, 2)
        nxt = 1 - cur

        def body(x, carry):
            for h, new in slab(k, cur, x):
                part = pl.ds(Y0 + 8 * h, 8)
                for p in range(NP):
                    A[nxt, p, x + 1, part, :] = new[p]
                for s in (0, 1):
                    if h == (0 if s == 0 else H - 1):
                        for q, p in enumerate(FACE[1][s]):
                            stage_rows(k + 1, x, q, s, new[p])
                    pack(k + 1, x, s, h, [new[p] for p in FACE[2][s]])
            return carry

        lax.fori_loop(0, WX, body, 0)
        stage_rest(k + 1, False, nxt)
        send(k + 1, False)
        wait_recv(k + 1, False)
        merge(k + 1, False, nxt)
        return carry

    lax.fori_loop(0, steps - 1, step, 0)

    def last(x, carry):
        k = steps - 1
        for h, new in slab(k, k % 2, x):
            part = pl.ds(8 * h, 8)
            keep = (S[0, x + 1, pl.ds(Y0 + 8 * h, 8), :] < 0.5) & (lane <= top)
            for p in range(NP):
                value = jnp.where(keep, new[p], 0.0)
                if p < NF:
                    oflow[p, x, part, :] = value
                else:
                    osol[p - NF, x, part, :] = value
        return carry

    lax.fori_loop(0, WX, last, 0)
    for s in range(steps):
        wait_send(s, s == 0)


def solution(mesh):
    names = ("gx", "gy", "gz")
    sizes = tuple(mesh.shape[a] for a in names)

    def per_device(flow, solute, rho, vel, lev, solid, owner):
        WX, WY, D = solid.shape
        steps = rho.shape[0]
        f32 = jnp.float32
        V = pltpu.VMEM
        DMA = pltpu.SemaphoreType.DMA
        hbm = pl.BlockSpec(memory_space=pl.ANY)
        n = len(NBR)
        return pl.pallas_call(
            functools.partial(kernel, sizes, steps),
            out_shape=(
                jax.ShapeDtypeStruct(flow.shape, f32),
                jax.ShapeDtypeStruct(solute.shape, f32),
            ),
            in_specs=[pl.BlockSpec(memory_space=pltpu.SMEM)] + [hbm] * 6,
            out_specs=(pl.BlockSpec(memory_space=pltpu.VMEM),) * 2,
            scratch_shapes=[
                V((2, NP, WX + 2, WY + 16, D), f32),
                V((3, WX + 2, WY + 16, D), f32),
                V((2, WY + 16, D), f32),
                V(rho.shape, rho.dtype),
                V(vel.shape, vel.dtype),
                V(lev.shape, lev.dtype),
                V(solid.shape, solid.dtype),
                V((steps, 2, NQ + 1, WY, D), f32),
                V((steps, 2, NQ + 1, WX, 1, D), f32),
                V((steps, 2, WY, D), f32),
                V((steps, 4, 2, 1, D), f32),
                V((steps, 4, 1, D), f32),
                V((steps, 2, NQ + 1, WY, D), f32),
                V((steps, 2, NQ + 1, WX, 1, D), f32),
                V((steps, 2, WY, D), f32),
                V((steps, 4, 2, 1, D), f32),
                V((steps, 4, WY, D), f32),
                V((steps, 4, 1, D), f32),
                DMA((6,)),
                DMA((steps, n)),
                DMA((steps, n)),
            ],
            compiler_params=pltpu.CompilerParams(
                collective_id=0, has_side_effects=True, vmem_limit_bytes=60 * 2**20
            ),
        )(owner, flow, solute, rho, vel, lev, solid)

    field = P(None, "gx", "gy", "gz")
    return jax.shard_map(
        per_device,
        mesh=mesh,
        in_specs=(field, field, field, P(None, None, "gx", "gy", "gz"), field, P("gx", "gy", "gz"), P()),
        out_specs=(field, field),
        check_vma=False,
    )
```

```python
import functools

import jax
import jax.numpy as jnp
from jax import lax
from jax.experimental import pallas as pl
from jax.experimental.pallas import tpu as pltpu
from jax.sharding import PartitionSpec as P

MESH = pl.DeviceIdType.MESH
BZC = 16

FLOW_DIRS = [
    (0, 0, 0),
    (1, 0, 0),
    (-1, 0, 0),
    (0, 1, 0),
    (0, -1, 0),
    (0, 0, 1),
    (0, 0, -1),
    (1, 1, 0),
    (-1, -1, 0),
    (1, -1, 0),
    (-1, 1, 0),
    (1, 0, 1),
    (-1, 0, -1),
    (1, 0, -1),
    (-1, 0, 1),
    (0, 1, 1),
    (0, -1, -1),
    (0, 1, -1),
    (0, -1, 1),
]
NF = 19
DIRS = FLOW_DIRS + FLOW_DIRS[:7]
NP = len(DIRS)
OPP = [FLOW_DIRS.index((-c[0], -c[1], -c[2])) for c in FLOW_DIRS]
OPP = OPP + [NF + o for o in OPP[:7]]
flow_omega = 1.25
solute_omega = 1.6
langmuir_rate = 0.05

FACE = [[[p for p in range(NP) if DIRS[p][a] == s] for s in (1, -1)] for a in range(3)]
NQ = 6
SPAN = 16
NBR = [c for c in FLOW_DIRS[1:] if c[2] and c[0]]
NBR += [c for c in FLOW_DIRS[1:] if c[2] and c[1]]
NBR += [c for c in FLOW_DIRS[1:] if c[2] and not c[0] and not c[1]]
NBR += [c for c in FLOW_DIRS[1:] if not c[2] and not (c[0] and c[1])]
NBR += [c for c in FLOW_DIRS[1:] if c[0] and c[1]]
XY = [c for c in NBR if c[0] and c[1]]
XZ = [c for c in NBR if c[0] and c[2]]
YZ = [c for c in NBR if c[1] and c[2]]
Y0 = 8


def side(step):
    return 0 if step > 0 else 1


def kernel(
    sizes,
    steps,
    owner_ref,
    flow_hbm,
    sol_hbm,
    rho_hbm,
    vel_hbm,
    lev_hbm,
    solid_hbm,
    oflow,
    osol,
    A,
    S,
    rho,
    vel,
    lev,
    solid,
    sx,
    sy,
    sz,
    sxy,
    syz,
    rx,
    ry,
    rz,
    rxy,
    rxz,
    ryz,
    in_sem,
    send_sem,
    recv_sem,
):
    WX, WY, D = solid.shape
    H = WY // 8
    names = ("gx", "gy", "gz")
    me = tuple(lax.axis_index(a) for a in names)

    copies = [
        pltpu.make_async_copy(
            flow_hbm, A.at[0, pl.ds(0, NF), pl.ds(1, WX), pl.ds(Y0, WY), :], in_sem.at[0]
        ),
        pltpu.make_async_copy(
            sol_hbm, A.at[0, pl.ds(NF, NP - NF), pl.ds(1, WX), pl.ds(Y0, WY), :], in_sem.at[1]
        ),
        pltpu.make_async_copy(solid_hbm, solid, in_sem.at[2]),
        pltpu.make_async_copy(rho_hbm, rho, in_sem.at[3]),
        pltpu.make_async_copy(vel_hbm, vel, in_sem.at[4]),
        pltpu.make_async_copy(lev_hbm, lev, in_sem.at[5]),
    ]
    for c in copies:
        c.start()

    def exists(c):
        ok = None
        for a in range(3):
            if c[a] > 0:
                t = me[a] < sizes[a] - 1
            elif c[a] < 0:
                t = me[a] > 0
            else:
                continue
            ok = t if ok is None else jnp.logical_and(ok, t)
        return ok

    def device(c):
        return tuple(me[a] + c[a] for a in range(3))

    def neg(c):
        return (-c[0], -c[1], -c[2])

    barrier = pltpu.get_barrier_semaphore()
    for c in NBR:

        @pl.when(exists(c))
        def _(c=c):
            pl.semaphore_signal(barrier, inc=1, device_id=device(c), device_id_type=MESH)

    n = [
        (me[a] > 0).astype(jnp.int32) + (me[a] < sizes[a] - 1).astype(jnp.int32) for a in range(3)
    ]
    pl.semaphore_wait(
        barrier, n[0] + n[1] + n[2] + n[0] * n[1] + n[0] * n[2] + n[1] * n[2]
    )

    count = jnp.int32(0)
    for i in range(owner_ref.shape[0]):
        count = count + (owner_ref[i] == me[2]).astype(jnp.int32)
    top = count * BZC - 1

    lane = lax.broadcasted_iota(jnp.int32, (8, D), 1)
    row = lax.broadcasted_iota(jnp.int32, (8, D), 0)
    halo_lane = (lane == top + 1, lane == D - 1)
    slot_lane = (lane - (SPAN - 1), (lane - (top + SPAN - 1) + 2 * D) % D)

    def landing(c, slot):
        if c in XY:
            return rxy.at[slot, XY.index(c)]
        if c in XZ:
            return rxz.at[slot, XZ.index(c)]
        if c in YZ:
            return ryz.at[slot, YZ.index(c)]
        a = [i for i in range(3) if c[i]][0]
        return (rx, ry, rz)[a].at[slot, side(c[a])]

    def clear_missing():
        for c in NBR:

            @pl.when(jnp.logical_not(exists(c)))
            def _(c=c):
                for k in range(steps):
                    ref = landing(c, k)
                    ref[...] = jnp.zeros(ref.shape, ref.dtype)

    def message(c, slot, first):
        nq = NQ + 1 if first else NQ
        i = NBR.index(c)
        if c in XY:
            d = XY.index(c)
            src, dst = sxy.at[slot, d, pl.ds(0, nq - NQ + 1)], rxy.at[slot, d, pl.ds(0, nq - NQ + 1)]
        elif c in XZ:
            src, dst = sz.at[slot, side(c[2])], rxz.at[slot, XZ.index(c)]
        elif c in YZ:
            d = YZ.index(c)
            src, dst = syz.at[slot, d], ryz.at[slot, d]
        elif c[0]:
            s = side(c[0])
            src, dst = sx.at[slot, s, pl.ds(0, nq)], rx.at[slot, s, pl.ds(0, nq)]
        elif c[1]:
            s = side(c[1])
            src, dst = sy.at[slot, s, pl.ds(0, nq)], ry.at[slot, s, pl.ds(0, nq)]
        else:
            s = side(c[2])
            src, dst = sz.at[slot, s], rz.at[slot, s]
        return pltpu.make_async_remote_copy(
            src_ref=src,
            dst_ref=dst,
            send_sem=send_sem.at[slot, i],
            recv_sem=recv_sem.at[slot, i],
            device_id=device(neg(c)),
            device_id_type=MESH,
        )

    def send(slot, first):
        for c in NBR:

            @pl.when(exists(neg(c)))
            def _(c=c):
                message(c, slot, first).start()

    def wait_recv(slot, first):
        for c in NBR:

            @pl.when(exists(c))
            def _(c=c):
                message(c, slot, first).wait_recv()

    def wait_send(slot, first):
        for c in NBR:

            @pl.when(exists(neg(c)))
            def _(c=c):
                message(c, slot, first).wait_send()

    def stage_row(slot, x, q, s, value):
        sy[slot, s, q, pl.ds(x, 1), :] = value[0:1] if s == 0 else value[7:8]

    def pack(acc, s, values):
        acc = pltpu.roll(acc, D - 1, 1)
        for q, value in enumerate(values):
            moved = pltpu.roll(value, q * SPAN + SPAN - 1, 1)
            acc = jnp.where(slot_lane[s] == q * SPAN, moved, acc)
        return acc

    def stage_rest(slot, first, cur, packed):
        for i, (s, h) in enumerate((s, h) for s in (0, 1) for h in range(H)):
            face = packed[i]
            if s == 1:
                face = pltpu.roll(face, D - top, 1)
            sz[slot, s, pl.ds(8 * h, 8), :] = face
            for d, c in enumerate(YZ):
                if side(c[2]) == s and h == (0 if c[1] > 0 else H - 1):
                    syz[slot, d] = face[0:1] if c[1] > 0 else face[7:8]
        for s in (0, 1):
            x = 1 if s == 0 else WX
            for q, p in enumerate(FACE[0][s]):
                sx[slot, s, q] = A[cur, p, x, pl.ds(Y0, WY), :]
            if first:
                sx[slot, s, NQ] = S[0, x, pl.ds(Y0, WY), :]
        for d, c in enumerate(XY):
            q = FACE[1][side(c[1])].index(FLOW_DIRS.index(c))
            x = 0 if c[0] > 0 else WX - 1
            sxy[slot, d, 0] = sy[slot, side(c[1]), q, pl.ds(x, 1), :]
            if first:
                sxy[slot, d, 1] = sy[slot, side(c[1]), NQ, pl.ds(x, 1), :]

    def merge(slot, first, cur):
        flag = [(NQ, None)] if first else []

        def put(p, x, rows, value):
            if p is None:
                S[0, x, rows, :] = value
            else:
                A[cur, p, x, rows, :] = value

        for s in (0, 1):
            x = WX + 1 if s == 0 else 0
            cx = 1 if s == 0 else -1
            edge = 0 if s == 0 else WX - 1
            for q, p in list(enumerate(FACE[0][s])) + flag:
                for h in range(H):
                    value = rx[slot, s, q, pl.ds(8 * h, 8), :]
                    for z in (0, 1):
                        cz = 1 - 2 * z
                        if p is None or DIRS[p] == (cx, 0, cz) and p < NF:
                            qz = NQ if p is None else FACE[2][z].index(p)
                            line = rxz[slot, XZ.index((cx, 0, cz)), pl.ds(8 * h, 8), :]
                            column = qz * SPAN + edge
                            line = jnp.broadcast_to(line[:, column : column + 1], (8, D))
                            value = jnp.where(halo_lane[z], line, value)
                    put(p, x, pl.ds(Y0 + 8 * h, 8), value)
        for s in (0, 1):
            y = Y0 + WY if s == 0 else Y0 - 1
            cy = 1 if s == 0 else -1
            for q, p in list(enumerate(FACE[1][s])) + flag:
                for half in range(WX // 8):
                    value = ry[slot, s, q, pl.ds(8 * half, 8), :]
                    for z in (0, 1):
                        cz = 1 - 2 * z
                        if p is None or DIRS[p] == (0, cy, cz) and p < NF:
                            qz = NQ if p is None else FACE[2][z].index(p)
                            line = jnp.broadcast_to(ryz[slot, YZ.index((0, cy, cz))], (8, D))
                            here = lane == row + (qz * SPAN + 8 * half)
                            line = jnp.sum(jnp.where(here, line, 0.0), axis=1, keepdims=True)
                            value = jnp.where(halo_lane[z], line, value)
                    for i in range(8):
                        put(p, 1 + 8 * half + i, pl.ds(y, 1), value[i : i + 1])
        for d, c in enumerate(XY):
            x = WX + 1 if c[0] > 0 else 0
            y = Y0 + WY if c[1] > 0 else Y0 - 1
            put(FLOW_DIRS.index(c), x, pl.ds(y, 1), rxy[slot, d, 0])
            if first:
                put(None, x, pl.ds(y, 1), rxy[slot, d, 1])
        for s in (0, 1):
            for h in range(H):
                rows = pl.ds(Y0 + 8 * h, 8)
                face = rz[slot, s, pl.ds(8 * h, 8), :]
                face = pltpu.roll(face, top + 1 if s == 0 else D - 1, 1)
                for q, p in list(enumerate(FACE[2][s])) + flag:
                    for x in range(WX):
                        moved = pltpu.roll(face, D - (q * SPAN + x), 1) if q + x else face
                        old = S[0, x + 1, rows, :] if p is None else A[cur, p, x + 1, rows, :]
                        put(p, x + 1, rows, jnp.where(halo_lane[s], moved, old))

    for c in copies[:3]:
        c.wait()

    for part in (0, Y0 + WY):
        for x in range(WX + 2):
            S[0, x, pl.ds(part, 8), :] = jnp.zeros((8, D), jnp.float32)

    blank = (jnp.zeros((8, D), jnp.float32),) * (2 * H)

    def first_stage(x, packed):
        packed = list(packed)
        flags = solid[x].astype(jnp.float32)
        S[0, x + 1, pl.ds(Y0, WY), :] = flags
        for h in range(H):
            part = pl.ds(Y0 + 8 * h, 8)
            flag = flags[8 * h : 8 * h + 8]
            for s in (0, 1):
                if h == (0 if s == 0 else H - 1):
                    for q, p in enumerate(FACE[1][s]):
                        stage_row(0, x, q, s, A[0, p, x + 1, part, :])
                    stage_row(0, x, NQ, s, flag)
                i = s * H + h
                packed[i] = pack(packed[i], s, [A[0, p, x + 1, part, :] for p in FACE[2][s]] + [flag])
        return tuple(packed)

    packed = lax.fori_loop(0, WX, first_stage, blank)
    stage_rest(0, True, 0, packed)
    send(0, True)
    clear_missing()
    for c in copies[3:]:
        c.wait()
    wait_send(0, True)
    wait_recv(0, True)
    merge(0, True, 0)

    def flags_z(x, carry):
        for start in range(0, WY + 16, 8):
            part = pl.ds(start, 8)
            flag = S[0, x, part, :]
            S[1, x, part, :] = pltpu.roll(flag, D - 1, 1)
            S[2, x, part, :] = pltpu.roll(flag, 1, 1)
        return carry

    lax.fori_loop(0, WX + 2, flags_z, 0)

    def cell(k, cur, x, h, start, u, level, density):
        t = steps - 1 - k

        def read(p):
            c = DIRS[p]
            here = A[cur, p, x + 1 + c[0], pl.ds(start + c[1], 8), :]
            if c == (0, 0, 0):
                return here
            if c[2]:
                s = side(c[2])
                here = pltpu.roll(here, D - 1 if s == 0 else 1, 1)
                flag = S[1 + s, x + 1 + c[0], pl.ds(start + c[1], 8), :]
            else:
                flag = S[0, x + 1 + c[0], pl.ds(start + c[1], 8), :]
            back = A[cur, OPP[p], x + 1, pl.ds(start, 8), :]
            return jnp.where(flag > 0.5, back, here)

        ux, uy, uz = u
        new = [None] * NP
        h0 = read(NF)
        hs = [read(NF + p) for p in range(1, 7)]
        mx, my, mz = hs[0] - hs[1], hs[2] - hs[3], hs[4] - hs[5]
        m0 = 0.25 * h0 + 0.125 * ((hs[0] + hs[1]) + (hs[2] + hs[3]) + (hs[4] + hs[5]))
        along = mx * ux + my * uy + mz * uz
        one = 1.0 + level
        common = (solute_omega - langmuir_rate / (one * one)) * m0 + (
            solute_omega * 0.5
        ) * along
        for p, v in enumerate([h0] + hs):
            new[NF + p] = (1.0 - solute_omega) * v + common
        inverse = 1.0 / density
        factor = (0.5 * solute_omega) * level * inverse
        g = [read(p) for p in range(NF)]
        a = [g[p] + g[p + 1] for p in range(1, NF, 2)]
        d = [g[p] - g[p + 1] for p in range(1, NF, 2)]
        ax, ay, az = 2.0 * a[0], 2.0 * a[1], 2.0 * a[2]
        sxy_, sxz_, syz_ = a[3] + a[4], a[5] + a[6], a[7] + a[8]
        qxy, qxz, qyz = a[3] - a[4], a[5] - a[6], a[7] - a[8]
        qxx, qyy, qzz = ax + sxy_ + sxz_, ay + sxy_ + syz_, az + sxz_ + syz_
        total = 12.0 * g[0] + (qxx + ay + az) + syz_
        jx = 2.0 * d[0] + (d[3] + d[4]) + (d[5] + d[6])
        jy = 2.0 * d[1] + (d[3] - d[4]) + (d[7] + d[8])
        jz = 2.0 * d[2] + (d[5] - d[6]) + (d[7] - d[8])
        vx = qxx * ux + qxy * uy + qxz * uz
        vy = qxy * ux + qyy * uy + qyz * uz
        vz = qxz * ux + qyz * uy + qzz * uz
        quad = vx * ux + vy * uy + vz * uz
        speed = ux * ux + uy * uy + uz * uz
        w = flow_omega / 36.0
        scalar = w * (total * (1.0 + 1.5 * speed) - 4.5 * quad) - factor * along
        tx = (3.0 * w) * (jx + 3.0 * vx - ux * total) + factor * mx
        ty = (3.0 * w) * (jy + 3.0 * vy - uy * total) + factor * my
        tz = (3.0 * w) * (jz + 3.0 * vz - uz * total) + factor * mz
        rest = 1.0 - flow_omega
        new[0] = rest * g[0] + scalar
        pairs = [tx, ty, tz, tx + ty, tx - ty, tx + tz, tx - tz, ty + tz, ty - tz]
        for i, v in enumerate(pairs):
            p = 1 + 2 * i
            new[p] = rest * g[p] + (scalar + v)
            new[p + 1] = rest * g[p + 1] + (scalar - v)
        return new

    def slab(k, cur, x):
        t = steps - 1 - k
        level = lev[t, x].astype(jnp.float32)
        density = rho[t, x].astype(jnp.float32)
        u = [vel[t, i, x].astype(jnp.float32) for i in range(3)]
        for h in range(H):
            cut = slice(8 * h, 8 * h + 8)
            yield h, cell(
                k, cur, x, h, Y0 + 8 * h, [v[cut] for v in u], level[cut], density[cut]
            )

    def step(k, carry):
        cur = lax.rem(k, 2)
        nxt = 1 - cur

        def body(x, packed):
            packed = list(packed)
            for h, new in slab(k, cur, x):
                part = pl.ds(Y0 + 8 * h, 8)
                for p in range(NP):
                    A[nxt, p, x + 1, part, :] = new[p]
                for s in (0, 1):
                    if h == (0 if s == 0 else H - 1):
                        for q, p in enumerate(FACE[1][s]):
                            stage_row(k + 1, x, q, s, new[p])
                    i = s * H + h
                    packed[i] = pack(packed[i], s, [new[p] for p in FACE[2][s]])
            return tuple(packed)

        packed = lax.fori_loop(0, WX, body, blank)
        stage_rest(k + 1, False, nxt, packed)
        send(k + 1, False)
        wait_send(k + 1, False)
        wait_recv(k + 1, False)
        merge(k + 1, False, nxt)
        return carry

    lax.fori_loop(0, steps - 1, step, 0)

    def last(x, carry):
        k = steps - 1
        for h, new in slab(k, k % 2, x):
            part = pl.ds(8 * h, 8)
            keep = (S[0, x + 1, pl.ds(Y0 + 8 * h, 8), :] < 0.5) & (lane <= top)
            for p in range(NP):
                value = jnp.where(keep, new[p], 0.0)
                if p < NF:
                    oflow[p, x, part, :] = value
                else:
                    osol[p - NF, x, part, :] = value
        return carry

    lax.fori_loop(0, WX, last, 0)


def solution(mesh):
    names = ("gx", "gy", "gz")
    sizes = tuple(mesh.shape[a] for a in names)

    def per_device(flow, solute, rho, vel, lev, solid, owner):
        WX, WY, D = solid.shape
        steps = rho.shape[0]
        f32 = jnp.float32
        V = pltpu.VMEM
        DMA = pltpu.SemaphoreType.DMA
        hbm = pl.BlockSpec(memory_space=pl.ANY)
        n = len(NBR)
        return pl.pallas_call(
            functools.partial(kernel, sizes, steps),
            out_shape=(
                jax.ShapeDtypeStruct(flow.shape, f32),
                jax.ShapeDtypeStruct(solute.shape, f32),
            ),
            in_specs=[pl.BlockSpec(memory_space=pltpu.SMEM)] + [hbm] * 6,
            out_specs=(pl.BlockSpec(memory_space=pltpu.VMEM),) * 2,
            scratch_shapes=[
                V((2, NP, WX + 2, WY + 16, D), f32),
                V((3, WX + 2, WY + 16, D), f32),
                V(rho.shape, rho.dtype),
                V(vel.shape, vel.dtype),
                V(lev.shape, lev.dtype),
                V(solid.shape, solid.dtype),
                V((steps, 2, NQ + 1, WY, D), f32),
                V((steps, 2, NQ + 1, WX, D), f32),
                V((steps, 2, WY, D), f32),
                V((steps, 4, 2, 1, D), f32),
                V((steps, 4, 1, D), f32),
                V((steps, 2, NQ + 1, WY, D), f32),
                V((steps, 2, NQ + 1, WX, D), f32),
                V((steps, 2, WY, D), f32),
                V((steps, 4, 2, 1, D), f32),
                V((steps, 4, WY, D), f32),
                V((steps, 4, 1, D), f32),
                DMA((6,)),
                DMA((steps, n)),
                DMA((steps, n)),
            ],
            compiler_params=pltpu.CompilerParams(
                collective_id=0, has_side_effects=True, vmem_limit_bytes=60 * 2**20
            ),
        )(owner, flow, solute, rho, vel, lev, solid)

    field = P(None, "gx", "gy", "gz")
    return jax.shard_map(
        per_device,
        mesh=mesh,
        in_specs=(field, field, field, P(None, None, "gx", "gy", "gz"), field, P("gx", "gy", "gz"), P()),
        out_specs=(field, field),
        check_vma=False,
    )
```

```python
import functools

import jax
import jax.numpy as jnp
from jax import lax
from jax.experimental import pallas as pl
from jax.experimental.pallas import tpu as pltpu
from jax.sharding import PartitionSpec as P

MESH = pl.DeviceIdType.MESH
BZC = 16

FLOW_DIRS = [
    (0, 0, 0),
    (1, 0, 0),
    (-1, 0, 0),
    (0, 1, 0),
    (0, -1, 0),
    (0, 0, 1),
    (0, 0, -1),
    (1, 1, 0),
    (-1, -1, 0),
    (1, -1, 0),
    (-1, 1, 0),
    (1, 0, 1),
    (-1, 0, -1),
    (1, 0, -1),
    (-1, 0, 1),
    (0, 1, 1),
    (0, -1, -1),
    (0, 1, -1),
    (0, -1, 1),
]
NF = 19
NP = NF + 7
OPP = [FLOW_DIRS.index((-c[0], -c[1], -c[2])) for c in FLOW_DIRS]
flow_omega = 1.25
solute_omega = 1.6
langmuir_rate = 0.05

FACE = [[[p for p in range(NF) if FLOW_DIRS[p][a] == s] for s in (1, -1)] for a in range(3)]
NQ = 5
SPAN = 18
FACES = FLOW_DIRS[1:7]
NBR = [c for c in FLOW_DIRS[1:] if c[2] and c[0]]
NBR += [c for c in FLOW_DIRS[1:] if c[2] and c[1]]
NBR += [c for c in FLOW_DIRS[1:] if c[2] and not c[0] and not c[1]]
NBR += [c for c in FLOW_DIRS[1:] if not c[2] and not (c[0] and c[1])]
NBR += [c for c in FLOW_DIRS[1:] if c[0] and c[1]]
XY = [c for c in NBR if c[0] and c[1]]
XZ = [c for c in NBR if c[0] and c[2]]
YZ = [c for c in NBR if c[1] and c[2]]
Y0 = 8


def side(step):
    return 0 if step > 0 else 1


def axis(c):
    return [i for i in range(3) if c[i]][0]


def neg(c):
    return (-c[0], -c[1], -c[2])


def kernel(
    sizes,
    steps,
    owner_ref,
    flow_hbm,
    sol_hbm,
    rho_hbm,
    vel_hbm,
    lev_hbm,
    solid_hbm,
    oflow,
    osol,
    A,
    B,
    S,
    Zf,
    ZR,
    PU,
    rho,
    vel,
    lev,
    solid,
    sx,
    sy,
    sz,
    sxy,
    sxz,
    syz,
    tx,
    ty,
    tz,
    rx,
    ry,
    rz,
    rxy,
    rxz,
    ryz,
    ux,
    uy,
    uz,
    in_sem,
    send_sem,
    recv_sem,
):
    WX, WY, D = solid.shape
    H = WY // 8
    names = ("gx", "gy", "gz")
    me = tuple(lax.axis_index(a) for a in names)

    inside = (pl.ds(1, WX), pl.ds(Y0, WY), slice(None))
    copies = [pltpu.make_async_copy(solid_hbm, solid, in_sem.at[0])]
    cuts = (0, 5, 10, 15, NF)
    for i, (lo, hi) in enumerate(zip(cuts, cuts[1:])):
        part = pl.ds(lo, hi - lo)
        copies.append(
            pltpu.make_async_copy(flow_hbm.at[part], A.at[(0, part) + inside], in_sem.at[1 + i])
        )
    copies.append(pltpu.make_async_copy(sol_hbm, B.at[(0, slice(None)) + inside], in_sem.at[5]))
    copies.append(pltpu.make_async_copy(lev_hbm, lev, in_sem.at[6]))
    copies.append(pltpu.make_async_copy(vel_hbm, vel, in_sem.at[7]))
    copies.append(pltpu.make_async_copy(rho_hbm, rho, in_sem.at[8]))
    for c in copies:
        c.start()

    def exists(c):
        ok = None
        for a in range(3):
            if c[a] > 0:
                t = me[a] < sizes[a] - 1
            elif c[a] < 0:
                t = me[a] > 0
            else:
                continue
            ok = t if ok is None else jnp.logical_and(ok, t)
        return ok

    def device(c):
        return tuple(me[a] + c[a] for a in range(3))

    barrier = pltpu.get_barrier_semaphore()
    for c in NBR:

        @pl.when(exists(c))
        def _(c=c):
            pl.semaphore_signal(barrier, inc=1, device_id=device(c), device_id_type=MESH)

    count = jnp.int32(0)
    for i in range(owner_ref.shape[0]):
        count = count + (owner_ref[i] == me[2]).astype(jnp.int32)
    top = count * BZC - 1

    lane = lax.broadcasted_iota(jnp.int32, (8, D), 1)
    row = lax.broadcasted_iota(jnp.int32, (8, D), 0)
    edge = (lane == top, lane == 0)
    last_column = SPAN - 2
    slot_lane = (lane - last_column, (lane - (top + last_column) + 2 * D) % D)

    n = [
        (me[a] > 0).astype(jnp.int32) + (me[a] < sizes[a] - 1).astype(jnp.int32) for a in range(3)
    ]
    pl.semaphore_wait(
        barrier, n[0] + n[1] + n[2] + n[0] * n[1] + n[0] * n[2] + n[1] * n[2]
    )

    def flow_refs(c, slot, first):
        nq = NQ + 1 if first else NQ
        if c in XY:
            part = (slot, XY.index(c), pl.ds(0, nq - NQ + 1))
            return sxy.at[part], rxy.at[part]
        if c in XZ:
            part = (slot, XZ.index(c))
            return sxz.at[part], rxz.at[part]
        if c in YZ:
            part = (slot, YZ.index(c))
            return syz.at[part], ryz.at[part]
        a = axis(c)
        part = (slot, side(c[a]))
        if a == 2:
            return sz.at[part], rz.at[part]
        part = part + (pl.ds(0, nq),)
        return ((sx, rx), (sy, ry))[a][0].at[part], ((sx, rx), (sy, ry))[a][1].at[part]

    def flow_message(c, slot, first):
        src, dst = flow_refs(c, slot, first)
        i = NBR.index(c)
        return pltpu.make_async_remote_copy(
            src_ref=src,
            dst_ref=dst,
            send_sem=send_sem.at[slot, i],
            recv_sem=recv_sem.at[slot, i],
            device_id=device(neg(c)),
            device_id_type=MESH,
        )

    def sol_message(c, slot):
        a = axis(c)
        part = (slot, side(c[a]))
        i = len(NBR) + FACES.index(c)
        return pltpu.make_async_remote_copy(
            src_ref=(tx, ty, tz)[a].at[part],
            dst_ref=(ux, uy, uz)[a].at[part],
            send_sem=send_sem.at[slot, i],
            recv_sem=recv_sem.at[slot, i],
            device_id=device(neg(c)),
            device_id_type=MESH,
        )

    def each(table, there, act):
        for c in table:

            @pl.when(exists(there(c)))
            def _(c=c):
                act(c)

    same = lambda c: c

    def send_flow(slot, first):
        each(NBR, neg, lambda c: flow_message(c, slot, first).start())

    def wait_flow(slot, first):
        each(NBR, neg, lambda c: flow_message(c, slot, first).wait_send())
        each(NBR, same, lambda c: flow_message(c, slot, first).wait_recv())

    def send_sol(slot):
        each(FACES, neg, lambda c: sol_message(c, slot).start())

    def wait_sol(slot):
        each(FACES, neg, lambda c: sol_message(c, slot).wait_send())
        each(FACES, same, lambda c: sol_message(c, slot).wait_recv())

    def clear_missing():
        for c in NBR:

            @pl.when(jnp.logical_not(exists(c)))
            def _(c=c):
                for k in range(2):
                    refs = [flow_refs(c, k, True)[1]]
                    if c in FACES:
                        refs.append((ux, uy, uz)[axis(c)].at[k, side(c[axis(c)])])
                    for ref in refs:
                        ref[...] = jnp.zeros(ref.shape, ref.dtype)

    def edge_row(value, s):
        return value[0:1] if s == 0 else value[7:8]

    def pack(acc, s, values):
        acc = pltpu.roll(acc, D - 1, 1)
        for q, value in enumerate(values):
            moved = pltpu.roll(value, q * SPAN + last_column, 1)
            acc = jnp.where(slot_lane[s] == q * SPAN, moved, acc)
        return acc

    def settle(face, s):
        return face if s == 0 else pltpu.roll(face, D - top, 1)

    def stage_flow(slot, first, cur, packed):
        for s in (0, 1):
            face = [settle(packed[s * H + h], s) for h in range(H)]
            for h in range(H):
                sz[slot, s, pl.ds(8 * h, 8), :] = face[h]
            for d, c in enumerate(YZ):
                if side(c[2]) == s:
                    syz[slot, d] = face[0][0:1] if c[1] > 0 else face[H - 1][7:8]
            for d, c in enumerate(XZ):
                if side(c[2]) == s:
                    column = 1 if c[0] > 0 else WX
                    q = FACE[2][s].index(FLOW_DIRS.index(c))
                    line = jnp.zeros((8, D), jnp.float32)
                    for at, qz in enumerate((q, NQ) if first else (q,)):
                        i = qz * SPAN + column
                        for h in range(H):
                            value = jnp.broadcast_to(face[h][:, i : i + 1], (8, D))
                            line = jnp.where(lane == row + (WY * at + 8 * h), value, line)
                    sxz[slot, d] = jnp.sum(line, axis=0, keepdims=True)
        for s in (0, 1):
            x = 1 if s == 0 else WX
            for q, p in enumerate(FACE[0][s]):
                sx[slot, s, q] = A[cur, p, x, pl.ds(Y0, WY), :]
            if first:
                sx[slot, s, NQ] = S[0, x, pl.ds(Y0, WY), :]
        for d, c in enumerate(XY):
            q = FACE[1][side(c[1])].index(FLOW_DIRS.index(c))
            x = 0 if c[0] > 0 else WX - 1
            sxy[slot, d, 0] = sy[slot, side(c[1]), q, pl.ds(x, 1), :]
            if first:
                sxy[slot, d, 1] = sy[slot, side(c[1]), NQ, pl.ds(x, 1), :]

    def column_of(line, start):
        line = jnp.broadcast_to(line, (8, D))
        return jnp.sum(jnp.where(lane == row + start, line, 0.0), axis=1, keepdims=True)

    def merge_flow(slot, first, cur):
        flag = [(NQ, None)] if first else []

        def put(p, x, rows, value):
            if p is None:
                S[0, x, rows, :] = value
            else:
                A[cur, p, x, rows, :] = value

        for s in (0, 1):
            x = WX + 1 if s == 0 else 0
            for q, p in list(enumerate(FACE[0][s])) + flag:
                put(p, x, pl.ds(Y0, WY), rx[slot, s, q])
            y = Y0 + WY if s == 0 else Y0 - 1
            for q, p in list(enumerate(FACE[1][s])) + flag:
                for half in range(WX // 8):
                    value = ry[slot, s, q, pl.ds(8 * half, 8), :]
                    for i in range(8):
                        put(p, 1 + 8 * half + i, pl.ds(y, 1), value[i : i + 1])
        for d, c in enumerate(XY):
            x = WX + 1 if c[0] > 0 else 0
            y = Y0 + WY if c[1] > 0 else Y0 - 1
            put(FLOW_DIRS.index(c), x, pl.ds(y, 1), rxy[slot, d, 0])
            if first:
                put(None, x, pl.ds(y, 1), rxy[slot, d, 1])
        for s in (0, 1):
            cz = 1 - 2 * s
            turn = (lambda v: pltpu.roll(v, top, 1)) if s == 0 else (lambda v: v)
            for h in range(H):
                face = rz[slot, s, pl.ds(8 * h, 8), :]
                for cx in (1, -1):
                    c = (cx, 0, cz)
                    q = FACE[2][s].index(FLOW_DIRS.index(c))
                    for at, qz in enumerate((q, NQ) if first else (q,)):
                        value = column_of(rxz[slot, XZ.index(c)], WY * at + 8 * h)
                        i = qz * SPAN + (WX + 1 if cx > 0 else 0)
                        face = jnp.where(lane == i, value, face)
                Zf[s, pl.ds(Y0 + 8 * h, 8), :] = turn(face)
            for y, cy in ((Y0 + WY, 1), (Y0 - 1, -1)):
                line = jnp.broadcast_to(ryz[slot, YZ.index((0, cy, cz))], (8, D))
                Zf[s, pl.ds(y, 1), :] = turn(line)[0:1]
            for t in range(3):
                face = Zf[s, pl.ds(Y0 - 1 + 8 * t, 8), :]
                for x in range(WX):
                    ZR[s, x, pl.ds(8 * t, 8), :] = pltpu.roll(face, D - x, 1) if x else face

    for c in copies[:6]:
        c.wait()

    zero = jnp.zeros((8, D), jnp.float32)
    for s in (0, 1):
        for part in range(0, WY + 16, 8):
            Zf[s, pl.ds(part, 8), :] = zero
    for part in (0, Y0 + WY):
        for x in range(WX + 2):
            S[0, x, pl.ds(part, 8), :] = zero

    blank = (zero,) * (2 * H)

    def stage_tile(slot, x, h, values, packed, flag=None):
        extra = [] if flag is None else [flag]
        for s in (0, 1):
            if h == (0 if s == 0 else H - 1):
                for q, value in enumerate([values[p] for p in FACE[1][s]] + extra):
                    sy[slot, s, q, pl.ds(x, 1), :] = edge_row(value, s)
            i = s * H + h
            packed[i] = pack(packed[i], s, [values[p] for p in FACE[2][s]] + extra)

    def stage_sol_tile(slot, x, h, values, packed):
        for s in (0, 1):
            if h == (0 if s == 0 else H - 1):
                ty[slot, s, pl.ds(x, 1), :] = edge_row(values[3 + s], s)
            i = s * H + h
            packed[i] = pack(packed[i], s, [values[5 + s]])

    def stage_sol(slot, cur, packed):
        for s in (0, 1):
            for h in range(H):
                tz[slot, s, pl.ds(8 * h, 8), :] = settle(packed[s * H + h], s)
            tx[slot, s] = B[cur, 1 + s, 1 if s == 0 else WX, pl.ds(Y0, WY), :]

    class Tiles:
        def __init__(self, ref, x, part):
            self.ref, self.x, self.part = ref, x, part

        def __getitem__(self, p):
            return self.ref[0, p, self.x + 1, self.part, :]

    def first_stage(x, packed):
        packed, other = list(packed[0]), list(packed[1])
        flags = solid[x].astype(jnp.float32)
        S[0, x + 1, pl.ds(Y0, WY), :] = flags
        for h in range(H):
            part = pl.ds(Y0 + 8 * h, 8)
            stage_tile(0, x, h, Tiles(A, x, part), packed, flags[8 * h : 8 * h + 8])
            stage_sol_tile(0, x, h, Tiles(B, x, part), other)
        return tuple(packed), tuple(other)

    packed, other = lax.fori_loop(0, WX, first_stage, (blank, blank))
    stage_flow(0, True, 0, packed)
    send_flow(0, True)
    stage_sol(0, 0, other)
    send_sol(0)
    clear_missing()
    for c in copies[6:]:
        c.wait()
    wait_flow(0, True)
    merge_flow(0, True, 0)
    for x in range(WX + 2):
        for t in range(0, WY + 16, 8):
            part = pl.ds(t, 8)
            flag = S[0, x, part, :]
            for s in (0, 1):
                halo = pltpu.roll(Zf[s, part, :], D - (NQ * SPAN + x), 1)
                moved = pltpu.roll(flag, D - 1 if s == 0 else 1, 1)
                S[1 + s, x, part, :] = jnp.where(edge[s], halo, moved)

    def solute_step(j, slot):
        t = steps - 1 - j
        cur = slot
        nxt = 1 - slot
        wait_sol(slot)
        for s in (0, 1):
            B[cur, 1 + s, WX + 1 if s == 0 else 0, pl.ds(Y0, WY), :] = ux[slot, s]
            y = Y0 + WY if s == 0 else Y0 - 1
            for half in range(WX // 8):
                value = uy[slot, s, pl.ds(8 * half, 8), :]
                for i in range(8):
                    B[cur, 3 + s, 1 + 8 * half + i, pl.ds(y, 1), :] = value[i : i + 1]
        halo = []
        for s in (0, 1):
            for h in range(H):
                face = uz[slot, s, pl.ds(8 * h, 8), :]
                halo.append(pltpu.roll(face, top - 1 if s == 0 else D - 1, 1))

        def body(x, carry):
            halo, packed = list(carry[0]), list(carry[1])
            level_ = lev[t, x].astype(jnp.float32)
            density_ = rho[t, x].astype(jnp.float32)
            u_ = [vel[t, i, x].astype(jnp.float32) for i in range(3)]
            for h in range(H):
                cut = slice(8 * h, 8 * h + 8)
                level, density, u = level_[cut], density_[cut], [v[cut] for v in u_]
                start = Y0 + 8 * h
                here = pl.ds(start, 8)
                hs = [B[cur, 0, x + 1, here, :]]
                for p in range(1, 7):
                    c = FLOW_DIRS[p]
                    rows = pl.ds(start + c[1], 8)
                    value = B[cur, p, x + 1 + c[0], rows, :]
                    if c[2]:
                        s = side(c[2])
                        value = pltpu.roll(value, D - 1 if s == 0 else 1, 1)
                        value = jnp.where(edge[s], halo[s * H + h], value)
                        flag = S[1 + s, x + 1, here, :]
                    else:
                        flag = S[0, x + 1 + c[0], rows, :]
                    hs.append(jnp.where(flag > 0.5, B[cur, OPP[p], x + 1, here, :], value))
                mx, my, mz = hs[1] - hs[2], hs[3] - hs[4], hs[5] - hs[6]
                m0 = 0.25 * hs[0] + 0.125 * ((hs[1] + hs[2]) + (hs[3] + hs[4]) + (hs[5] + hs[6]))
                along = mx * u[0] + my * u[1] + mz * u[2]
                one = 1.0 + level
                common = (solute_omega - langmuir_rate / (one * one)) * m0 + (
                    solute_omega * 0.5
                ) * along
                new = [(1.0 - solute_omega) * v + common for v in hs]
                for p in range(7):
                    B[nxt, p, x + 1, here, :] = new[p]
                stage_sol_tile(nxt, x, h, new, packed)
                factor = (0.5 * solute_omega) * level * (1.0 / density)
                speed = u[0] * u[0] + u[1] * u[1] + u[2] * u[2]
                saved = [factor * mx, factor * my, factor * mz, factor * along]
                for i, v in enumerate(saved + u + [1.0 + 1.5 * speed]):
                    PU[i, x, pl.ds(8 * h, 8), :] = v
            return tuple(pltpu.roll(v, D - 1, 1) for v in halo), tuple(packed)

        _, packed = lax.fori_loop(0, WX, body, (tuple(halo), blank))
        stage_sol(nxt, nxt, packed)

    def flow_tile(cur, x, h):
        start = Y0 + 8 * h

        def read(p):
            c = FLOW_DIRS[p]
            rows = pl.ds(start + c[1], 8)
            here = A[cur, p, x + 1 + c[0], rows, :]
            if c == (0, 0, 0):
                return here
            if c[2]:
                s = side(c[2])
                here = pltpu.roll(here, D - 1 if s == 0 else 1, 1)
                lift = FACE[2][s].index(p) * SPAN + 1 + c[0]
                halo = ZR[s, x, pl.ds(8 * h + 1 + c[1], 8), :]
                halo = pltpu.roll(halo, D - lift, 1) if lift else halo
                here = jnp.where(edge[s], halo, here)
                flag = S[1 + s, x + 1 + c[0], rows, :]
            else:
                flag = S[0, x + 1 + c[0], rows, :]
            back = A[cur, OPP[p], x + 1, pl.ds(start, 8), :]
            return jnp.where(flag > 0.5, back, here)

        part = pl.ds(8 * h, 8)
        px, py, pz, along, ux, uy, uz, stretch = [PU[i, x, part, :] for i in range(8)]
        g = [read(p) for p in range(NF)]
        a = [g[p] + g[p + 1] for p in range(1, NF, 2)]
        d = [g[p] - g[p + 1] for p in range(1, NF, 2)]
        ax, ay, az = 2.0 * a[0], 2.0 * a[1], 2.0 * a[2]
        sxy_, sxz_, syz_ = a[3] + a[4], a[5] + a[6], a[7] + a[8]
        qxy, qxz, qyz = a[3] - a[4], a[5] - a[6], a[7] - a[8]
        qxx, qyy, qzz = ax + sxy_ + sxz_, ay + sxy_ + syz_, az + sxz_ + syz_
        total = 12.0 * g[0] + (qxx + ay + az) + syz_
        jx = 2.0 * d[0] + (d[3] + d[4]) + (d[5] + d[6])
        jy = 2.0 * d[1] + (d[3] - d[4]) + (d[7] + d[8])
        jz = 2.0 * d[2] + (d[5] - d[6]) + (d[7] - d[8])
        vx = qxx * ux + qxy * uy + qxz * uz
        vy = qxy * ux + qyy * uy + qyz * uz
        vz = qxz * ux + qyz * uy + qzz * uz
        quad = vx * ux + vy * uy + vz * uz
        w = flow_omega / 36.0
        scalar = w * (total * stretch - 4.5 * quad) - along
        tx_ = (3.0 * w) * (jx + 3.0 * vx - ux * total) + px
        ty_ = (3.0 * w) * (jy + 3.0 * vy - uy * total) + py
        tz_ = (3.0 * w) * (jz + 3.0 * vz - uz * total) + pz
        rest = 1.0 - flow_omega
        new = [rest * g[0] + scalar]
        pairs = [tx_, ty_, tz_, tx_ + ty_, tx_ - ty_, tx_ + tz_, tx_ - tz_, ty_ + tz_, ty_ - tz_]
        for i, v in enumerate(pairs):
            p = 1 + 2 * i
            new.append(rest * g[p] + (scalar + v))
            new.append(rest * g[p + 1] + (scalar - v))
        return new

    solute_step(0, 0)
    send_sol(1)

    def step(k, carry):
        cur = lax.rem(k, 2)
        nxt = 1 - cur

        def body(x, packed):
            packed = list(packed)
            for h in range(H):
                new = flow_tile(cur, x, h)
                for p in range(NF):
                    A[nxt, p, x + 1, pl.ds(Y0 + 8 * h, 8), :] = new[p]
                stage_tile(nxt, x, h, new, packed)
            return tuple(packed)

        packed = lax.fori_loop(0, WX, body, blank)
        stage_flow(nxt, False, nxt, packed)
        send_flow(nxt, False)
        solute_step(k + 1, nxt)

        @pl.when(k < steps - 2)
        def _():
            send_sol(cur)

        wait_flow(nxt, False)
        merge_flow(nxt, False, nxt)
        return carry

    lax.fori_loop(0, steps - 1, step, 0)

    def last(x, carry):
        for h in range(H):
            new = flow_tile((steps - 1) % 2, x, h)
            part = pl.ds(8 * h, 8)
            here = pl.ds(Y0 + 8 * h, 8)
            keep = (S[0, x + 1, here, :] < 0.5) & (lane <= top)
            for p in range(NF):
                oflow[p, x, part, :] = jnp.where(keep, new[p], 0.0)
            for p in range(NP - NF):
                osol[p, x, part, :] = jnp.where(keep, B[steps % 2, p, x + 1, here, :], 0.0)
        return carry

    lax.fori_loop(0, WX, last, 0)


def solution(mesh):
    names = ("gx", "gy", "gz")
    sizes = tuple(mesh.shape[a] for a in names)

    def per_device(flow, solute, rho, vel, lev, solid, owner):
        WX, WY, D = solid.shape
        steps = rho.shape[0]
        f32 = jnp.float32
        V = pltpu.VMEM
        DMA = pltpu.SemaphoreType.DMA
        hbm = pl.BlockSpec(memory_space=pl.ANY)
        n = len(NBR) + len(FACES)
        faces = [
            V((2, 2, NQ + 1, WY, D), f32),
            V((2, 2, NQ + 1, WX, D), f32),
            V((2, 2, WY, D), f32),
            V((2, 4, 2, 1, D), f32),
            V((2, 4, 1, D), f32),
            V((2, 4, 1, D), f32),
        ]
        sides = [V((2, 2, WY, D), f32), V((2, 2, WX, D), f32), V((2, 2, WY, D), f32)]
        return pl.pallas_call(
            functools.partial(kernel, sizes, steps),
            out_shape=(
                jax.ShapeDtypeStruct(flow.shape, f32),
                jax.ShapeDtypeStruct(solute.shape, f32),
            ),
            in_specs=[pl.BlockSpec(memory_space=pltpu.SMEM)] + [hbm] * 6,
            out_specs=(pl.BlockSpec(memory_space=pltpu.VMEM),) * 2,
            scratch_shapes=[
                V((2, NF, WX + 2, WY + 16, D), f32),
                V((2, NP - NF, WX + 2, WY + 16, D), f32),
                V((3, WX + 2, WY + 16, D), f32),
                V((2, WY + 16, D), f32),
                V((2, WX, WY + 8, D), f32),
                V((8, WX, WY, D), f32),
                V(rho.shape, rho.dtype),
                V(vel.shape, vel.dtype),
                V(lev.shape, lev.dtype),
                V(solid.shape, solid.dtype),
            ]
            + (faces + sides) * 2
            + [DMA((9,)), DMA((2, n)), DMA((2, n))],
            compiler_params=pltpu.CompilerParams(
                collective_id=0, has_side_effects=True, vmem_limit_bytes=60 * 2**20
            ),
        )(owner, flow, solute, rho, vel, lev, solid)

    field = P(None, "gx", "gy", "gz")
    return jax.shard_map(
        per_device,
        mesh=mesh,
        in_specs=(field, field, field, P(None, None, "gx", "gy", "gz"), field, P("gx", "gy", "gz"), P()),
        out_specs=(field, field),
        check_vma=False,
    )
```

```python
import functools

import jax
import jax.numpy as jnp
from jax import lax
from jax.experimental import pallas as pl
from jax.experimental.pallas import tpu as pltpu
from jax.sharding import PartitionSpec as P

MESH = pl.DeviceIdType.MESH
BZC = 16

FLOW_DIRS = [
    (0, 0, 0),
    (1, 0, 0),
    (-1, 0, 0),
    (0, 1, 0),
    (0, -1, 0),
    (0, 0, 1),
    (0, 0, -1),
    (1, 1, 0),
    (-1, -1, 0),
    (1, -1, 0),
    (-1, 1, 0),
    (1, 0, 1),
    (-1, 0, -1),
    (1, 0, -1),
    (-1, 0, 1),
    (0, 1, 1),
    (0, -1, -1),
    (0, 1, -1),
    (0, -1, 1),
]
NF = 19
NP = NF + 7
OPP = [FLOW_DIRS.index((-c[0], -c[1], -c[2])) for c in FLOW_DIRS]
flow_omega = 1.25
solute_omega = 1.6
langmuir_rate = 0.05

FACE = [[[p for p in range(NF) if FLOW_DIRS[p][a] == s] for s in (1, -1)] for a in range(3)]
NQ = 5
SPAN = 18
FACES = FLOW_DIRS[1:7]
NBR = [c for c in FLOW_DIRS[1:] if c[2] and c[0]]
NBR += [c for c in FLOW_DIRS[1:] if c[2] and c[1]]
NBR += [c for c in FLOW_DIRS[1:] if c[2] and not c[0] and not c[1]]
NBR += [c for c in FLOW_DIRS[1:] if not c[2] and not (c[0] and c[1])]
NBR += [c for c in FLOW_DIRS[1:] if c[0] and c[1]]
XY = [c for c in NBR if c[0] and c[1]]
XZ = [c for c in NBR if c[0] and c[2]]
YZ = [c for c in NBR if c[1] and c[2]]
FLAT = [c for c in NBR if not c[2]]
UPDOWN = [c for c in NBR if c[2]]
U_FLOW, U_SOL = 2, 4
Y0 = 8


def side(step):
    return 0 if step > 0 else 1


def axis(c):
    return [i for i in range(3) if c[i]][0]


def neg(c):
    return (-c[0], -c[1], -c[2])


def kernel(
    sizes,
    steps,
    owner_ref,
    flow_hbm,
    sol_hbm,
    rho_hbm,
    vel_hbm,
    lev_hbm,
    solid_hbm,
    oflow,
    osol,
    A0,
    A1,
    B0,
    B1,
    S,
    Zf,
    ZR,
    PU,
    rho,
    vel,
    lev,
    solid,
    sx,
    sy,
    sz,
    sxy,
    sxz,
    syz,
    tx,
    ty,
    tz,
    rx,
    ry,
    rz,
    rxy,
    rxz,
    ryz,
    ux,
    uy,
    uz,
    in_sem,
    send_sem,
    recv_sem,
):
    WX, WY, D = solid.shape
    H = WY // 8
    A, B = (A0, A1), (B0, B1)
    names = ("gx", "gy", "gz")
    me = tuple(lax.axis_index(a) for a in names)

    inside = (pl.ds(1, WX), pl.ds(Y0, WY), slice(None))
    copies = [pltpu.make_async_copy(solid_hbm, solid, in_sem.at[0])]
    cuts = (0, 5, 10, 15, NF)
    for i, (lo, hi) in enumerate(zip(cuts, cuts[1:])):
        part = pl.ds(lo, hi - lo)
        copies.append(
            pltpu.make_async_copy(flow_hbm.at[part], A0.at[(part,) + inside], in_sem.at[1 + i])
        )
    copies.append(pltpu.make_async_copy(sol_hbm, B0.at[(slice(None),) + inside], in_sem.at[5]))
    copies.append(pltpu.make_async_copy(lev_hbm, lev, in_sem.at[6]))
    copies.append(pltpu.make_async_copy(vel_hbm, vel, in_sem.at[7]))
    copies.append(pltpu.make_async_copy(rho_hbm, rho, in_sem.at[8]))
    for c in copies:
        c.start()

    def exists(c):
        ok = None
        for a in range(3):
            if c[a] > 0:
                t = me[a] < sizes[a] - 1
            elif c[a] < 0:
                t = me[a] > 0
            else:
                continue
            ok = t if ok is None else jnp.logical_and(ok, t)
        return ok

    def device(c):
        return tuple(me[a] + c[a] for a in range(3))

    barrier = pltpu.get_barrier_semaphore()
    for c in NBR:

        @pl.when(exists(c))
        def _(c=c):
            pl.semaphore_signal(barrier, inc=1, device_id=device(c), device_id_type=MESH)

    count = jnp.int32(0)
    for i in range(owner_ref.shape[0]):
        count = count + (owner_ref[i] == me[2]).astype(jnp.int32)
    top = count * BZC - 1

    lane = lax.broadcasted_iota(jnp.int32, (8, D), 1)
    row = lax.broadcasted_iota(jnp.int32, (8, D), 0)
    edge = (lane == top, lane == 0)
    last_column = SPAN - 2
    slot_lane = (lane - last_column, (lane - (top + last_column) + 2 * D) % D)

    n = [
        (me[a] > 0).astype(jnp.int32) + (me[a] < sizes[a] - 1).astype(jnp.int32) for a in range(3)
    ]
    pl.semaphore_wait(
        barrier, n[0] + n[1] + n[2] + n[0] * n[1] + n[0] * n[2] + n[1] * n[2]
    )

    def flow_refs(c, slot, first):
        nq = NQ + 1 if first else NQ
        if c in XY:
            part = (slot, XY.index(c), pl.ds(0, nq - NQ + 1))
            return sxy.at[part], rxy.at[part]
        if c in XZ:
            part = (slot, XZ.index(c))
            return sxz.at[part], rxz.at[part]
        if c in YZ:
            part = (slot, YZ.index(c))
            return syz.at[part], ryz.at[part]
        a = axis(c)
        part = (slot, side(c[a]))
        if a == 2:
            return sz.at[part], rz.at[part]
        part = part + (pl.ds(0, nq),)
        return ((sx, rx), (sy, ry))[a][0].at[part], ((sx, rx), (sy, ry))[a][1].at[part]

    def flow_message(c, slot, first):
        src, dst = flow_refs(c, slot, first)
        i = NBR.index(c)
        return pltpu.make_async_remote_copy(
            src_ref=src,
            dst_ref=dst,
            send_sem=send_sem.at[slot, i],
            recv_sem=recv_sem.at[slot, i],
            device_id=device(neg(c)),
            device_id_type=MESH,
        )

    def sol_message(c, slot):
        a = axis(c)
        part = (slot, side(c[a]))
        i = len(NBR) + FACES.index(c)
        return pltpu.make_async_remote_copy(
            src_ref=(tx, ty, tz)[a].at[part],
            dst_ref=(ux, uy, uz)[a].at[part],
            send_sem=send_sem.at[slot, i],
            recv_sem=recv_sem.at[slot, i],
            device_id=device(neg(c)),
            device_id_type=MESH,
        )

    def each(table, there, act):
        for c in table:

            @pl.when(exists(there(c)))
            def _(c=c):
                act(c)

    same = lambda c: c

    def send_flow(slot, first):
        each(NBR, neg, lambda c: flow_message(c, slot, first).start())

    def wait_flow(slot, first):
        each(NBR, neg, lambda c: flow_message(c, slot, first).wait_send())
        each(FLAT, same, lambda c: flow_message(c, slot, first).wait_recv())
        merge_flat(slot, first, slot)
        each(UPDOWN, same, lambda c: flow_message(c, slot, first).wait_recv())
        merge_z(slot, first)

    def send_sol(slot):
        each(FACES, neg, lambda c: sol_message(c, slot).start())

    def wait_sol(slot):
        each(FACES, neg, lambda c: sol_message(c, slot).wait_send())
        each(FACES, same, lambda c: sol_message(c, slot).wait_recv())

    def clear_missing():
        for c in NBR:

            @pl.when(jnp.logical_not(exists(c)))
            def _(c=c):
                for k in range(2):
                    refs = [flow_refs(c, k, True)[1]]
                    if c in FACES:
                        refs.append((ux, uy, uz)[axis(c)].at[k, side(c[axis(c)])])
                    for ref in refs:
                        ref[...] = jnp.zeros(ref.shape, ref.dtype)

    def over_x(body, init, unroll):
        def trip(i, carry):
            for j in range(unroll):
                carry = body(unroll * i + j, carry)
            return carry

        return lax.fori_loop(0, WX // unroll, trip, init)

    def edge_row(value, s):
        return value[0:1] if s == 0 else value[7:8]

    def pack(acc, s, values):
        acc = pltpu.roll(acc, D - 1, 1)
        for q, value in enumerate(values):
            moved = pltpu.roll(value, q * SPAN + last_column, 1)
            acc = jnp.where(slot_lane[s] == q * SPAN, moved, acc)
        return acc

    def settle(face, s):
        return face if s == 0 else pltpu.roll(face, D - top, 1)

    def stage_flow(slot, first, cur, packed):
        for s in (0, 1):
            face = [settle(packed[s * H + h], s) for h in range(H)]
            for h in range(H):
                sz[slot, s, pl.ds(8 * h, 8), :] = face[h]
            for d, c in enumerate(YZ):
                if side(c[2]) == s:
                    syz[slot, d] = face[0][0:1] if c[1] > 0 else face[H - 1][7:8]
            for d, c in enumerate(XZ):
                if side(c[2]) == s:
                    column = 1 if c[0] > 0 else WX
                    q = FACE[2][s].index(FLOW_DIRS.index(c))
                    line = jnp.zeros((8, D), jnp.float32)
                    for at, qz in enumerate((q, NQ) if first else (q,)):
                        i = qz * SPAN + column
                        for h in range(H):
                            value = jnp.broadcast_to(face[h][:, i : i + 1], (8, D))
                            line = jnp.where(lane == row + (WY * at + 8 * h), value, line)
                    sxz[slot, d] = jnp.sum(line, axis=0, keepdims=True)
        for s in (0, 1):
            x = 1 if s == 0 else WX
            for q, p in enumerate(FACE[0][s]):
                sx[slot, s, q] = A[cur][p, x, pl.ds(Y0, WY), :]
            if first:
                sx[slot, s, NQ] = S[0, x, pl.ds(Y0, WY), :]
        for d, c in enumerate(XY):
            q = FACE[1][side(c[1])].index(FLOW_DIRS.index(c))
            x = 0 if c[0] > 0 else WX - 1
            sxy[slot, d, 0] = sy[slot, side(c[1]), q, pl.ds(x, 1), :]
            if first:
                sxy[slot, d, 1] = sy[slot, side(c[1]), NQ, pl.ds(x, 1), :]

    def column_of(line, start):
        line = jnp.broadcast_to(line, (8, D))
        return jnp.sum(jnp.where(lane == row + start, line, 0.0), axis=1, keepdims=True)

    def merge_flat(slot, first, cur):
        flag = [(NQ, None)] if first else []

        def put(p, x, rows, value):
            if p is None:
                S[0, x, rows, :] = value
            else:
                A[cur][p, x, rows, :] = value

        for s in (0, 1):
            x = WX + 1 if s == 0 else 0
            for q, p in list(enumerate(FACE[0][s])) + flag:
                put(p, x, pl.ds(Y0, WY), rx[slot, s, q])
            y = Y0 + WY if s == 0 else Y0 - 1
            for q, p in list(enumerate(FACE[1][s])) + flag:
                for half in range(WX // 8):
                    value = ry[slot, s, q, pl.ds(8 * half, 8), :]
                    for i in range(8):
                        put(p, 1 + 8 * half + i, pl.ds(y, 1), value[i : i + 1])
        for d, c in enumerate(XY):
            x = WX + 1 if c[0] > 0 else 0
            y = Y0 + WY if c[1] > 0 else Y0 - 1
            put(FLOW_DIRS.index(c), x, pl.ds(y, 1), rxy[slot, d, 0])
            if first:
                put(None, x, pl.ds(y, 1), rxy[slot, d, 1])

    def merge_z(slot, first):
        for s in (0, 1):
            cz = 1 - 2 * s
            turn = (lambda v: pltpu.roll(v, top, 1)) if s == 0 else (lambda v: v)
            for h in range(H):
                face = rz[slot, s, pl.ds(8 * h, 8), :]
                for cx in (1, -1):
                    c = (cx, 0, cz)
                    q = FACE[2][s].index(FLOW_DIRS.index(c))
                    for at, qz in enumerate((q, NQ) if first else (q,)):
                        value = column_of(rxz[slot, XZ.index(c)], WY * at + 8 * h)
                        i = qz * SPAN + (WX + 1 if cx > 0 else 0)
                        face = jnp.where(lane == i, value, face)
                Zf[s, pl.ds(Y0 + 8 * h, 8), :] = turn(face)
            for y, cy in ((Y0 + WY, 1), (Y0 - 1, -1)):
                line = jnp.broadcast_to(ryz[slot, YZ.index((0, cy, cz))], (8, D))
                Zf[s, pl.ds(y, 1), :] = turn(line)[0:1]
            for t in range(3):
                face = Zf[s, pl.ds(Y0 - 1 + 8 * t, 8), :]
                for x in range(WX):
                    ZR[s, x, pl.ds(8 * t, 8), :] = pltpu.roll(face, D - x, 1) if x else face

    for c in copies[:6]:
        c.wait()

    zero = jnp.zeros((8, D), jnp.float32)
    for s in (0, 1):
        for part in range(0, WY + 16, 8):
            Zf[s, pl.ds(part, 8), :] = zero
    for part in (0, Y0 + WY):
        for x in range(WX + 2):
            S[0, x, pl.ds(part, 8), :] = zero

    blank = (zero,) * (2 * H)

    def stage_tile(slot, x, h, values, packed, flag=None):
        extra = [] if flag is None else [flag]
        for s in (0, 1):
            if h == (0 if s == 0 else H - 1):
                for q, value in enumerate([values[p] for p in FACE[1][s]] + extra):
                    sy[slot, s, q, pl.ds(x, 1), :] = edge_row(value, s)
            i = s * H + h
            packed[i] = pack(packed[i], s, [values[p] for p in FACE[2][s]] + extra)

    def stage_sol_tile(slot, x, h, values, packed):
        for s in (0, 1):
            if h == (0 if s == 0 else H - 1):
                ty[slot, s, pl.ds(x, 1), :] = edge_row(values[3 + s], s)
            i = s * H + h
            packed[i] = pack(packed[i], s, [values[5 + s]])

    def stage_sol(slot, cur, packed):
        for s in (0, 1):
            for h in range(H):
                tz[slot, s, pl.ds(8 * h, 8), :] = settle(packed[s * H + h], s)
            tx[slot, s] = B[cur][1 + s, 1 if s == 0 else WX, pl.ds(Y0, WY), :]

    class Tiles:
        def __init__(self, ref, x, part):
            self.ref, self.x, self.part = ref, x, part

        def __getitem__(self, p):
            return self.ref[p, self.x + 1, self.part, :]

    def first_stage(x, packed):
        packed, other = list(packed[0]), list(packed[1])
        flags = solid[x].astype(jnp.float32)
        S[0, x + 1, pl.ds(Y0, WY), :] = flags
        for h in range(H):
            part = pl.ds(Y0 + 8 * h, 8)
            stage_tile(0, x, h, Tiles(A0, x, part), packed, flags[8 * h : 8 * h + 8])
            stage_sol_tile(0, x, h, Tiles(B0, x, part), other)
        return tuple(packed), tuple(other)

    packed, other = over_x(first_stage, (blank, blank), 2)
    stage_flow(0, True, 0, packed)
    send_flow(0, True)
    stage_sol(0, 0, other)
    send_sol(0)
    clear_missing()
    for c in copies[6:]:
        c.wait()
    wait_flow(0, True)
    for x in range(WX + 2):
        for t in range(0, WY + 16, 8):
            part = pl.ds(t, 8)
            flag = S[0, x, part, :]
            for s in (0, 1):
                halo = pltpu.roll(Zf[s, part, :], D - (NQ * SPAN + x), 1)
                moved = pltpu.roll(flag, D - 1 if s == 0 else 1, 1)
                S[1 + s, x, part, :] = jnp.where(edge[s], halo, moved)

    def solute_step(j, slot):
        t = steps - 1 - j
        cur = slot
        nxt = 1 - slot
        wait_sol(slot)
        for s in (0, 1):
            B[cur][1 + s, WX + 1 if s == 0 else 0, pl.ds(Y0, WY), :] = ux[slot, s]
            y = Y0 + WY if s == 0 else Y0 - 1
            for half in range(WX // 8):
                value = uy[slot, s, pl.ds(8 * half, 8), :]
                for i in range(8):
                    B[cur][3 + s, 1 + 8 * half + i, pl.ds(y, 1), :] = value[i : i + 1]
        halo = []
        for s in (0, 1):
            for h in range(H):
                face = uz[slot, s, pl.ds(8 * h, 8), :]
                halo.append(pltpu.roll(face, top - 1 if s == 0 else D - 1, 1))

        def body(x, carry):
            halo, packed = list(carry[0]), list(carry[1])
            level_ = lev[t, x].astype(jnp.float32)
            density_ = rho[t, x].astype(jnp.float32)
            u_ = [vel[t, i, x].astype(jnp.float32) for i in range(3)]
            for h in range(H):
                cut = slice(8 * h, 8 * h + 8)
                level, density, u = level_[cut], density_[cut], [v[cut] for v in u_]
                start = Y0 + 8 * h
                here = pl.ds(start, 8)
                hs = [B[cur][0, x + 1, here, :]]
                for p in range(1, 7):
                    c = FLOW_DIRS[p]
                    rows = pl.ds(start + c[1], 8)
                    value = B[cur][p, x + 1 + c[0], rows, :]
                    if c[2]:
                        s = side(c[2])
                        value = pltpu.roll(value, D - 1 if s == 0 else 1, 1)
                        value = jnp.where(edge[s], halo[s * H + h], value)
                        flag = S[1 + s, x + 1, here, :]
                    else:
                        flag = S[0, x + 1 + c[0], rows, :]
                    hs.append(jnp.where(flag > 0.5, B[cur][OPP[p], x + 1, here, :], value))
                mx, my, mz = hs[1] - hs[2], hs[3] - hs[4], hs[5] - hs[6]
                m0 = 0.25 * hs[0] + 0.125 * ((hs[1] + hs[2]) + (hs[3] + hs[4]) + (hs[5] + hs[6]))
                along = mx * u[0] + my * u[1] + mz * u[2]
                one = 1.0 + level
                common = (solute_omega - langmuir_rate / (one * one)) * m0 + (
                    solute_omega * 0.5
                ) * along
                new = [(1.0 - solute_omega) * v + common for v in hs]
                for p in range(7):
                    B[nxt][p, x + 1, here, :] = new[p]
                stage_sol_tile(nxt, x, h, new, packed)
                factor = (0.5 * solute_omega) * level * (1.0 / density)
                speed = u[0] * u[0] + u[1] * u[1] + u[2] * u[2]
                saved = [factor * mx, factor * my, factor * mz, factor * along]
                for i, v in enumerate(saved + u + [1.0 + 1.5 * speed]):
                    PU[i, x, pl.ds(8 * h, 8), :] = v
            return tuple(pltpu.roll(v, D - 1, 1) for v in halo), tuple(packed)

        _, packed = over_x(body, (tuple(halo), blank), U_SOL)
        stage_sol(nxt, nxt, packed)

    def flow_tile(cur, x, h):
        start = Y0 + 8 * h

        def read(p):
            c = FLOW_DIRS[p]
            rows = pl.ds(start + c[1], 8)
            here = A[cur][p, x + 1 + c[0], rows, :]
            if c == (0, 0, 0):
                return here
            if c[2]:
                s = side(c[2])
                here = pltpu.roll(here, D - 1 if s == 0 else 1, 1)
                lift = FACE[2][s].index(p) * SPAN + 1 + c[0]
                halo = ZR[s, x, pl.ds(8 * h + 1 + c[1], 8), :]
                halo = pltpu.roll(halo, D - lift, 1) if lift else halo
                here = jnp.where(edge[s], halo, here)
                flag = S[1 + s, x + 1 + c[0], rows, :]
            else:
                flag = S[0, x + 1 + c[0], rows, :]
            back = A[cur][OPP[p], x + 1, pl.ds(start, 8), :]
            return jnp.where(flag > 0.5, back, here)

        part = pl.ds(8 * h, 8)
        px, py, pz, along, ux, uy, uz, stretch = [PU[i, x, part, :] for i in range(8)]
        g = [read(p) for p in range(NF)]
        a = [g[p] + g[p + 1] for p in range(1, NF, 2)]
        d = [g[p] - g[p + 1] for p in range(1, NF, 2)]
        ax, ay, az = 2.0 * a[0], 2.0 * a[1], 2.0 * a[2]
        sxy_, sxz_, syz_ = a[3] + a[4], a[5] + a[6], a[7] + a[8]
        qxy, qxz, qyz = a[3] - a[4], a[5] - a[6], a[7] - a[8]
        qxx, qyy, qzz = ax + sxy_ + sxz_, ay + sxy_ + syz_, az + sxz_ + syz_
        total = 12.0 * g[0] + (qxx + ay + az) + syz_
        jx = 2.0 * d[0] + (d[3] + d[4]) + (d[5] + d[6])
        jy = 2.0 * d[1] + (d[3] - d[4]) + (d[7] + d[8])
        jz = 2.0 * d[2] + (d[5] - d[6]) + (d[7] - d[8])
        vx = qxx * ux + qxy * uy + qxz * uz
        vy = qxy * ux + qyy * uy + qyz * uz
        vz = qxz * ux + qyz * uy + qzz * uz
        quad = vx * ux + vy * uy + vz * uz
        w = flow_omega / 36.0
        scalar = w * (total * stretch - 4.5 * quad) - along
        tx_ = (3.0 * w) * (jx + 3.0 * vx - ux * total) + px
        ty_ = (3.0 * w) * (jy + 3.0 * vy - uy * total) + py
        tz_ = (3.0 * w) * (jz + 3.0 * vz - uz * total) + pz
        rest = 1.0 - flow_omega
        new = [rest * g[0] + scalar]
        pairs = [tx_, ty_, tz_, tx_ + ty_, tx_ - ty_, tx_ + tz_, tx_ - tz_, ty_ + tz_, ty_ - tz_]
        for i, v in enumerate(pairs):
            p = 1 + 2 * i
            new.append(rest * g[p] + (scalar + v))
            new.append(rest * g[p + 1] + (scalar - v))
        return new

    solute_step(0, 0)
    send_sol(1)

    def step(k):
        cur = k % 2
        nxt = 1 - cur

        def body(x, packed):
            packed = list(packed)
            for h in range(H):
                new = flow_tile(cur, x, h)
                for p in range(NF):
                    A[nxt][p, x + 1, pl.ds(Y0 + 8 * h, 8), :] = new[p]
                stage_tile(nxt, x, h, new, packed)
            return tuple(packed)

        packed = over_x(body, blank, U_FLOW)
        stage_flow(nxt, False, nxt, packed)
        send_flow(nxt, False)
        solute_step(k + 1, nxt)

        if k < steps - 2:
            send_sol(cur)
        wait_flow(nxt, False)

    for k in range(steps - 1):
        step(k)

    def last(x, carry):
        for h in range(H):
            new = flow_tile((steps - 1) % 2, x, h)
            part = pl.ds(8 * h, 8)
            here = pl.ds(Y0 + 8 * h, 8)
            keep = (S[0, x + 1, here, :] < 0.5) & (lane <= top)
            for p in range(NF):
                oflow[p, x, part, :] = jnp.where(keep, new[p], 0.0)
            for p in range(NP - NF):
                osol[p, x, part, :] = jnp.where(keep, B[steps % 2][p, x + 1, here, :], 0.0)
        return carry

    over_x(last, 0, U_FLOW)


def solution(mesh):
    names = ("gx", "gy", "gz")
    sizes = tuple(mesh.shape[a] for a in names)

    def per_device(flow, solute, rho, vel, lev, solid, owner):
        WX, WY, D = solid.shape
        steps = rho.shape[0]
        f32 = jnp.float32
        V = pltpu.VMEM
        DMA = pltpu.SemaphoreType.DMA
        hbm = pl.BlockSpec(memory_space=pl.ANY)
        n = len(NBR) + len(FACES)
        faces = [
            V((2, 2, NQ + 1, WY, D), f32),
            V((2, 2, NQ + 1, WX, D), f32),
            V((2, 2, WY, D), f32),
            V((2, 4, 2, 1, D), f32),
            V((2, 4, 1, D), f32),
            V((2, 4, 1, D), f32),
        ]
        sides = [V((2, 2, WY, D), f32), V((2, 2, WX, D), f32), V((2, 2, WY, D), f32)]
        return pl.pallas_call(
            functools.partial(kernel, sizes, steps),
            out_shape=(
                jax.ShapeDtypeStruct(flow.shape, f32),
                jax.ShapeDtypeStruct(solute.shape, f32),
            ),
            in_specs=[pl.BlockSpec(memory_space=pltpu.SMEM)] + [hbm] * 6,
            out_specs=(pl.BlockSpec(memory_space=pltpu.VMEM),) * 2,
            scratch_shapes=[
                V((NF, WX + 2, WY + 16, D), f32),
                V((NF, WX + 2, WY + 16, D), f32),
                V((NP - NF, WX + 2, WY + 16, D), f32),
                V((NP - NF, WX + 2, WY + 16, D), f32),
                V((3, WX + 2, WY + 16, D), f32),
                V((2, WY + 16, D), f32),
                V((2, WX, WY + 8, D), f32),
                V((8, WX, WY, D), f32),
                V(rho.shape, rho.dtype),
                V(vel.shape, vel.dtype),
                V(lev.shape, lev.dtype),
                V(solid.shape, solid.dtype),
            ]
            + (faces + sides) * 2
            + [DMA((9,)), DMA((2, n)), DMA((2, n))],
            compiler_params=pltpu.CompilerParams(
                collective_id=0, has_side_effects=True, vmem_limit_bytes=60 * 2**20
            ),
        )(owner, flow, solute, rho, vel, lev, solid)

    field = P(None, "gx", "gy", "gz")
    return jax.shard_map(
        per_device,
        mesh=mesh,
        in_specs=(field, field, field, P(None, None, "gx", "gy", "gz"), field, P("gx", "gy", "gz"), P()),
        out_specs=(field, field),
        check_vma=False,
    )
```

```python
import functools

import jax
import jax.numpy as jnp
from jax import lax
from jax.experimental import pallas as pl
from jax.experimental.pallas import tpu as pltpu
from jax.sharding import PartitionSpec as P

MESH = pl.DeviceIdType.MESH
BZC = 16

FLOW_DIRS = [
    (0, 0, 0),
    (1, 0, 0),
    (-1, 0, 0),
    (0, 1, 0),
    (0, -1, 0),
    (0, 0, 1),
    (0, 0, -1),
    (1, 1, 0),
    (-1, -1, 0),
    (1, -1, 0),
    (-1, 1, 0),
    (1, 0, 1),
    (-1, 0, -1),
    (1, 0, -1),
    (-1, 0, 1),
    (0, 1, 1),
    (0, -1, -1),
    (0, 1, -1),
    (0, -1, 1),
]
NF = 19
NP = NF + 7
OPP = [FLOW_DIRS.index((-c[0], -c[1], -c[2])) for c in FLOW_DIRS]
flow_omega = 1.25
solute_omega = 1.6
langmuir_rate = 0.05

FACE = [[[p for p in range(NF) if FLOW_DIRS[p][a] == s] for s in (1, -1)] for a in range(3)]
NQ = 5
SPAN = 18
FACES = FLOW_DIRS[1:7]
NBR = [c for c in FLOW_DIRS[1:] if c[2] and c[0]]
NBR += [c for c in FLOW_DIRS[1:] if c[2] and c[1]]
NBR += [c for c in FLOW_DIRS[1:] if c[2] and not c[0] and not c[1]]
NBR += [c for c in FLOW_DIRS[1:] if not c[2] and not (c[0] and c[1])]
NBR += [c for c in FLOW_DIRS[1:] if c[0] and c[1]]
XY = [c for c in NBR if c[0] and c[1]]
XZ = [c for c in NBR if c[0] and c[2]]
YZ = [c for c in NBR if c[1] and c[2]]
FLAT = [c for c in NBR if not c[2]]
UPDOWN = [c for c in NBR if c[2]]
U_FLOW, U_SOL = 2, 4
Y0 = 8


def side(step):
    return 0 if step > 0 else 1


def axis(c):
    return [i for i in range(3) if c[i]][0]


def neg(c):
    return (-c[0], -c[1], -c[2])


def kernel(
    sizes,
    steps,
    owner_ref,
    flow_hbm,
    sol_hbm,
    rho_hbm,
    vel_hbm,
    lev_hbm,
    solid_hbm,
    oflow,
    osol,
    A0,
    A1,
    B0,
    B1,
    S,
    Zf,
    ZR,
    PU,
    rho,
    vel,
    lev,
    solid,
    sx,
    sy,
    sz,
    sxy,
    sxz,
    syz,
    tx,
    ty,
    tz,
    rx,
    ry,
    rz,
    rxy,
    rxz,
    ryz,
    ux,
    uy,
    uz,
    in_sem,
    send_sem,
    recv_sem,
):
    WX, WY, D = solid.shape
    H = WY // 8
    A, B = (A0, A1), (B0, B1)
    names = ("gx", "gy", "gz")
    me = tuple(lax.axis_index(a) for a in names)

    inside = (pl.ds(1, WX), pl.ds(Y0, WY), slice(None))
    copies = [pltpu.make_async_copy(solid_hbm, solid, in_sem.at[0])]
    cuts = (0, 5, 10, 15, NF)
    for i, (lo, hi) in enumerate(zip(cuts, cuts[1:])):
        part = pl.ds(lo, hi - lo)
        copies.append(
            pltpu.make_async_copy(flow_hbm.at[part], A0.at[(part,) + inside], in_sem.at[1 + i])
        )
    copies.append(pltpu.make_async_copy(sol_hbm, B0.at[(slice(None),) + inside], in_sem.at[5]))
    copies.append(pltpu.make_async_copy(lev_hbm, lev, in_sem.at[6]))
    copies.append(pltpu.make_async_copy(vel_hbm, vel, in_sem.at[7]))
    copies.append(pltpu.make_async_copy(rho_hbm, rho, in_sem.at[8]))
    for c in copies:
        c.start()

    def exists(c):
        ok = None
        for a in range(3):
            if c[a] > 0:
                t = me[a] < sizes[a] - 1
            elif c[a] < 0:
                t = me[a] > 0
            else:
                continue
            ok = t if ok is None else jnp.logical_and(ok, t)
        return ok

    def device(c):
        return tuple(me[a] + c[a] for a in range(3))

    barrier = pltpu.get_barrier_semaphore()
    for c in NBR:

        @pl.when(exists(c))
        def _(c=c):
            pl.semaphore_signal(barrier, inc=1, device_id=device(c), device_id_type=MESH)

    count = jnp.int32(0)
    for i in range(owner_ref.shape[0]):
        count = count + (owner_ref[i] == me[2]).astype(jnp.int32)
    top = count * BZC - 1

    lane = lax.broadcasted_iota(jnp.int32, (8, D), 1)
    row = lax.broadcasted_iota(jnp.int32, (8, D), 0)
    edge = (lane == top, lane == 0)
    last_column = SPAN - 2
    slot_lane = (lane - last_column, lax.rem(lane - (top + last_column - SPAN) + 2 * D, D) - SPAN)

    n = [
        (me[a] > 0).astype(jnp.int32) + (me[a] < sizes[a] - 1).astype(jnp.int32) for a in range(3)
    ]
    pl.semaphore_wait(
        barrier, n[0] + n[1] + n[2] + n[0] * n[1] + n[0] * n[2] + n[1] * n[2]
    )

    def flow_refs(c, slot, first):
        nq = NQ + 1 if first else NQ
        if c in XY:
            part = (slot, XY.index(c), pl.ds(0, nq - NQ + 1))
            return sxy.at[part], rxy.at[part]
        if c in XZ:
            part = (slot, XZ.index(c))
            return sxz.at[part], rxz.at[part]
        if c in YZ:
            part = (slot, YZ.index(c))
            return syz.at[part], ryz.at[part]
        a = axis(c)
        part = (slot, side(c[a]))
        if a == 2:
            return sz.at[part], rz.at[part]
        part = part + (pl.ds(0, nq),)
        return ((sx, rx), (sy, ry))[a][0].at[part], ((sx, rx), (sy, ry))[a][1].at[part]

    def flow_message(c, slot, first):
        src, dst = flow_refs(c, slot, first)
        i = NBR.index(c)
        return pltpu.make_async_remote_copy(
            src_ref=src,
            dst_ref=dst,
            send_sem=send_sem.at[slot, i],
            recv_sem=recv_sem.at[slot, i],
            device_id=device(neg(c)),
            device_id_type=MESH,
        )

    def sol_message(c, slot):
        a = axis(c)
        part = (slot, side(c[a]))
        i = len(NBR) + FACES.index(c)
        return pltpu.make_async_remote_copy(
            src_ref=(tx, ty, tz)[a].at[part],
            dst_ref=(ux, uy, uz)[a].at[part],
            send_sem=send_sem.at[slot, i],
            recv_sem=recv_sem.at[slot, i],
            device_id=device(neg(c)),
            device_id_type=MESH,
        )

    def each(table, there, act):
        for c in table:

            @pl.when(exists(there(c)))
            def _(c=c):
                act(c)

    same = lambda c: c

    def send_flow(slot, first):
        each(NBR, neg, lambda c: flow_message(c, slot, first).start())

    def wait_flow(slot, first):
        each(NBR, neg, lambda c: flow_message(c, slot, first).wait_send())
        each(FLAT, same, lambda c: flow_message(c, slot, first).wait_recv())
        merge_flat(slot, first, slot)
        each(UPDOWN, same, lambda c: flow_message(c, slot, first).wait_recv())
        merge_z(slot, first)

    def send_sol(slot):
        each(FACES, neg, lambda c: sol_message(c, slot).start())

    def wait_sol(slot):
        each(FACES, neg, lambda c: sol_message(c, slot).wait_send())
        each(FACES, same, lambda c: sol_message(c, slot).wait_recv())

    def clear_missing():
        for c in NBR:

            @pl.when(jnp.logical_not(exists(c)))
            def _(c=c):
                for k in range(2):
                    refs = [flow_refs(c, k, True)[1]]
                    if c in FACES:
                        refs.append((ux, uy, uz)[axis(c)].at[k, side(c[axis(c)])])
                    for ref in refs:
                        ref[...] = jnp.zeros(ref.shape, ref.dtype)

    def over_x(body, init, unroll):
        def trip(i, carry):
            for j in range(unroll):
                carry = body(unroll * i + j, carry, j, unroll)
            return carry

        return lax.fori_loop(0, WX // unroll, trip, init)

    def edge_row(value, s):
        return value[0:1] if s == 0 else value[7:8]

    def pack(acc, s, values, j, unroll):
        if j == 0:
            acc = pltpu.roll(acc, D - unroll, 1)
        back = unroll - 1 - j
        for q, value in enumerate(values):
            moved = pltpu.roll(value, q * SPAN + last_column - back, 1)
            acc = jnp.where(slot_lane[s] == q * SPAN - back, moved, acc)
        return acc

    def settle(face, s):
        return face if s == 0 else pltpu.roll(face, D - top, 1)

    def stage_flow(slot, first, cur, packed):
        for s in (0, 1):
            face = [settle(packed[s * H + h], s) for h in range(H)]
            for h in range(H):
                sz[slot, s, pl.ds(8 * h, 8), :] = face[h]
            for d, c in enumerate(YZ):
                if side(c[2]) == s:
                    syz[slot, d] = face[0][0:1] if c[1] > 0 else face[H - 1][7:8]
            for d, c in enumerate(XZ):
                if side(c[2]) == s:
                    column = 1 if c[0] > 0 else WX
                    q = FACE[2][s].index(FLOW_DIRS.index(c))
                    line = jnp.zeros((8, D), jnp.float32)
                    for at, qz in enumerate((q, NQ) if first else (q,)):
                        i = qz * SPAN + column
                        for h in range(H):
                            value = jnp.broadcast_to(face[h][:, i : i + 1], (8, D))
                            line = jnp.where(lane == row + (WY * at + 8 * h), value, line)
                    sxz[slot, d] = jnp.sum(line, axis=0, keepdims=True)
        for s in (0, 1):
            x = 1 if s == 0 else WX
            for q, p in enumerate(FACE[0][s]):
                sx[slot, s, q] = A[cur][p, x, pl.ds(Y0, WY), :]
            if first:
                sx[slot, s, NQ] = S[0, x, pl.ds(Y0, WY), :]
        for d, c in enumerate(XY):
            q = FACE[1][side(c[1])].index(FLOW_DIRS.index(c))
            x = 0 if c[0] > 0 else WX - 1
            sxy[slot, d, 0] = sy[slot, side(c[1]), q, pl.ds(x, 1), :]
            if first:
                sxy[slot, d, 1] = sy[slot, side(c[1]), NQ, pl.ds(x, 1), :]

    def column_of(line, start):
        line = jnp.broadcast_to(line, (8, D))
        return jnp.sum(jnp.where(lane == row + start, line, 0.0), axis=1, keepdims=True)

    def merge_flat(slot, first, cur):
        flag = [(NQ, None)] if first else []

        def put(p, x, rows, value):
            if p is None:
                S[0, x, rows, :] = value
            else:
                A[cur][p, x, rows, :] = value

        for s in (0, 1):
            x = WX + 1 if s == 0 else 0
            for q, p in list(enumerate(FACE[0][s])) + flag:
                put(p, x, pl.ds(Y0, WY), rx[slot, s, q])
            y = Y0 + WY if s == 0 else Y0 - 1
            for q, p in list(enumerate(FACE[1][s])) + flag:
                for half in range(WX // 8):
                    value = ry[slot, s, q, pl.ds(8 * half, 8), :]
                    for i in range(8):
                        put(p, 1 + 8 * half + i, pl.ds(y, 1), value[i : i + 1])
        for d, c in enumerate(XY):
            x = WX + 1 if c[0] > 0 else 0
            y = Y0 + WY if c[1] > 0 else Y0 - 1
            put(FLOW_DIRS.index(c), x, pl.ds(y, 1), rxy[slot, d, 0])
            if first:
                put(None, x, pl.ds(y, 1), rxy[slot, d, 1])

    def merge_z(slot, first):
        for s in (0, 1):
            cz = 1 - 2 * s
            turn = (lambda v: pltpu.roll(v, top, 1)) if s == 0 else (lambda v: v)
            for h in range(H):
                face = rz[slot, s, pl.ds(8 * h, 8), :]
                for cx in (1, -1):
                    c = (cx, 0, cz)
                    q = FACE[2][s].index(FLOW_DIRS.index(c))
                    for at, qz in enumerate((q, NQ) if first else (q,)):
                        value = column_of(rxz[slot, XZ.index(c)], WY * at + 8 * h)
                        i = qz * SPAN + (WX + 1 if cx > 0 else 0)
                        face = jnp.where(lane == i, value, face)
                Zf[s, pl.ds(Y0 + 8 * h, 8), :] = turn(face)
            for y, cy in ((Y0 + WY, 1), (Y0 - 1, -1)):
                line = jnp.broadcast_to(ryz[slot, YZ.index((0, cy, cz))], (8, D))
                Zf[s, pl.ds(y, 1), :] = turn(line)[0:1]
            for t in range(3):
                face = Zf[s, pl.ds(Y0 - 1 + 8 * t, 8), :]
                for x in range(WX):
                    ZR[s, x, pl.ds(8 * t, 8), :] = pltpu.roll(face, D - x, 1) if x else face

    for c in copies[:6]:
        c.wait()

    zero = jnp.zeros((8, D), jnp.float32)
    for s in (0, 1):
        for part in range(0, WY + 16, 8):
            Zf[s, pl.ds(part, 8), :] = zero
    for part in (0, Y0 + WY):
        for x in range(WX + 2):
            S[0, x, pl.ds(part, 8), :] = zero

    blank = (zero,) * (2 * H)

    def stage_tile(slot, x, h, values, packed, trip, flag=None):
        extra = [] if flag is None else [flag]
        for s in (0, 1):
            if h == (0 if s == 0 else H - 1):
                for q, value in enumerate([values[p] for p in FACE[1][s]] + extra):
                    sy[slot, s, q, pl.ds(x, 1), :] = edge_row(value, s)
            i = s * H + h
            packed[i] = pack(packed[i], s, [values[p] for p in FACE[2][s]] + extra, *trip)

    def stage_sol_tile(slot, x, h, values, packed, trip):
        for s in (0, 1):
            if h == (0 if s == 0 else H - 1):
                ty[slot, s, pl.ds(x, 1), :] = edge_row(values[3 + s], s)
            i = s * H + h
            packed[i] = pack(packed[i], s, [values[5 + s]], *trip)

    def stage_sol(slot, cur, packed):
        for s in (0, 1):
            for h in range(H):
                tz[slot, s, pl.ds(8 * h, 8), :] = settle(packed[s * H + h], s)
            tx[slot, s] = B[cur][1 + s, 1 if s == 0 else WX, pl.ds(Y0, WY), :]

    class Tiles:
        def __init__(self, ref, x, part):
            self.ref, self.x, self.part = ref, x, part

        def __getitem__(self, p):
            return self.ref[p, self.x + 1, self.part, :]

    def first_stage(x, packed, *trip):
        packed, other = list(packed[0]), list(packed[1])
        flags = solid[x].astype(jnp.float32)
        S[0, x + 1, pl.ds(Y0, WY), :] = flags
        for h in range(H):
            part = pl.ds(Y0 + 8 * h, 8)
            stage_tile(0, x, h, Tiles(A0, x, part), packed, trip, flags[8 * h : 8 * h + 8])
            stage_sol_tile(0, x, h, Tiles(B0, x, part), other, trip)
        return tuple(packed), tuple(other)

    packed, other = over_x(first_stage, (blank, blank), 4)
    stage_flow(0, True, 0, packed)
    send_flow(0, True)
    stage_sol(0, 0, other)
    send_sol(0)
    clear_missing()
    for c in copies[6:]:
        c.wait()
    wait_flow(0, True)
    for x in range(WX + 2):
        for t in range(0, WY + 16, 8):
            part = pl.ds(t, 8)
            flag = S[0, x, part, :]
            for s in (0, 1):
                halo = pltpu.roll(Zf[s, part, :], D - (NQ * SPAN + x), 1)
                moved = pltpu.roll(flag, D - 1 if s == 0 else 1, 1)
                S[1 + s, x, part, :] = jnp.where(edge[s], halo, moved)

    def solute_step(j, slot):
        t = steps - 1 - j
        cur = slot
        nxt = 1 - slot
        wait_sol(slot)
        for s in (0, 1):
            B[cur][1 + s, WX + 1 if s == 0 else 0, pl.ds(Y0, WY), :] = ux[slot, s]
            y = Y0 + WY if s == 0 else Y0 - 1
            for half in range(WX // 8):
                value = uy[slot, s, pl.ds(8 * half, 8), :]
                for i in range(8):
                    B[cur][3 + s, 1 + 8 * half + i, pl.ds(y, 1), :] = value[i : i + 1]
        halo = []
        for s in (0, 1):
            for h in range(H):
                face = uz[slot, s, pl.ds(8 * h, 8), :]
                halo.append(pltpu.roll(face, top - 1 if s == 0 else D - 1, 1))

        def body(x, carry, *trip):
            halo, packed = list(carry[0]), list(carry[1])
            level_ = lev[t, x].astype(jnp.float32)
            density_ = rho[t, x].astype(jnp.float32)
            u_ = [vel[t, i, x].astype(jnp.float32) for i in range(3)]
            for h in range(H):
                cut = slice(8 * h, 8 * h + 8)
                level, density, u = level_[cut], density_[cut], [v[cut] for v in u_]
                start = Y0 + 8 * h
                here = pl.ds(start, 8)
                hs = [B[cur][0, x + 1, here, :]]
                for p in range(1, 7):
                    c = FLOW_DIRS[p]
                    rows = pl.ds(start + c[1], 8)
                    value = B[cur][p, x + 1 + c[0], rows, :]
                    if c[2]:
                        s = side(c[2])
                        value = pltpu.roll(value, D - 1 if s == 0 else 1, 1)
                        value = jnp.where(edge[s], halo[s * H + h], value)
                        flag = S[1 + s, x + 1, here, :]
                    else:
                        flag = S[0, x + 1 + c[0], rows, :]
                    hs.append(jnp.where(flag > 0.5, B[cur][OPP[p], x + 1, here, :], value))
                mx, my, mz = hs[1] - hs[2], hs[3] - hs[4], hs[5] - hs[6]
                m0 = 0.25 * hs[0] + 0.125 * ((hs[1] + hs[2]) + (hs[3] + hs[4]) + (hs[5] + hs[6]))
                along = mx * u[0] + my * u[1] + mz * u[2]
                one = 1.0 + level
                common = (solute_omega - langmuir_rate / (one * one)) * m0 + (
                    solute_omega * 0.5
                ) * along
                new = [(1.0 - solute_omega) * v + common for v in hs]
                for p in range(7):
                    B[nxt][p, x + 1, here, :] = new[p]
                stage_sol_tile(nxt, x, h, new, packed, trip)
                factor = (0.5 * solute_omega) * level * (1.0 / density)
                speed = u[0] * u[0] + u[1] * u[1] + u[2] * u[2]
                saved = [factor * mx, factor * my, factor * mz, factor * along]
                for i, v in enumerate(saved + u + [1.0 + 1.5 * speed]):
                    PU[i, x, pl.ds(8 * h, 8), :] = v
            return tuple(pltpu.roll(v, D - 1, 1) for v in halo), tuple(packed)

        _, packed = over_x(body, (tuple(halo), blank), U_SOL)
        stage_sol(nxt, nxt, packed)

    def flow_tile(cur, x, h, sign=1.0):
        start = Y0 + 8 * h

        def read(p):
            c = FLOW_DIRS[p]
            rows = pl.ds(start + c[1], 8)
            here = A[cur][p, x + 1 + c[0], rows, :]
            if c == (0, 0, 0):
                return here
            if c[2]:
                s = side(c[2])
                here = pltpu.roll(here, D - 1 if s == 0 else 1, 1)
                lift = FACE[2][s].index(p) * SPAN + 1 + c[0]
                halo = ZR[s, x, pl.ds(8 * h + 1 + c[1], 8), :]
                halo = pltpu.roll(halo, D - lift, 1) if lift else halo
                here = jnp.where(edge[s], halo, here)
                flag = S[1 + s, x + 1 + c[0], rows, :]
            else:
                flag = S[0, x + 1 + c[0], rows, :]
            back = A[cur][OPP[p], x + 1, pl.ds(start, 8), :]
            return jnp.where(flag > 0.5, back, here)

        part = pl.ds(8 * h, 8)
        px, py, pz, along, ux, uy, uz, stretch = [PU[i, x, part, :] for i in range(8)]
        g = [read(p) for p in range(NF)]
        a = [g[p] + g[p + 1] for p in range(1, NF, 2)]
        d = [g[p] - g[p + 1] for p in range(1, NF, 2)]
        ax, ay, az = 2.0 * a[0], 2.0 * a[1], 2.0 * a[2]
        sxy_, sxz_, syz_ = a[3] + a[4], a[5] + a[6], a[7] + a[8]
        qxy, qxz, qyz = a[3] - a[4], a[5] - a[6], a[7] - a[8]
        qxx, qyy, qzz = ax + sxy_ + sxz_, ay + sxy_ + syz_, az + sxz_ + syz_
        total = 12.0 * g[0] + (qxx + ay + az) + syz_
        jx = 2.0 * d[0] + (d[3] + d[4]) + (d[5] + d[6])
        jy = 2.0 * d[1] + (d[3] - d[4]) + (d[7] + d[8])
        jz = 2.0 * d[2] + (d[5] - d[6]) + (d[7] - d[8])
        vx = qxx * ux + qxy * uy + qxz * uz
        vy = qxy * ux + qyy * uy + qyz * uz
        vz = qxz * ux + qyz * uy + qzz * uz
        quad = vx * ux + vy * uy + vz * uz
        w = sign * flow_omega / 36.0
        if sign < 0:
            px, py, pz, along = -px, -py, -pz, -along
        scalar = w * (total * stretch - 4.5 * quad) - along
        tx_ = (3.0 * w) * (jx + 3.0 * vx - ux * total) + px
        ty_ = (3.0 * w) * (jy + 3.0 * vy - uy * total) + py
        tz_ = (3.0 * w) * (jz + 3.0 * vz - uz * total) + pz
        rest = sign * (1.0 - flow_omega)
        new = [rest * g[0] + scalar]
        pairs = [tx_, ty_, tz_, tx_ + ty_, tx_ - ty_, tx_ + tz_, tx_ - tz_, ty_ + tz_, ty_ - tz_]
        for i, v in enumerate(pairs):
            p = 1 + 2 * i
            new.append(rest * g[p] + (scalar + v))
            new.append(rest * g[p + 1] + (scalar - v))
        return new

    solute_step(0, 0)
    send_sol(1)

    def step(k):
        cur = k % 2
        nxt = 1 - cur

        def body(x, packed, *trip):
            packed = list(packed)
            for h in range(H):
                new = flow_tile(cur, x, h)
                for p in range(NF):
                    A[nxt][p, x + 1, pl.ds(Y0 + 8 * h, 8), :] = new[p]
                stage_tile(nxt, x, h, new, packed, trip)
            return tuple(packed)

        packed = over_x(body, blank, U_FLOW)
        stage_flow(nxt, False, nxt, packed)
        send_flow(nxt, False)
        solute_step(k + 1, nxt)

        if k < steps - 2:
            send_sol(cur)
        wait_flow(nxt, False)

    for k in range(steps - 1):
        step(k)

    def last(x, carry, *trip):
        for h in range(H):
            new = flow_tile((steps - 1) % 2, x, h, -1.0)
            part = pl.ds(8 * h, 8)
            here = pl.ds(Y0 + 8 * h, 8)
            keep = (S[0, x + 1, here, :] < 0.5) & (lane <= top)
            for p in range(NF):
                oflow[p, x, part, :] = jnp.where(keep, new[p], 0.0)
            for p in range(NP - NF):
                osol[p, x, part, :] = jnp.where(keep, -B[steps % 2][p, x + 1, here, :], 0.0)
        return carry

    over_x(last, 0, U_FLOW)


def solution(mesh):
    names = ("gx", "gy", "gz")
    sizes = tuple(mesh.shape[a] for a in names)

    def per_device(flow, solute, rho, vel, lev, solid, owner):
        WX, WY, D = solid.shape
        steps = rho.shape[0]
        f32 = jnp.float32
        V = pltpu.VMEM
        DMA = pltpu.SemaphoreType.DMA
        hbm = pl.BlockSpec(memory_space=pltpu.HBM)
        n = len(NBR) + len(FACES)
        faces = [
            V((2, 2, NQ + 1, WY, D), f32),
            V((2, 2, NQ + 1, WX, D), f32),
            V((2, 2, WY, D), f32),
            V((2, 4, 2, 1, D), f32),
            V((2, 4, 1, D), f32),
            V((2, 4, 1, D), f32),
        ]
        sides = [V((2, 2, WY, D), f32), V((2, 2, WX, D), f32), V((2, 2, WY, D), f32)]
        minus_flow, minus_sol = pl.pallas_call(
            functools.partial(kernel, sizes, steps),
            out_shape=(
                pltpu.VMEM(flow.shape, f32),
                pltpu.VMEM(solute.shape, f32),
            ),
            in_specs=[pl.BlockSpec(memory_space=pltpu.SMEM)] + [hbm] * 6,
            out_specs=(pl.BlockSpec(memory_space=pltpu.VMEM),) * 2,
            scratch_shapes=[
                V((NF, WX + 2, WY + 16, D), f32),
                V((NF, WX + 2, WY + 16, D), f32),
                V((NP - NF, WX + 2, WY + 16, D), f32),
                V((NP - NF, WX + 2, WY + 16, D), f32),
                V((3, WX + 2, WY + 16, D), f32),
                V((2, WY + 16, D), f32),
                V((2, WX, WY + 8, D), f32),
                V((8, WX, WY, D), f32),
                V(rho.shape, rho.dtype),
                V(vel.shape, vel.dtype),
                V(lev.shape, lev.dtype),
                V(solid.shape, solid.dtype),
            ]
            + (faces + sides) * 2
            + [DMA((9,)), DMA((2, n)), DMA((2, n))],
            compiler_params=pltpu.CompilerParams(
                collective_id=0, has_side_effects=True, vmem_limit_bytes=60 * 2**20
            ),
        )(owner, flow, solute, rho, vel, lev, solid)
        return -minus_flow, -minus_sol

    field = P(None, "gx", "gy", "gz")
    return jax.shard_map(
        per_device,
        mesh=mesh,
        in_specs=(field, field, field, P(None, None, "gx", "gy", "gz"), field, P("gx", "gy", "gz"), P()),
        out_specs=(field, field),
        check_vma=False,
    )
```

```python
import functools

import jax
import jax.numpy as jnp
from jax import lax
from jax.experimental import pallas as pl
from jax.experimental.pallas import tpu as pltpu
from jax.sharding import PartitionSpec as P

MESH = pl.DeviceIdType.MESH
BZC = 16

FLOW_DIRS = [
    (0, 0, 0),
    (1, 0, 0),
    (-1, 0, 0),
    (0, 1, 0),
    (0, -1, 0),
    (0, 0, 1),
    (0, 0, -1),
    (1, 1, 0),
    (-1, -1, 0),
    (1, -1, 0),
    (-1, 1, 0),
    (1, 0, 1),
    (-1, 0, -1),
    (1, 0, -1),
    (-1, 0, 1),
    (0, 1, 1),
    (0, -1, -1),
    (0, 1, -1),
    (0, -1, 1),
]
NF = 19
NP = NF + 7
OPP = [FLOW_DIRS.index((-c[0], -c[1], -c[2])) for c in FLOW_DIRS]
flow_omega = 1.25
solute_omega = 1.6
langmuir_rate = 0.05

FACE = [[[p for p in range(NF) if FLOW_DIRS[p][a] == s] for s in (1, -1)] for a in range(3)]
NQ = 5
SPAN = 18
FACES = FLOW_DIRS[1:7]
NBR = [c for c in FLOW_DIRS[1:] if c[2] and c[0]]
NBR += [c for c in FLOW_DIRS[1:] if c[2] and c[1]]
NBR += [c for c in FLOW_DIRS[1:] if c[2] and not c[0] and not c[1]]
NBR += [c for c in FLOW_DIRS[1:] if not c[2] and not (c[0] and c[1])]
NBR += [c for c in FLOW_DIRS[1:] if c[0] and c[1]]
XY = [c for c in NBR if c[0] and c[1]]
XZ = [c for c in NBR if c[0] and c[2]]
YZ = [c for c in NBR if c[1] and c[2]]
FLAT = [c for c in NBR if not c[2]]
INNER = [c for c in NBR if not c[0]]
UPDOWN = [c for c in NBR if c[2]]
U_SOL = 4
OUTER = (5, 4, 3, 2)
Y0 = 8


def side(step):
    return 0 if step > 0 else 1


def axis(c):
    return [i for i in range(3) if c[i]][0]


def neg(c):
    return (-c[0], -c[1], -c[2])


def kernel(
    sizes,
    steps,
    owner_ref,
    flow_hbm,
    sol_hbm,
    rho_hbm,
    vel_hbm,
    lev_hbm,
    solid_hbm,
    oflow,
    osol,
    A0,
    A1,
    B0,
    B1,
    S,
    Zf,
    ZR,
    PU,
    rho,
    vel,
    lev,
    solid,
    sx,
    sy,
    sz,
    sxy,
    sxz,
    syz,
    tx,
    ty,
    tz,
    rx,
    ry,
    rz,
    rxy,
    rxz,
    ryz,
    ux,
    uy,
    uz,
    in_sem,
    send_sem,
    recv_sem,
):
    WX, WY, D = solid.shape
    H = WY // 8
    A, B = (A0, A1), (B0, B1)
    names = ("gx", "gy", "gz")
    me = tuple(lax.axis_index(a) for a in names)

    inside = (pl.ds(1, WX), pl.ds(Y0, WY), slice(None))
    copies = [pltpu.make_async_copy(solid_hbm, solid, in_sem.at[0])]
    cuts = (0, 5, 10, 15, NF)
    for i, (lo, hi) in enumerate(zip(cuts, cuts[1:])):
        part = pl.ds(lo, hi - lo)
        copies.append(
            pltpu.make_async_copy(flow_hbm.at[part], A0.at[(part,) + inside], in_sem.at[1 + i])
        )
    copies.append(pltpu.make_async_copy(sol_hbm, B0.at[(slice(None),) + inside], in_sem.at[5]))
    copies.append(pltpu.make_async_copy(lev_hbm, lev, in_sem.at[6]))
    copies.append(pltpu.make_async_copy(vel_hbm, vel, in_sem.at[7]))
    copies.append(pltpu.make_async_copy(rho_hbm, rho, in_sem.at[8]))
    for c in copies:
        c.start()

    def exists(c):
        ok = None
        for a in range(3):
            if c[a] > 0:
                t = me[a] < sizes[a] - 1
            elif c[a] < 0:
                t = me[a] > 0
            else:
                continue
            ok = t if ok is None else jnp.logical_and(ok, t)
        return ok

    def device(c):
        return tuple(me[a] + c[a] for a in range(3))

    barrier = pltpu.get_barrier_semaphore()
    for c in NBR:

        @pl.when(exists(c))
        def _(c=c):
            pl.semaphore_signal(barrier, inc=1, device_id=device(c), device_id_type=MESH)

    count = jnp.int32(0)
    for i in range(owner_ref.shape[0]):
        count = count + (owner_ref[i] == me[2]).astype(jnp.int32)
    top = count * BZC - 1

    lane = lax.broadcasted_iota(jnp.int32, (8, D), 1)
    row = lax.broadcasted_iota(jnp.int32, (8, D), 0)
    edge = (lane == top, lane == 0)
    last_column = SPAN - 2
    slot_lane = (lane, lax.rem(lane - top + 2 * D, D))

    n = [
        (me[a] > 0).astype(jnp.int32) + (me[a] < sizes[a] - 1).astype(jnp.int32) for a in range(3)
    ]
    pl.semaphore_wait(
        barrier, n[0] + n[1] + n[2] + n[0] * n[1] + n[0] * n[2] + n[1] * n[2]
    )

    def flow_refs(c, slot, first, phase=0, span=None):
        nq = NQ + 1 if first else NQ
        if c in XY:
            part = (slot, XY.index(c), pl.ds(0, nq - NQ + 1))
            return sxy.at[part], rxy.at[part]
        if c in XZ:
            part = (slot, XZ.index(c))
            return sxz.at[part], rxz.at[part]
        if c in YZ:
            part = (slot, phase, YZ.index(c))
            return syz.at[part], ryz.at[part]
        a = axis(c)
        if a == 2:
            part = (slot, phase, side(c[a]))
            return sz.at[part], rz.at[part]
        part = (slot, side(c[a]), pl.ds(0, nq))
        if a == 0:
            return sx.at[part], rx.at[part]
        part = part + (pl.ds(2 * span[0], 2 * (span[1] - span[0])),)
        return sy.at[part], ry.at[part]

    def flow_message(c, slot, first, phase, span):
        src, dst = flow_refs(c, slot, first, phase, span)
        i = INNER.index(c) + len(NBR) if phase else NBR.index(c)
        return pltpu.make_async_remote_copy(
            src_ref=src,
            dst_ref=dst,
            send_sem=send_sem.at[slot, i],
            recv_sem=recv_sem.at[slot, i],
            device_id=device(neg(c)),
            device_id_type=MESH,
        )

    def sol_message(c, slot):
        a = axis(c)
        part = (slot, side(c[a]))
        i = len(NBR) + len(INNER) + FACES.index(c)
        return pltpu.make_async_remote_copy(
            src_ref=(tx, ty, tz)[a].at[part],
            dst_ref=(ux, uy, uz)[a].at[part],
            send_sem=send_sem.at[slot, i],
            recv_sem=recv_sem.at[slot, i],
            device_id=device(neg(c)),
            device_id_type=MESH,
        )

    def each(table, there, act):
        for c in table:

            @pl.when(exists(there(c)))
            def _(c=c):
                act(c)

    same = lambda c: c

    def send_flow(slot, first, phase, span):
        table = INNER if phase else NBR
        each(table, neg, lambda c: flow_message(c, slot, first, phase, span).start())

    def wait_flow(slot, first, phase, span, xs):
        table = INNER if phase else NBR
        each(table, neg, lambda c: flow_message(c, slot, first, phase, span).wait_send())
        flat = [c for c in table if not c[2]]
        each(flat, same, lambda c: flow_message(c, slot, first, phase, span).wait_recv())
        merge_flat(slot, first, slot, phase, span)
        far = [c for c in table if c[2]]
        each(far, same, lambda c: flow_message(c, slot, first, phase, span).wait_recv())
        merge_z(slot, first, phase, xs)

    def send_sol(slot):
        each(FACES, neg, lambda c: sol_message(c, slot).start())

    def wait_sol(slot):
        each(FACES, neg, lambda c: sol_message(c, slot).wait_send())
        each(FACES, same, lambda c: sol_message(c, slot).wait_recv())

    def clear_missing():
        for c in NBR:

            @pl.when(jnp.logical_not(exists(c)))
            def _(c=c):
                for k in range(2):
                    refs = [flow_refs(c, k, True, f, (0, WX // 2))[1] for f in (0, 1)]
                    if c in FACES:
                        refs.append((ux, uy, uz)[axis(c)].at[k, side(c[axis(c)])])
                    for ref in refs:
                        ref[...] = jnp.zeros(ref.shape, ref.dtype)

    def over_x(body, init, unroll):
        def trip(i, carry):
            for j in range(unroll):
                carry = body(unroll * i + j, carry, j, unroll)
            return carry

        return lax.fori_loop(0, WX // unroll, trip, init)

    def edge_row(value, s):
        return value[0:1] if s == 0 else value[7:8]

    def pack(acc, s, values, j, unroll):
        if j == 0:
            acc = pltpu.roll(acc, D - unroll, 1)
        return put_lanes(acc, s, values, last_column - (unroll - 1 - j))

    def put_lanes(acc, s, values, at):
        for q, value in enumerate(values):
            moved = pltpu.roll(value, q * SPAN + at, 1)
            acc = jnp.where(slot_lane[s] == q * SPAN + at, moved, acc)
        return acc

    def settle(face, s):
        return face if s == 0 else pltpu.roll(face, D - top, 1)

    def stage_flow(slot, first, cur, packed, phase):
        for s in (0, 1):
            low, high = packed[: 2 * H], packed[2 * H :]
            face = [settle(low[s * H + h] + high[s * H + h], s) for h in range(H)]
            for h in range(H):
                sz[slot, phase, s, pl.ds(8 * h, 8), :] = face[h]
            for d, c in enumerate(YZ):
                if side(c[2]) == s:
                    syz[slot, phase, d] = face[0][0:1] if c[1] > 0 else face[H - 1][7:8]
            if phase:
                continue
            for d, c in enumerate(XZ):
                if side(c[2]) == s:
                    column = 1 if c[0] > 0 else WX
                    q = FACE[2][s].index(FLOW_DIRS.index(c))
                    line = jnp.zeros((8, D), jnp.float32)
                    for at, qz in enumerate((q, NQ) if first else (q,)):
                        i = qz * SPAN + column
                        for h in range(H):
                            value = jnp.broadcast_to(face[h][:, i : i + 1], (8, D))
                            line = jnp.where(lane == row + (WY * at + 8 * h), value, line)
                    sxz[slot, d] = jnp.sum(line, axis=0, keepdims=True)
        if phase:
            return
        for s in (0, 1):
            x = 1 if s == 0 else WX
            for q, p in enumerate(FACE[0][s]):
                sx[slot, s, q] = A[cur][p, x, pl.ds(Y0, WY), :]
            if first:
                sx[slot, s, NQ] = S[0, x, pl.ds(Y0, WY), :]
        for d, c in enumerate(XY):
            q = FACE[1][side(c[1])].index(FLOW_DIRS.index(c))
            r = 0 if c[0] > 0 else 1
            sxy[slot, d, 0] = sy[slot, side(c[1]), q, r]
            if first:
                sxy[slot, d, 1] = sy[slot, side(c[1]), NQ, r]

    def column_of(line, start):
        line = jnp.broadcast_to(line, (8, D))
        return jnp.sum(jnp.where(lane == row + start, line, 0.0), axis=1, keepdims=True)

    def merge_flat(slot, first, cur, phase, span):
        flag = [(NQ, None)] if first else []

        def put(p, x, rows, value):
            if p is None:
                S[0, x, rows, :] = value
            else:
                A[cur][p, x, rows, :] = value

        for s in (0, 1):
            if not phase:
                x = WX + 1 if s == 0 else 0
                for q, p in list(enumerate(FACE[0][s])) + flag:
                    put(p, x, pl.ds(Y0, WY), rx[slot, s, q])
            y = Y0 + WY if s == 0 else Y0 - 1
            for q, p in list(enumerate(FACE[1][s])) + flag:
                for r in range(2 * span[0], 2 * span[1]):
                    x = WX - 1 - r // 2 if r % 2 else r // 2
                    put(p, 1 + x, pl.ds(y, 1), ry[slot, s, q, r])
        if phase:
            return
        for d, c in enumerate(XY):
            x = WX + 1 if c[0] > 0 else 0
            y = Y0 + WY if c[1] > 0 else Y0 - 1
            put(FLOW_DIRS.index(c), x, pl.ds(y, 1), rxy[slot, d, 0])
            if first:
                put(None, x, pl.ds(y, 1), rxy[slot, d, 1])

    def merge_z(slot, first, phase, xs):
        for s in (0, 1):
            cz = 1 - 2 * s
            turn = (lambda v: pltpu.roll(v, top, 1)) if s == 0 else (lambda v: v)
            for h in range(H):
                part = pl.ds(Y0 + 8 * h, 8)
                face = rz[slot, phase, s, pl.ds(8 * h, 8), :]
                if not phase:
                    for cx in (1, -1):
                        c = (cx, 0, cz)
                        q = FACE[2][s].index(FLOW_DIRS.index(c))
                        for at, qz in enumerate((q, NQ) if first else (q,)):
                            value = column_of(rxz[slot, XZ.index(c)], WY * at + 8 * h)
                            i = qz * SPAN + (WX + 1 if cx > 0 else 0)
                            face = jnp.where(lane == i, value, face)
                    Zf[s, part, :] = turn(face)
                else:
                    Zf[s, part, :] = Zf[s, part, :] + turn(face)
            for y, cy in ((Y0 + WY, 1), (Y0 - 1, -1)):
                line = jnp.broadcast_to(ryz[slot, phase, YZ.index((0, cy, cz))], (8, D))
                line = turn(line)[0:1]
                Zf[s, pl.ds(y, 1), :] = Zf[s, pl.ds(y, 1), :] + line if phase else line
            for t in range(3):
                face = Zf[s, pl.ds(Y0 - 1 + 8 * t, 8), :]
                for x in xs:
                    ZR[s, x, pl.ds(8 * t, 8), :] = pltpu.roll(face, D - x, 1) if x else face

    for c in copies[:6]:
        c.wait()

    zero = jnp.zeros((8, D), jnp.float32)
    for s in (0, 1):
        for part in range(0, WY + 16, 8):
            Zf[s, pl.ds(part, 8), :] = zero
    for part in (0, Y0 + WY):
        for x in range(WX + 2):
            S[0, x, pl.ds(part, 8), :] = zero

    blank = (zero,) * (2 * H)

    def stage_tile(slot, i, b, h, values, packed, end, flag=None):
        extra = [] if flag is None else [flag]
        for s in (0, 1):
            if h == (0 if s == 0 else H - 1):
                for q, value in enumerate([values[p] for p in FACE[1][s]] + extra):
                    sy[slot, s, q, 2 * i + b] = edge_row(value, s)
            at = b * 2 * H + s * H + h
            acc = pltpu.roll(packed[at], 1 if b else D - 1, 1)
            values_z = [values[p] for p in FACE[2][s]] + extra
            packed[at] = put_lanes(acc, s, values_z, WX + 1 - end if b else end)

    def stage_sol_tile(slot, x, h, values, packed, trip):
        for s in (0, 1):
            if h == (0 if s == 0 else H - 1):
                ty[slot, s, pl.ds(x, 1), :] = edge_row(values[3 + s], s)
            i = s * H + h
            packed[i] = pack(packed[i], s, [values[5 + s]], *trip)

    def stage_sol(slot, cur, packed):
        for s in (0, 1):
            for h in range(H):
                tz[slot, s, pl.ds(8 * h, 8), :] = settle(packed[s * H + h], s)
            tx[slot, s] = B[cur][1 + s, 1 if s == 0 else WX, pl.ds(Y0, WY), :]

    class Tiles:
        def __init__(self, ref, x, part):
            self.ref, self.x, self.part = ref, x, part

        def __getitem__(self, p):
            return self.ref[p, self.x + 1, self.part, :]

    def first_stage(i, packed):
        packed = list(packed)
        for b in (0, 1):
            x = WX - 1 - i if b else i
            flags = solid[x].astype(jnp.float32)
            S[0, x + 1, pl.ds(Y0, WY), :] = flags
            for h in range(H):
                part = pl.ds(Y0 + 8 * h, 8)
                flag = flags[8 * h : 8 * h + 8]
                stage_tile(0, i, b, h, Tiles(A0, x, part), packed, WX // 2, flag)
        return tuple(packed)

    def first_sol(x, other, *trip):
        other = list(other)
        for h in range(H):
            stage_sol_tile(0, x, h, Tiles(B0, x, pl.ds(Y0 + 8 * h, 8)), other, trip)
        return tuple(other)

    whole = (0, WX // 2)
    packed = lax.fori_loop(0, WX // 2, first_stage, blank * 2)
    stage_flow(0, True, 0, packed, 0)
    send_flow(0, True, 0, whole)
    other = over_x(first_sol, blank, 4)
    stage_sol(0, 0, other)
    send_sol(0)
    clear_missing()
    for c in copies[6:]:
        c.wait()
    wait_flow(0, True, 0, whole, range(WX))
    for x in range(WX + 2):
        for t in range(0, WY + 16, 8):
            part = pl.ds(t, 8)
            flag = S[0, x, part, :]
            for s in (0, 1):
                halo = pltpu.roll(Zf[s, part, :], D - (NQ * SPAN + x), 1)
                moved = pltpu.roll(flag, D - 1 if s == 0 else 1, 1)
                S[1 + s, x, part, :] = jnp.where(edge[s], halo, moved)

    def solute_step(j, slot):
        t = steps - 1 - j
        cur = slot
        nxt = 1 - slot
        wait_sol(slot)
        for s in (0, 1):
            B[cur][1 + s, WX + 1 if s == 0 else 0, pl.ds(Y0, WY), :] = ux[slot, s]
            y = Y0 + WY if s == 0 else Y0 - 1
            for half in range(WX // 8):
                value = uy[slot, s, pl.ds(8 * half, 8), :]
                for i in range(8):
                    B[cur][3 + s, 1 + 8 * half + i, pl.ds(y, 1), :] = value[i : i + 1]
        halo = []
        for s in (0, 1):
            for h in range(H):
                face = uz[slot, s, pl.ds(8 * h, 8), :]
                halo.append(pltpu.roll(face, top - 1 if s == 0 else D - 1, 1))

        def body(x, carry, *trip):
            halo, packed = list(carry[0]), list(carry[1])
            level_ = lev[t, x].astype(jnp.float32)
            density_ = rho[t, x].astype(jnp.float32)
            u_ = [vel[t, i, x].astype(jnp.float32) for i in range(3)]
            for h in range(H):
                cut = slice(8 * h, 8 * h + 8)
                level, density, u = level_[cut], density_[cut], [v[cut] for v in u_]
                start = Y0 + 8 * h
                here = pl.ds(start, 8)
                hs = [B[cur][0, x + 1, here, :]]
                for p in range(1, 7):
                    c = FLOW_DIRS[p]
                    rows = pl.ds(start + c[1], 8)
                    value = B[cur][p, x + 1 + c[0], rows, :]
                    if c[2]:
                        s = side(c[2])
                        value = pltpu.roll(value, D - 1 if s == 0 else 1, 1)
                        value = jnp.where(edge[s], halo[s * H + h], value)
                        flag = S[1 + s, x + 1, here, :]
                    else:
                        flag = S[0, x + 1 + c[0], rows, :]
                    hs.append(jnp.where(flag > 0.5, B[cur][OPP[p], x + 1, here, :], value))
                mx, my, mz = hs[1] - hs[2], hs[3] - hs[4], hs[5] - hs[6]
                m0 = 0.25 * hs[0] + 0.125 * ((hs[1] + hs[2]) + (hs[3] + hs[4]) + (hs[5] + hs[6]))
                along = mx * u[0] + my * u[1] + mz * u[2]
                one = 1.0 + level
                common = (solute_omega - langmuir_rate / (one * one)) * m0 + (
                    solute_omega * 0.5
                ) * along
                new = [(1.0 - solute_omega) * v + common for v in hs]
                for p in range(7):
                    B[nxt][p, x + 1, here, :] = new[p]
                stage_sol_tile(nxt, x, h, new, packed, trip)
                factor = (0.5 * solute_omega) * level * (1.0 / density)
                speed = u[0] * u[0] + u[1] * u[1] + u[2] * u[2]
                saved = [factor * mx, factor * my, factor * mz, factor * along]
                for i, v in enumerate(saved + u + [1.0 + 1.5 * speed]):
                    PU[i, x, pl.ds(8 * h, 8), :] = v
            return tuple(pltpu.roll(v, D - 1, 1) for v in halo), tuple(packed)

        _, packed = over_x(body, (tuple(halo), blank), U_SOL)
        stage_sol(nxt, nxt, packed)

    def flow_tile(cur, x, h, sign=1.0):
        start = Y0 + 8 * h

        def read(p):
            c = FLOW_DIRS[p]
            rows = pl.ds(start + c[1], 8)
            here = A[cur][p, x + 1 + c[0], rows, :]
            if c == (0, 0, 0):
                return here
            if c[2]:
                s = side(c[2])
                here = pltpu.roll(here, D - 1 if s == 0 else 1, 1)
                lift = FACE[2][s].index(p) * SPAN + 1 + c[0]
                halo = ZR[s, x, pl.ds(8 * h + 1 + c[1], 8), :]
                halo = pltpu.roll(halo, D - lift, 1) if lift else halo
                here = jnp.where(edge[s], halo, here)
                flag = S[1 + s, x + 1 + c[0], rows, :]
            else:
                flag = S[0, x + 1 + c[0], rows, :]
            back = A[cur][OPP[p], x + 1, pl.ds(start, 8), :]
            return jnp.where(flag > 0.5, back, here)

        part = pl.ds(8 * h, 8)
        px, py, pz, along, ux, uy, uz, stretch = [PU[i, x, part, :] for i in range(8)]
        g = [read(p) for p in range(NF)]
        a = [g[p] + g[p + 1] for p in range(1, NF, 2)]
        d = [g[p] - g[p + 1] for p in range(1, NF, 2)]
        ax, ay, az = 2.0 * a[0], 2.0 * a[1], 2.0 * a[2]
        sxy_, sxz_, syz_ = a[3] + a[4], a[5] + a[6], a[7] + a[8]
        qxy, qxz, qyz = a[3] - a[4], a[5] - a[6], a[7] - a[8]
        qxx, qyy, qzz = ax + sxy_ + sxz_, ay + sxy_ + syz_, az + sxz_ + syz_
        total = 12.0 * g[0] + (qxx + ay + az) + syz_
        jx = 2.0 * d[0] + (d[3] + d[4]) + (d[5] + d[6])
        jy = 2.0 * d[1] + (d[3] - d[4]) + (d[7] + d[8])
        jz = 2.0 * d[2] + (d[5] - d[6]) + (d[7] - d[8])
        vx = qxx * ux + qxy * uy + qxz * uz
        vy = qxy * ux + qyy * uy + qyz * uz
        vz = qxz * ux + qyz * uy + qzz * uz
        quad = vx * ux + vy * uy + vz * uz
        w = sign * flow_omega / 36.0
        if sign < 0:
            px, py, pz, along = -px, -py, -pz, -along
        scalar = w * (total * stretch - 4.5 * quad) - along
        tx_ = (3.0 * w) * (jx + 3.0 * vx - ux * total) + px
        ty_ = (3.0 * w) * (jy + 3.0 * vy - uy * total) + py
        tz_ = (3.0 * w) * (jz + 3.0 * vz - uz * total) + pz
        rest = sign * (1.0 - flow_omega)
        new = [rest * g[0] + scalar]
        pairs = [tx_, ty_, tz_, tx_ + ty_, tx_ - ty_, tx_ + tz_, tx_ - tz_, ty_ + tz_, ty_ - tz_]
        for i, v in enumerate(pairs):
            p = 1 + 2 * i
            new.append(rest * g[p] + (scalar + v))
            new.append(rest * g[p + 1] + (scalar - v))
        return new

    solute_step(0, 0)
    send_sol(1)

    def outer_slabs(k):
        return [x for x in range(WX) if x < OUTER[k] or x >= WX - OUTER[k]]

    def flow_phase(k, phase):
        cur = k % 2
        nxt = 1 - cur
        span = (OUTER[k], WX // 2) if phase else (0, OUTER[k])

        def body(i, packed):
            packed = list(packed)
            for b in (0, 1):
                x = WX - 1 - i if b else i
                for h in range(H):
                    if k < steps - 1:
                        new = flow_tile(cur, x, h)
                        for p in range(NF):
                            A[nxt][p, x + 1, pl.ds(Y0 + 8 * h, 8), :] = new[p]
                        stage_tile(nxt, i, b, h, new, packed, span[1])
                    else:
                        new = flow_tile(cur, x, h, -1.0)
                        part = pl.ds(8 * h, 8)
                        here = pl.ds(Y0 + 8 * h, 8)
                        keep = (S[0, x + 1, here, :] < 0.5) & (lane <= top)
                        for p in range(NF):
                            oflow[p, x, part, :] = jnp.where(keep, new[p], 0.0)
                        for p in range(NP - NF):
                            osol[p, x, part, :] = jnp.where(
                                keep, -B[steps % 2][p, x + 1, here, :], 0.0
                            )
            return tuple(packed)

        if k == steps - 1:
            lax.fori_loop(span[0], span[1], lambda i, c: (body(i, ()), c)[1], 0)
            return
        packed = lax.fori_loop(span[0], span[1], body, blank * 2)
        stage_flow(nxt, False, nxt, packed, phase)
        send_flow(nxt, False, phase, span)

    for k in range(steps):
        slot = k % 2
        outer = outer_slabs(k)
        if k:
            wait_flow(slot, False, 0, (0, OUTER[k - 1]), outer)
        flow_phase(k, 0)
        if k:
            inner = [x for x in range(WX) if x not in outer]
            wait_flow(slot, False, 1, (OUTER[k - 1], WX // 2), inner)
        flow_phase(k, 1)
        if k < steps - 1:
            solute_step(k + 1, 1 - slot)
            if k < steps - 2:
                send_sol(slot)


def solution(mesh):
    names = ("gx", "gy", "gz")
    sizes = tuple(mesh.shape[a] for a in names)

    def per_device(flow, solute, rho, vel, lev, solid, owner):
        WX, WY, D = solid.shape
        steps = rho.shape[0]
        f32 = jnp.float32
        V = pltpu.VMEM
        DMA = pltpu.SemaphoreType.DMA
        hbm = pl.BlockSpec(memory_space=pltpu.HBM)
        n = len(NBR) + len(INNER) + len(FACES)
        faces = [
            V((2, 2, NQ + 1, WY, D), f32),
            V((2, 2, NQ + 1, WX, 1, D), f32),
            V((2, 2, 2, WY, D), f32),
            V((2, 4, 2, 1, D), f32),
            V((2, 4, 1, D), f32),
            V((2, 2, 4, 1, D), f32),
        ]
        sides = [V((2, 2, WY, D), f32), V((2, 2, WX, D), f32), V((2, 2, WY, D), f32)]
        minus_flow, minus_sol = pl.pallas_call(
            functools.partial(kernel, sizes, steps),
            out_shape=(
                pltpu.VMEM(flow.shape, f32),
                pltpu.VMEM(solute.shape, f32),
            ),
            in_specs=[pl.BlockSpec(memory_space=pltpu.SMEM)] + [hbm] * 6,
            out_specs=(pl.BlockSpec(memory_space=pltpu.VMEM),) * 2,
            scratch_shapes=[
                V((NF, WX + 2, WY + 16, D), f32),
                V((NF, WX + 2, WY + 16, D), f32),
                V((NP - NF, WX + 2, WY + 16, D), f32),
                V((NP - NF, WX + 2, WY + 16, D), f32),
                V((3, WX + 2, WY + 16, D), f32),
                V((2, WY + 16, D), f32),
                V((2, WX, WY + 8, D), f32),
                V((8, WX, WY, D), f32),
                V(rho.shape, rho.dtype),
                V(vel.shape, vel.dtype),
                V(lev.shape, lev.dtype),
                V(solid.shape, solid.dtype),
            ]
            + (faces + sides) * 2
            + [DMA((9,)), DMA((2, n)), DMA((2, n))],
            compiler_params=pltpu.CompilerParams(
                collective_id=0, has_side_effects=True, vmem_limit_bytes=60 * 2**20
            ),
        )(owner, flow, solute, rho, vel, lev, solid)
        return -minus_flow, -minus_sol

    field = P(None, "gx", "gy", "gz")
    return jax.shard_map(
        per_device,
        mesh=mesh,
        in_specs=(field, field, field, P(None, None, "gx", "gy", "gz"), field, P("gx", "gy", "gz"), P()),
        out_specs=(field, field),
        check_vma=False,
    )
```

```python
import functools

import jax
import jax.numpy as jnp
from jax import lax
from jax.experimental import pallas as pl
from jax.experimental.pallas import tpu as pltpu
from jax.sharding import PartitionSpec as P

MESH = pl.DeviceIdType.MESH
BZC = 16

FLOW_DIRS = [
    (0, 0, 0),
    (1, 0, 0),
    (-1, 0, 0),
    (0, 1, 0),
    (0, -1, 0),
    (0, 0, 1),
    (0, 0, -1),
    (1, 1, 0),
    (-1, -1, 0),
    (1, -1, 0),
    (-1, 1, 0),
    (1, 0, 1),
    (-1, 0, -1),
    (1, 0, -1),
    (-1, 0, 1),
    (0, 1, 1),
    (0, -1, -1),
    (0, 1, -1),
    (0, -1, 1),
]
NF = 19
NP = NF + 7
OPP = [FLOW_DIRS.index((-c[0], -c[1], -c[2])) for c in FLOW_DIRS]
flow_omega = 1.25
solute_omega = 1.6
langmuir_rate = 0.05

FACE = [[[p for p in range(NF) if FLOW_DIRS[p][a] == s] for s in (1, -1)] for a in range(3)]
NQ = 5
SPAN = 18
FACES = FLOW_DIRS[1:7]
NBR = [c for c in FLOW_DIRS[1:] if c[2] and c[0]]
NBR += [c for c in FLOW_DIRS[1:] if c[2] and c[1]]
NBR += [c for c in FLOW_DIRS[1:] if c[2] and not c[0] and not c[1]]
NBR += [c for c in FLOW_DIRS[1:] if not c[2] and not (c[0] and c[1])]
NBR += [c for c in FLOW_DIRS[1:] if c[0] and c[1]]
XY = [c for c in NBR if c[0] and c[1]]
XZ = [c for c in NBR if c[0] and c[2]]
YZ = [c for c in NBR if c[1] and c[2]]
FLAT = [c for c in NBR if not c[2]]
INNER = [c for c in NBR if not c[0]]
UPDOWN = [c for c in NBR if c[2]]
U_SOL = 4
OUTER = (5, 4, 3, 2)
Y0 = 8


def side(step):
    return 0 if step > 0 else 1


def axis(c):
    return [i for i in range(3) if c[i]][0]


def neg(c):
    return (-c[0], -c[1], -c[2])


def kernel(
    sizes,
    steps,
    owner_ref,
    flow_hbm,
    sol_hbm,
    rho_hbm,
    vel_hbm,
    lev_hbm,
    solid_hbm,
    oflow,
    osol,
    A0,
    A1,
    B0,
    B1,
    S,
    Zf,
    ZR,
    PU,
    rho,
    vel,
    lev,
    solid,
    sx,
    sy,
    sz,
    sxy,
    sxz,
    syz,
    tx,
    ty,
    tz,
    rx,
    ry,
    rz,
    rxy,
    rxz,
    ryz,
    ux,
    uy,
    uz,
    in_sem,
    send_sem,
    recv_sem,
):
    WX, WY, D = solid.shape
    H = WY // 8
    A, B = (A0, A1), (B0, B1)
    names = ("gx", "gy", "gz")
    me = tuple(lax.axis_index(a) for a in names)

    inside = (pl.ds(1, WX), pl.ds(Y0, WY), slice(None))
    copies = [pltpu.make_async_copy(solid_hbm, solid, in_sem.at[0])]
    cuts = (0, 5, 10, 15, NF)
    for i, (lo, hi) in enumerate(zip(cuts, cuts[1:])):
        part = pl.ds(lo, hi - lo)
        copies.append(
            pltpu.make_async_copy(flow_hbm.at[part], A0.at[(part,) + inside], in_sem.at[1 + i])
        )
    copies.append(pltpu.make_async_copy(sol_hbm, B0.at[(slice(None),) + inside], in_sem.at[5]))
    copies.append(pltpu.make_async_copy(lev_hbm, lev, in_sem.at[6]))
    copies.append(pltpu.make_async_copy(vel_hbm, vel, in_sem.at[7]))
    copies.append(pltpu.make_async_copy(rho_hbm, rho, in_sem.at[8]))
    for c in copies:
        c.start()

    def exists(c):
        ok = None
        for a in range(3):
            if c[a] > 0:
                t = me[a] < sizes[a] - 1
            elif c[a] < 0:
                t = me[a] > 0
            else:
                continue
            ok = t if ok is None else jnp.logical_and(ok, t)
        return ok

    def device(c):
        return tuple(me[a] + c[a] for a in range(3))

    barrier = pltpu.get_barrier_semaphore()
    for c in NBR:

        @pl.when(exists(c))
        def _(c=c):
            pl.semaphore_signal(barrier, inc=1, device_id=device(c), device_id_type=MESH)

    count = jnp.int32(0)
    for i in range(owner_ref.shape[0]):
        count = count + (owner_ref[i] == me[2]).astype(jnp.int32)
    top = count * BZC - 1

    lane = lax.broadcasted_iota(jnp.int32, (8, D), 1)
    row = lax.broadcasted_iota(jnp.int32, (8, D), 0)
    edge = (lane == top, lane == 0)
    last_column = SPAN - 2
    slot_lane = (lane, lax.rem(lane - top + 2 * D, D))

    def flow_refs(c, slot, first, phase=0, span=None):
        nq = NQ + 1 if first else NQ
        if c in XY:
            part = (slot, XY.index(c), pl.ds(0, nq - NQ + 1))
            return sxy.at[part], rxy.at[part]
        if c in XZ:
            part = (slot, XZ.index(c))
            return sxz.at[part], rxz.at[part]
        if c in YZ:
            part = (slot, phase, YZ.index(c))
            return syz.at[part], ryz.at[part]
        a = axis(c)
        if a == 2:
            part = (slot, phase, side(c[a]))
            return sz.at[part], rz.at[part]
        part = (slot, side(c[a]), pl.ds(0, nq))
        if a == 0:
            return sx.at[part], rx.at[part]
        part = part + (pl.ds(2 * span[0], 2 * (span[1] - span[0])),)
        return sy.at[part], ry.at[part]

    def flow_message(c, slot, first, phase, span):
        src, dst = flow_refs(c, slot, first, phase, span)
        i = INNER.index(c) + len(NBR) if phase else NBR.index(c)
        return pltpu.make_async_remote_copy(
            src_ref=src,
            dst_ref=dst,
            send_sem=send_sem.at[i],
            recv_sem=recv_sem.at[slot, i],
            device_id=device(neg(c)),
            device_id_type=MESH,
        )

    def sol_message(c, slot):
        a = axis(c)
        part = (slot, side(c[a]))
        i = len(NBR) + len(INNER) + FACES.index(c)
        return pltpu.make_async_remote_copy(
            src_ref=(tx, ty, tz)[a].at[part],
            dst_ref=(ux, uy, uz)[a].at[part],
            send_sem=send_sem.at[i],
            recv_sem=recv_sem.at[slot, i],
            device_id=device(neg(c)),
            device_id_type=MESH,
        )

    def each(table, there, act):
        for c in table:

            @pl.when(exists(there(c)))
            def _(c=c):
                act(c)

    same = lambda c: c

    def send_flow(slot, first, phase, span):
        table = INNER if phase else NBR
        each(table, neg, lambda c: flow_message(c, slot, first, phase, span).start())

    def wait_flow(slot, first, phase, span, xs):
        table = INNER if phase else NBR
        each(table, neg, lambda c: flow_message(c, slot, first, phase, span).wait_send())
        flat = [c for c in table if not c[2]]
        each(flat, same, lambda c: flow_message(c, slot, first, phase, span).wait_recv())
        merge_flat(slot, first, slot, phase, span)
        far = [c for c in table if c[2]]
        each(far, same, lambda c: flow_message(c, slot, first, phase, span).wait_recv())
        merge_z(slot, first, phase, xs)

    def send_sol(slot):
        each(FACES, neg, lambda c: sol_message(c, slot).start())

    def wait_sol(slot):
        each(FACES, neg, lambda c: sol_message(c, slot).wait_send())
        each(FACES, same, lambda c: sol_message(c, slot).wait_recv())

    def clear_missing():
        for c in NBR:

            @pl.when(jnp.logical_not(exists(c)))
            def _(c=c):
                for k in range(2):
                    refs = [flow_refs(c, k, True, f, (0, WX // 2))[1] for f in (0, 1)]
                    if c in FACES:
                        refs.append((ux, uy, uz)[axis(c)].at[k, side(c[axis(c)])])
                    for ref in refs:
                        ref[...] = jnp.zeros(ref.shape, ref.dtype)

    def over_x(body, init, unroll):
        def trip(i, carry):
            for j in range(unroll):
                carry = body(unroll * i + j, carry, j, unroll)
            return carry

        return lax.fori_loop(0, WX // unroll, trip, init)

    def edge_row(value, s):
        return value[0:1] if s == 0 else value[7:8]

    def pack(acc, s, values, j, unroll):
        if j == 0:
            acc = pltpu.roll(acc, D - unroll, 1)
        return put_lanes(acc, s, values, last_column - (unroll - 1 - j))

    def put_lanes(acc, s, values, at):
        for q, value in enumerate(values):
            moved = pltpu.roll(value, q * SPAN + at, 1)
            acc = jnp.where(slot_lane[s] == q * SPAN + at, moved, acc)
        return acc

    def settle(face, s):
        return face if s == 0 else pltpu.roll(face, D - top, 1)

    def stage_flow(slot, first, cur, packed, phase):
        for s in (0, 1):
            low, high = packed[: 2 * H], packed[2 * H :]
            face = [settle(low[s * H + h] + high[s * H + h], s) for h in range(H)]
            for h in range(H):
                sz[slot, phase, s, pl.ds(8 * h, 8), :] = face[h]
            for d, c in enumerate(YZ):
                if side(c[2]) == s:
                    syz[slot, phase, d] = face[0][0:1] if c[1] > 0 else face[H - 1][7:8]
            if phase:
                continue
            for d, c in enumerate(XZ):
                if side(c[2]) == s:
                    column = 1 if c[0] > 0 else WX
                    q = FACE[2][s].index(FLOW_DIRS.index(c))
                    line = jnp.zeros((8, D), jnp.float32)
                    for at, qz in enumerate((q, NQ) if first else (q,)):
                        i = qz * SPAN + column
                        for h in range(H):
                            value = jnp.broadcast_to(face[h][:, i : i + 1], (8, D))
                            line = jnp.where(lane == row + (WY * at + 8 * h), value, line)
                    sxz[slot, d] = jnp.sum(line, axis=0, keepdims=True)
        if phase:
            return
        for s in (0, 1):
            x = 1 if s == 0 else WX
            for q, p in enumerate(FACE[0][s]):
                sx[slot, s, q] = A[cur][p, x, pl.ds(Y0, WY), :]
            if first:
                sx[slot, s, NQ] = S[0, x, pl.ds(Y0, WY), :]
        for d, c in enumerate(XY):
            q = FACE[1][side(c[1])].index(FLOW_DIRS.index(c))
            r = 0 if c[0] > 0 else 1
            sxy[slot, d, 0] = sy[slot, side(c[1]), q, r]
            if first:
                sxy[slot, d, 1] = sy[slot, side(c[1]), NQ, r]

    def column_of(line, start):
        line = jnp.broadcast_to(line, (8, D))
        return jnp.sum(jnp.where(lane == row + start, line, 0.0), axis=1, keepdims=True)

    def merge_flat(slot, first, cur, phase, span):
        flag = [(NQ, None)] if first else []

        def put(p, x, rows, value):
            if p is None:
                S[0, x, rows, :] = value
            else:
                A[cur][p, x, rows, :] = value

        for s in (0, 1):
            if not phase:
                x = WX + 1 if s == 0 else 0
                for q, p in list(enumerate(FACE[0][s])) + flag:
                    put(p, x, pl.ds(Y0, WY), rx[slot, s, q])
            y = Y0 + WY if s == 0 else Y0 - 1
            for q, p in list(enumerate(FACE[1][s])) + flag:
                for r in range(2 * span[0], 2 * span[1]):
                    x = WX - 1 - r // 2 if r % 2 else r // 2
                    put(p, 1 + x, pl.ds(y, 1), ry[slot, s, q, r])
        if phase:
            return
        for d, c in enumerate(XY):
            x = WX + 1 if c[0] > 0 else 0
            y = Y0 + WY if c[1] > 0 else Y0 - 1
            put(FLOW_DIRS.index(c), x, pl.ds(y, 1), rxy[slot, d, 0])
            if first:
                put(None, x, pl.ds(y, 1), rxy[slot, d, 1])

    def merge_z(slot, first, phase, xs):
        for s in (0, 1):
            cz = 1 - 2 * s
            turn = (lambda v: pltpu.roll(v, top, 1)) if s == 0 else (lambda v: v)
            for h in range(H):
                part = pl.ds(Y0 + 8 * h, 8)
                face = rz[slot, phase, s, pl.ds(8 * h, 8), :]
                if not phase:
                    for cx in (1, -1):
                        c = (cx, 0, cz)
                        q = FACE[2][s].index(FLOW_DIRS.index(c))
                        for at, qz in enumerate((q, NQ) if first else (q,)):
                            value = column_of(rxz[slot, XZ.index(c)], WY * at + 8 * h)
                            i = qz * SPAN + (WX + 1 if cx > 0 else 0)
                            face = jnp.where(lane == i, value, face)
                    Zf[s, part, :] = turn(face)
                else:
                    Zf[s, part, :] = Zf[s, part, :] + turn(face)
            for y, cy in ((Y0 + WY, 1), (Y0 - 1, -1)):
                line = jnp.broadcast_to(ryz[slot, phase, YZ.index((0, cy, cz))], (8, D))
                line = turn(line)[0:1]
                Zf[s, pl.ds(y, 1), :] = Zf[s, pl.ds(y, 1), :] + line if phase else line
            for t in range(3):
                face = Zf[s, pl.ds(Y0 - 1 + 8 * t, 8), :]
                for x in xs:
                    ZR[s, x, pl.ds(8 * t, 8), :] = pltpu.roll(face, D - x, 1) if x else face

    for c in copies[:6]:
        c.wait()

    zero = jnp.zeros((8, D), jnp.float32)
    for s in (0, 1):
        for part in range(0, WY + 16, 8):
            Zf[s, pl.ds(part, 8), :] = zero
    for part in (0, Y0 + WY):
        for x in range(WX + 2):
            S[0, x, pl.ds(part, 8), :] = zero

    blank = (zero,) * (2 * H)

    def stage_tile(slot, i, b, h, values, packed, end, flag=None):
        extra = [] if flag is None else [flag]
        for s in (0, 1):
            if h == (0 if s == 0 else H - 1):
                for q, value in enumerate([values[p] for p in FACE[1][s]] + extra):
                    sy[slot, s, q, 2 * i + b] = edge_row(value, s)
            at = b * 2 * H + s * H + h
            acc = pltpu.roll(packed[at], 1 if b else D - 1, 1)
            values_z = [values[p] for p in FACE[2][s]] + extra
            packed[at] = put_lanes(acc, s, values_z, WX + 1 - end if b else end)

    def stage_sol_tile(slot, x, h, values, packed, trip):
        for s in (0, 1):
            if h == (0 if s == 0 else H - 1):
                ty[slot, s, pl.ds(x, 1), :] = edge_row(values[3 + s], s)
            i = s * H + h
            packed[i] = pack(packed[i], s, [values[5 + s]], *trip)

    def stage_sol(slot, cur, packed):
        for s in (0, 1):
            for h in range(H):
                tz[slot, s, pl.ds(8 * h, 8), :] = settle(packed[s * H + h], s)
            tx[slot, s] = B[cur][1 + s, 1 if s == 0 else WX, pl.ds(Y0, WY), :]

    class Tiles:
        def __init__(self, ref, x, part):
            self.ref, self.x, self.part = ref, x, part

        def __getitem__(self, p):
            return self.ref[p, self.x + 1, self.part, :]

    def first_stage(i, packed):
        packed = list(packed)
        for b in (0, 1):
            x = WX - 1 - i if b else i
            flags = solid[x].astype(jnp.float32)
            S[0, x + 1, pl.ds(Y0, WY), :] = flags
            for h in range(H):
                part = pl.ds(Y0 + 8 * h, 8)
                flag = flags[8 * h : 8 * h + 8]
                stage_tile(0, i, b, h, Tiles(A0, x, part), packed, WX // 2, flag)
        return tuple(packed)

    def first_sol(x, other, *trip):
        other = list(other)
        for h in range(H):
            stage_sol_tile(0, x, h, Tiles(B0, x, pl.ds(Y0 + 8 * h, 8)), other, trip)
        return tuple(other)

    whole = (0, WX // 2)
    packed = lax.fori_loop(0, WX // 2, first_stage, blank * 2)
    stage_flow(0, True, 0, packed, 0)
    n = [
        (me[a] > 0).astype(jnp.int32) + (me[a] < sizes[a] - 1).astype(jnp.int32) for a in range(3)
    ]
    pl.semaphore_wait(
        barrier, n[0] + n[1] + n[2] + n[0] * n[1] + n[0] * n[2] + n[1] * n[2]
    )
    send_flow(0, True, 0, whole)
    other = over_x(first_sol, blank, 4)
    stage_sol(0, 0, other)
    send_sol(0)
    clear_missing()
    for c in copies[6:]:
        c.wait()
    own = [(x + 1, Y0 + 8 * h) for x in range(WX) for h in range(H)]
    for x, t in own:
        part = pl.ds(t, 8)
        for s in (0, 1):
            S[1 + s, x, part, :] = pltpu.roll(S[0, x, part, :], D - 1 if s == 0 else 1, 1)
    wait_flow(0, True, 0, whole, range(WX))
    for x in range(WX + 2):
        for t in range(0, WY + 16, 8):
            part = pl.ds(t, 8)
            flag = S[0, x, part, :]
            for s in (0, 1):
                halo = pltpu.roll(Zf[s, part, :], D - (NQ * SPAN + x), 1)
                if (x, t) in own:
                    moved = S[1 + s, x, part, :]
                else:
                    moved = pltpu.roll(flag, D - 1 if s == 0 else 1, 1)
                S[1 + s, x, part, :] = jnp.where(edge[s], halo, moved)

    def solute_step(j, slot):
        t = steps - 1 - j
        cur = slot
        nxt = 1 - slot
        wait_sol(slot)
        for s in (0, 1):
            B[cur][1 + s, WX + 1 if s == 0 else 0, pl.ds(Y0, WY), :] = ux[slot, s]
            y = Y0 + WY if s == 0 else Y0 - 1
            for half in range(WX // 8):
                value = uy[slot, s, pl.ds(8 * half, 8), :]
                for i in range(8):
                    B[cur][3 + s, 1 + 8 * half + i, pl.ds(y, 1), :] = value[i : i + 1]
        halo = []
        for s in (0, 1):
            for h in range(H):
                face = uz[slot, s, pl.ds(8 * h, 8), :]
                halo.append(pltpu.roll(face, top - 1 if s == 0 else D - 1, 1))

        def body(x, carry, *trip):
            halo, packed = list(carry[0]), list(carry[1])
            level_ = lev[t, x].astype(jnp.float32)
            density_ = rho[t, x].astype(jnp.float32)
            u_ = [vel[t, i, x].astype(jnp.float32) for i in range(3)]
            for h in range(H):
                cut = slice(8 * h, 8 * h + 8)
                level, density, u = level_[cut], density_[cut], [v[cut] for v in u_]
                start = Y0 + 8 * h
                here = pl.ds(start, 8)
                hs = [B[cur][0, x + 1, here, :]]
                for p in range(1, 7):
                    c = FLOW_DIRS[p]
                    rows = pl.ds(start + c[1], 8)
                    value = B[cur][p, x + 1 + c[0], rows, :]
                    if c[2]:
                        s = side(c[2])
                        value = pltpu.roll(value, D - 1 if s == 0 else 1, 1)
                        value = jnp.where(edge[s], halo[s * H + h], value)
                        flag = S[1 + s, x + 1, here, :]
                    else:
                        flag = S[0, x + 1 + c[0], rows, :]
                    hs.append(jnp.where(flag > 0.5, B[cur][OPP[p], x + 1, here, :], value))
                mx, my, mz = hs[1] - hs[2], hs[3] - hs[4], hs[5] - hs[6]
                m0 = 0.25 * hs[0] + 0.125 * ((hs[1] + hs[2]) + (hs[3] + hs[4]) + (hs[5] + hs[6]))
                along = mx * u[0] + my * u[1] + mz * u[2]
                one = 1.0 + level
                common = (solute_omega - langmuir_rate / (one * one)) * m0 + (
                    solute_omega * 0.5
                ) * along
                new = [(1.0 - solute_omega) * v + common for v in hs]
                for p in range(7):
                    B[nxt][p, x + 1, here, :] = new[p]
                stage_sol_tile(nxt, x, h, new, packed, trip)
                factor = (0.5 * solute_omega) * level * (1.0 / density)
                speed = u[0] * u[0] + u[1] * u[1] + u[2] * u[2]
                saved = [factor * mx, factor * my, factor * mz, factor * along]
                for i, v in enumerate(saved + u + [1.0 + 1.5 * speed]):
                    PU[i, x, pl.ds(8 * h, 8), :] = v
            return tuple(pltpu.roll(v, D - 1, 1) for v in halo), tuple(packed)

        _, packed = over_x(body, (tuple(halo), blank), U_SOL)
        stage_sol(nxt, nxt, packed)

    def flow_tile(cur, x, h, sign=1.0):
        start = Y0 + 8 * h

        def read(p):
            c = FLOW_DIRS[p]
            rows = pl.ds(start + c[1], 8)
            here = A[cur][p, x + 1 + c[0], rows, :]
            if c == (0, 0, 0):
                return here
            if c[2]:
                s = side(c[2])
                here = pltpu.roll(here, D - 1 if s == 0 else 1, 1)
                lift = FACE[2][s].index(p) * SPAN + 1 + c[0]
                halo = ZR[s, x, pl.ds(8 * h + 1 + c[1], 8), :]
                halo = pltpu.roll(halo, D - lift, 1) if lift else halo
                here = jnp.where(edge[s], halo, here)
                flag = S[1 + s, x + 1 + c[0], rows, :]
            else:
                flag = S[0, x + 1 + c[0], rows, :]
            back = A[cur][OPP[p], x + 1, pl.ds(start, 8), :]
            return jnp.where(flag > 0.5, back, here)

        part = pl.ds(8 * h, 8)
        px, py, pz, along, ux, uy, uz, stretch = [PU[i, x, part, :] for i in range(8)]
        g = [read(p) for p in range(NF)]
        a = [g[p] + g[p + 1] for p in range(1, NF, 2)]
        d = [g[p] - g[p + 1] for p in range(1, NF, 2)]
        ax, ay, az = 2.0 * a[0], 2.0 * a[1], 2.0 * a[2]
        sxy_, sxz_, syz_ = a[3] + a[4], a[5] + a[6], a[7] + a[8]
        qxy, qxz, qyz = a[3] - a[4], a[5] - a[6], a[7] - a[8]
        qxx, qyy, qzz = ax + sxy_ + sxz_, ay + sxy_ + syz_, az + sxz_ + syz_
        total = 12.0 * g[0] + (qxx + ay + az) + syz_
        jx = 2.0 * d[0] + (d[3] + d[4]) + (d[5] + d[6])
        jy = 2.0 * d[1] + (d[3] - d[4]) + (d[7] + d[8])
        jz = 2.0 * d[2] + (d[5] - d[6]) + (d[7] - d[8])
        vx = qxx * ux + qxy * uy + qxz * uz
        vy = qxy * ux + qyy * uy + qyz * uz
        vz = qxz * ux + qyz * uy + qzz * uz
        quad = vx * ux + vy * uy + vz * uz
        w = sign * flow_omega / 36.0
        if sign < 0:
            px, py, pz, along = -px, -py, -pz, -along
        scalar = w * (total * stretch - 4.5 * quad) - along
        tx_ = (3.0 * w) * (jx + 3.0 * vx - ux * total) + px
        ty_ = (3.0 * w) * (jy + 3.0 * vy - uy * total) + py
        tz_ = (3.0 * w) * (jz + 3.0 * vz - uz * total) + pz
        rest = sign * (1.0 - flow_omega)
        new = [rest * g[0] + scalar]
        pairs = [tx_, ty_, tz_, tx_ + ty_, tx_ - ty_, tx_ + tz_, tx_ - tz_, ty_ + tz_, ty_ - tz_]
        for i, v in enumerate(pairs):
            p = 1 + 2 * i
            new.append(rest * g[p] + (scalar + v))
            new.append(rest * g[p + 1] + (scalar - v))
        return new

    solute_step(0, 0)
    send_sol(1)

    def outer_slabs(k):
        return [x for x in range(WX) if x < OUTER[k] or x >= WX - OUTER[k]]

    def flow_phase(k, phase):
        cur = k % 2
        nxt = 1 - cur
        span = (OUTER[k], WX // 2) if phase else (0, OUTER[k])

        def body(i, packed):
            packed = list(packed)
            for b in (0, 1):
                x = WX - 1 - i if b else i
                for h in range(H):
                    if k < steps - 1:
                        new = flow_tile(cur, x, h)
                        for p in range(NF):
                            A[nxt][p, x + 1, pl.ds(Y0 + 8 * h, 8), :] = new[p]
                        stage_tile(nxt, i, b, h, new, packed, span[1])
                    else:
                        new = flow_tile(cur, x, h, -1.0)
                        part = pl.ds(8 * h, 8)
                        here = pl.ds(Y0 + 8 * h, 8)
                        keep = (S[0, x + 1, here, :] < 0.5) & (lane <= top)
                        for p in range(NF):
                            oflow[p, x, part, :] = jnp.where(keep, new[p], 0.0)
                        for p in range(NP - NF):
                            osol[p, x, part, :] = jnp.where(
                                keep, -B[steps % 2][p, x + 1, here, :], 0.0
                            )
            return tuple(packed)

        if k == steps - 1:
            lax.fori_loop(span[0], span[1], lambda i, c: (body(i, ()), c)[1], 0)
            return
        packed = lax.fori_loop(span[0], span[1], body, blank * 2)
        stage_flow(nxt, False, nxt, packed, phase)
        send_flow(nxt, False, phase, span)

    for k in range(steps):
        slot = k % 2
        outer = outer_slabs(k)
        if k:
            wait_flow(slot, False, 0, (0, OUTER[k - 1]), outer)
        flow_phase(k, 0)
        if k:
            inner = [x for x in range(WX) if x not in outer]
            wait_flow(slot, False, 1, (OUTER[k - 1], WX // 2), inner)
        flow_phase(k, 1)
        if k < steps - 1:
            solute_step(k + 1, 1 - slot)
            if k < steps - 2:
                send_sol(slot)


def solution(mesh):
    names = ("gx", "gy", "gz")
    sizes = tuple(mesh.shape[a] for a in names)

    def per_device(flow, solute, rho, vel, lev, solid, owner):
        WX, WY, D = solid.shape
        steps = rho.shape[0]
        f32 = jnp.float32
        V = pltpu.VMEM
        DMA = pltpu.SemaphoreType.DMA
        hbm = pl.BlockSpec(memory_space=pltpu.HBM)
        n = len(NBR) + len(INNER) + len(FACES)
        faces = [
            V((2, 2, NQ + 1, WY, D), f32),
            V((2, 2, NQ + 1, WX, 1, D), f32),
            V((2, 2, 2, WY, D), f32),
            V((2, 4, 2, 1, D), f32),
            V((2, 4, 1, D), f32),
            V((2, 2, 4, 1, D), f32),
        ]
        sides = [V((2, 2, WY, D), f32), V((2, 2, WX, D), f32), V((2, 2, WY, D), f32)]
        minus_flow, minus_sol = pl.pallas_call(
            functools.partial(kernel, sizes, steps),
            out_shape=(
                pltpu.VMEM(flow.shape, f32),
                pltpu.VMEM(solute.shape, f32),
            ),
            in_specs=[pl.BlockSpec(memory_space=pltpu.SMEM)] + [hbm] * 6,
            out_specs=(pl.BlockSpec(memory_space=pltpu.VMEM),) * 2,
            scratch_shapes=[
                V((NF, WX + 2, WY + 16, D), f32),
                V((NF, WX + 2, WY + 16, D), f32),
                V((NP - NF, WX + 2, WY + 16, D), f32),
                V((NP - NF, WX + 2, WY + 16, D), f32),
                V((3, WX + 2, WY + 16, D), f32),
                V((2, WY + 16, D), f32),
                V((2, WX, WY + 8, D), f32),
                V((8, WX, WY, D), f32),
                V(rho.shape, rho.dtype),
                V(vel.shape, vel.dtype),
                V(lev.shape, lev.dtype),
                V(solid.shape, solid.dtype),
            ]
            + (faces + sides) * 2
            + [DMA((9,)), DMA((n,)), DMA((2, n))],
            compiler_params=pltpu.CompilerParams(
                collective_id=0, has_side_effects=True, vmem_limit_bytes=60 * 2**20
            ),
        )(owner, flow, solute, rho, vel, lev, solid)
        return -minus_flow, -minus_sol

    field = P(None, "gx", "gy", "gz")
    return jax.shard_map(
        per_device,
        mesh=mesh,
        in_specs=(field, field, field, P(None, None, "gx", "gy", "gz"), field, P("gx", "gy", "gz"), P()),
        out_specs=(field, field),
        check_vma=False,
    )
```

```python
import functools

import jax
import jax.numpy as jnp
from jax import lax
from jax.experimental import pallas as pl
from jax.experimental.pallas import tpu as pltpu
from jax.sharding import PartitionSpec as P

MESH = pl.DeviceIdType.MESH
BZC = 16

FLOW_DIRS = [
    (0, 0, 0),
    (1, 0, 0),
    (-1, 0, 0),
    (0, 1, 0),
    (0, -1, 0),
    (0, 0, 1),
    (0, 0, -1),
    (1, 1, 0),
    (-1, -1, 0),
    (1, -1, 0),
    (-1, 1, 0),
    (1, 0, 1),
    (-1, 0, -1),
    (1, 0, -1),
    (-1, 0, 1),
    (0, 1, 1),
    (0, -1, -1),
    (0, 1, -1),
    (0, -1, 1),
]
NF = 19
NP = NF + 7
OPP = [FLOW_DIRS.index((-c[0], -c[1], -c[2])) for c in FLOW_DIRS]
flow_omega = 1.25
solute_omega = 1.6
langmuir_rate = 0.05

FACE = [[[p for p in range(NF) if FLOW_DIRS[p][a] == s] for s in (1, -1)] for a in range(3)]
NQ = 5
SPAN = 18
FACES = FLOW_DIRS[1:7]
NBR = [c for c in FLOW_DIRS[1:] if c[2] and c[0]]
NBR += [c for c in FLOW_DIRS[1:] if c[2] and c[1]]
NBR += [c for c in FLOW_DIRS[1:] if c[2] and not c[0] and not c[1]]
NBR += [c for c in FLOW_DIRS[1:] if not c[2] and not (c[0] and c[1])]
NBR += [c for c in FLOW_DIRS[1:] if c[0] and c[1]]
XY = [c for c in NBR if c[0] and c[1]]
XZ = [c for c in NBR if c[0] and c[2]]
YZ = [c for c in NBR if c[1] and c[2]]
FLAT = [c for c in NBR if not c[2]]
INNER = [c for c in NBR if not c[0]]
UPDOWN = [c for c in NBR if c[2]]
U_SOL = 4
OUTER = (5, 4, 3, 2)
Y0 = 8


def side(step):
    return 0 if step > 0 else 1


def axis(c):
    return [i for i in range(3) if c[i]][0]


def neg(c):
    return (-c[0], -c[1], -c[2])


def kernel(
    sizes,
    steps,
    owner_ref,
    flow_hbm,
    sol_hbm,
    rho_hbm,
    vel_hbm,
    lev_hbm,
    solid_hbm,
    oflow,
    osol,
    A0,
    A1,
    B0,
    B1,
    S,
    Zf,
    ZR,
    PU,
    rho,
    vel,
    lev,
    solid,
    sx,
    sy,
    sz,
    sxy,
    sxz,
    syz,
    tx,
    ty,
    tz,
    rx,
    ry,
    rz,
    rxy,
    rxz,
    ryz,
    ux,
    uy,
    uz,
    in_sem,
    send_sem,
    recv_sem,
):
    WX, WY, D = solid.shape
    H = WY // 8
    A, B = (A0, A1), (B0, B1)
    names = ("gx", "gy", "gz")
    me = tuple(lax.axis_index(a) for a in names)

    inside = (pl.ds(1, WX), pl.ds(Y0, WY), slice(None))
    copies = [pltpu.make_async_copy(solid_hbm, solid, in_sem.at[0])]
    cuts = (0, 5, 10, 15, NF)
    for i, (lo, hi) in enumerate(zip(cuts, cuts[1:])):
        part = pl.ds(lo, hi - lo)
        copies.append(
            pltpu.make_async_copy(flow_hbm.at[part], A0.at[(part,) + inside], in_sem.at[1 + i])
        )
    copies.append(pltpu.make_async_copy(sol_hbm, B0.at[(slice(None),) + inside], in_sem.at[5]))
    copies.append(pltpu.make_async_copy(lev_hbm, lev, in_sem.at[6]))
    copies.append(pltpu.make_async_copy(vel_hbm, vel, in_sem.at[7]))
    copies.append(pltpu.make_async_copy(rho_hbm, rho, in_sem.at[8]))
    for c in copies:
        c.start()

    def exists(c):
        ok = None
        for a in range(3):
            if c[a] > 0:
                t = me[a] < sizes[a] - 1
            elif c[a] < 0:
                t = me[a] > 0
            else:
                continue
            ok = t if ok is None else jnp.logical_and(ok, t)
        return ok

    def device(c):
        return tuple(me[a] + c[a] for a in range(3))

    barrier = pltpu.get_barrier_semaphore()
    for c in NBR:

        @pl.when(exists(c))
        def _(c=c):
            pl.semaphore_signal(barrier, inc=1, device_id=device(c), device_id_type=MESH)

    count = jnp.int32(0)
    for i in range(owner_ref.shape[0]):
        count = count + (owner_ref[i] == me[2]).astype(jnp.int32)
    top = count * BZC - 1

    lane = lax.broadcasted_iota(jnp.int32, (8, D), 1)
    row = lax.broadcasted_iota(jnp.int32, (8, D), 0)
    edge = (lane == top, lane == 0)
    last_column = SPAN - 2
    slot_lane = (lane, lax.rem(lane - top + 2 * D, D))

    def flow_refs(c, slot, first, phase=0, span=None):
        nq = NQ + 1 if first else NQ
        if c in XY:
            part = (slot, XY.index(c), pl.ds(0, nq - NQ + 1))
            return sxy.at[part], rxy.at[part]
        if c in XZ:
            part = (slot, XZ.index(c))
            return sxz.at[part], rxz.at[part]
        if c in YZ:
            part = (slot, phase, YZ.index(c))
            return syz.at[part], ryz.at[part]
        a = axis(c)
        if a == 2:
            part = (slot, phase, side(c[a]))
            return sz.at[part], rz.at[part]
        part = (slot, side(c[a]), pl.ds(0, nq))
        if a == 0:
            return sx.at[part], rx.at[part]
        part = part + (pl.ds(2 * span[0], 2 * (span[1] - span[0])),)
        return sy.at[part], ry.at[part]

    def flow_message(c, slot, first, phase, span):
        src, dst = flow_refs(c, slot, first, phase, span)
        i = INNER.index(c) + len(NBR) if phase else NBR.index(c)
        return pltpu.make_async_remote_copy(
            src_ref=src,
            dst_ref=dst,
            send_sem=send_sem.at[i],
            recv_sem=recv_sem.at[slot, i],
            device_id=device(neg(c)),
            device_id_type=MESH,
        )

    def sol_message(c, slot):
        a = axis(c)
        part = (slot, side(c[a]))
        i = len(NBR) + len(INNER) + FACES.index(c)
        return pltpu.make_async_remote_copy(
            src_ref=(tx, ty, tz)[a].at[part],
            dst_ref=(ux, uy, uz)[a].at[part],
            send_sem=send_sem.at[i],
            recv_sem=recv_sem.at[slot, i],
            device_id=device(neg(c)),
            device_id_type=MESH,
        )

    def each(table, there, act):
        for c in table:

            @pl.when(exists(there(c)))
            def _(c=c):
                act(c)

    same = lambda c: c

    def send_flow(slot, first, phase, span):
        table = INNER if phase else NBR
        each(table, neg, lambda c: flow_message(c, slot, first, phase, span).start())

    def wait_flow(slot, first, phase, span, xs):
        table = INNER if phase else NBR
        each(table, neg, lambda c: flow_message(c, slot, first, phase, span).wait_send())
        flat = [c for c in table if not c[2]]
        each(flat, same, lambda c: flow_message(c, slot, first, phase, span).wait_recv())
        merge_flat(slot, first, slot, phase, span)
        far = [c for c in table if c[2]]
        each(far, same, lambda c: flow_message(c, slot, first, phase, span).wait_recv())
        merge_z(slot, first, phase, xs)

    def send_sol(slot):
        each(FACES, neg, lambda c: sol_message(c, slot).start())

    def wait_sol(slot):
        each(FACES, neg, lambda c: sol_message(c, slot).wait_send())
        each(FACES, same, lambda c: sol_message(c, slot).wait_recv())

    def clear_missing():
        for c in NBR:

            @pl.when(jnp.logical_not(exists(c)))
            def _(c=c):
                for k in range(2):
                    refs = [flow_refs(c, k, True, f, (0, WX // 2))[1] for f in (0, 1)]
                    if c in FACES:
                        refs.append((ux, uy, uz)[axis(c)].at[k, side(c[axis(c)])])
                    for ref in refs:
                        ref[...] = jnp.zeros(ref.shape, ref.dtype)

    def over_x(body, init, unroll):
        def trip(i, carry):
            for j in range(unroll):
                carry = body(unroll * i + j, carry, j, unroll)
            return carry

        return lax.fori_loop(0, WX // unroll, trip, init)

    def edge_row(value, s):
        return value[0:1] if s == 0 else value[7:8]

    def pack(acc, s, values, j, unroll):
        if j == 0:
            acc = pltpu.roll(acc, D - unroll, 1)
        return put_lanes(acc, s, values, last_column - (unroll - 1 - j))

    def put_lanes(acc, s, values, at):
        for q, value in enumerate(values):
            moved = pltpu.roll(value, q * SPAN + at, 1)
            acc = jnp.where(slot_lane[s] == q * SPAN + at, moved, acc)
        return acc

    def settle(face, s):
        return face if s == 0 else pltpu.roll(face, D - top, 1)

    def stage_flow(slot, first, cur, packed, phase):
        for s in (0, 1):
            low, high = packed[: 2 * H], packed[2 * H :]
            face = [settle(low[s * H + h] + high[s * H + h], s) for h in range(H)]
            for h in range(H):
                sz[slot, phase, s, pl.ds(8 * h, 8), :] = face[h]
            for d, c in enumerate(YZ):
                if side(c[2]) == s:
                    syz[slot, phase, d] = face[0][0:1] if c[1] > 0 else face[H - 1][7:8]
            if phase:
                continue
            for d, c in enumerate(XZ):
                if side(c[2]) == s:
                    column = 1 if c[0] > 0 else WX
                    q = FACE[2][s].index(FLOW_DIRS.index(c))
                    line = jnp.zeros((8, D), jnp.float32)
                    for at, qz in enumerate((q, NQ) if first else (q,)):
                        i = qz * SPAN + column
                        for h in range(H):
                            value = jnp.broadcast_to(face[h][:, i : i + 1], (8, D))
                            line = jnp.where(lane == row + (WY * at + 8 * h), value, line)
                    sxz[slot, d] = jnp.sum(line, axis=0, keepdims=True)
        if phase:
            return
        for s in (0, 1):
            x = 1 if s == 0 else WX
            for q, p in enumerate(FACE[0][s]):
                sx[slot, s, q] = A[cur][p, x, pl.ds(Y0, WY), :]
            if first:
                sx[slot, s, NQ] = S[0, x, pl.ds(Y0, WY), :]
        for d, c in enumerate(XY):
            q = FACE[1][side(c[1])].index(FLOW_DIRS.index(c))
            r = 0 if c[0] > 0 else 1
            sxy[slot, d, 0] = sy[slot, side(c[1]), q, r]
            if first:
                sxy[slot, d, 1] = sy[slot, side(c[1]), NQ, r]

    def column_of(line, start):
        line = jnp.broadcast_to(line, (8, D))
        return jnp.sum(jnp.where(lane == row + start, line, 0.0), axis=1, keepdims=True)

    def merge_flat(slot, first, cur, phase, span):
        flag = [(NQ, None)] if first else []

        def put(p, x, rows, value):
            if p is None:
                S[0, x, rows, :] = value
            else:
                A[cur][p, x, rows, :] = value

        for s in (0, 1):
            if not phase:
                x = WX + 1 if s == 0 else 0
                for q, p in list(enumerate(FACE[0][s])) + flag:
                    put(p, x, pl.ds(Y0, WY), rx[slot, s, q])
            y = Y0 + WY if s == 0 else Y0 - 1
            for q, p in list(enumerate(FACE[1][s])) + flag:
                for r in range(2 * span[0], 2 * span[1]):
                    x = WX - 1 - r // 2 if r % 2 else r // 2
                    put(p, 1 + x, pl.ds(y, 1), ry[slot, s, q, r])
        if phase:
            return
        for d, c in enumerate(XY):
            x = WX + 1 if c[0] > 0 else 0
            y = Y0 + WY if c[1] > 0 else Y0 - 1
            put(FLOW_DIRS.index(c), x, pl.ds(y, 1), rxy[slot, d, 0])
            if first:
                put(None, x, pl.ds(y, 1), rxy[slot, d, 1])

    def merge_z(slot, first, phase, xs):
        for s in (0, 1):
            cz = 1 - 2 * s
            turn = (lambda v: pltpu.roll(v, top, 1)) if s == 0 else (lambda v: v)
            for h in range(H):
                part = pl.ds(Y0 + 8 * h, 8)
                face = rz[slot, phase, s, pl.ds(8 * h, 8), :]
                if not phase:
                    for cx in (1, -1):
                        c = (cx, 0, cz)
                        q = FACE[2][s].index(FLOW_DIRS.index(c))
                        for at, qz in enumerate((q, NQ) if first else (q,)):
                            value = column_of(rxz[slot, XZ.index(c)], WY * at + 8 * h)
                            i = qz * SPAN + (WX + 1 if cx > 0 else 0)
                            face = jnp.where(lane == i, value, face)
                    Zf[s, part, :] = turn(face)
                else:
                    Zf[s, part, :] = Zf[s, part, :] + turn(face)
            for y, cy in ((Y0 + WY, 1), (Y0 - 1, -1)):
                line = jnp.broadcast_to(ryz[slot, phase, YZ.index((0, cy, cz))], (8, D))
                line = turn(line)[0:1]
                Zf[s, pl.ds(y, 1), :] = Zf[s, pl.ds(y, 1), :] + line if phase else line
            for t in range(3):
                face = Zf[s, pl.ds(Y0 - 1 + 8 * t, 8), :]
                for x in xs:
                    ZR[s, x, pl.ds(8 * t, 8), :] = pltpu.roll(face, D - x, 1) if x else face

    for c in copies[:6]:
        c.wait()

    zero = jnp.zeros((8, D), jnp.float32)
    for s in (0, 1):
        for part in range(0, WY + 16, 8):
            Zf[s, pl.ds(part, 8), :] = zero
    for part in (0, Y0 + WY):
        for x in range(WX + 2):
            S[0, x, pl.ds(part, 8), :] = zero

    blank = (zero,) * (2 * H)

    def stage_tile(slot, i, b, h, values, packed, end, flag=None):
        extra = [] if flag is None else [flag]
        for s in (0, 1):
            if h == (0 if s == 0 else H - 1):
                for q, value in enumerate([values[p] for p in FACE[1][s]] + extra):
                    sy[slot, s, q, 2 * i + b] = edge_row(value, s)
            at = b * 2 * H + s * H + h
            acc = pltpu.roll(packed[at], 1 if b else D - 1, 1)
            values_z = [values[p] for p in FACE[2][s]] + extra
            packed[at] = put_lanes(acc, s, values_z, WX + 1 - end if b else end)

    def stage_sol_tile(slot, x, h, values, packed, trip):
        for s in (0, 1):
            if h == (0 if s == 0 else H - 1):
                ty[slot, s, pl.ds(x, 1), :] = edge_row(values[3 + s], s)
            i = s * H + h
            packed[i] = pack(packed[i], s, [values[5 + s]], *trip)

    def stage_sol(slot, cur, packed):
        for s in (0, 1):
            for h in range(H):
                tz[slot, s, pl.ds(8 * h, 8), :] = settle(packed[s * H + h], s)
            tx[slot, s] = B[cur][1 + s, 1 if s == 0 else WX, pl.ds(Y0, WY), :]

    class Tiles:
        def __init__(self, ref, x, part):
            self.ref, self.x, self.part = ref, x, part

        def __getitem__(self, p):
            return self.ref[p, self.x + 1, self.part, :]

    def first_stage(i, packed):
        packed = list(packed)
        for b in (0, 1):
            x = WX - 1 - i if b else i
            flags = solid[x].astype(jnp.float32)
            S[0, x + 1, pl.ds(Y0, WY), :] = flags
            for h in range(H):
                part = pl.ds(Y0 + 8 * h, 8)
                flag = flags[8 * h : 8 * h + 8]
                stage_tile(0, i, b, h, Tiles(A0, x, part), packed, WX // 2, flag)
        return tuple(packed)

    def first_sol(x, other, *trip):
        other = list(other)
        for h in range(H):
            stage_sol_tile(0, x, h, Tiles(B0, x, pl.ds(Y0 + 8 * h, 8)), other, trip)
        return tuple(other)

    whole = (0, WX // 2)
    packed = lax.fori_loop(0, WX // 2, first_stage, blank * 2)
    stage_flow(0, True, 0, packed, 0)
    n = [
        (me[a] > 0).astype(jnp.int32) + (me[a] < sizes[a] - 1).astype(jnp.int32) for a in range(3)
    ]
    pl.semaphore_wait(
        barrier, n[0] + n[1] + n[2] + n[0] * n[1] + n[0] * n[2] + n[1] * n[2]
    )
    send_flow(0, True, 0, whole)
    other = over_x(first_sol, blank, 4)
    stage_sol(0, 0, other)
    send_sol(0)
    clear_missing()
    for c in copies[6:]:
        c.wait()
    def saved_tiles(t, x):
        level_ = lev[t, x].astype(jnp.float32)
        density_ = rho[t, x].astype(jnp.float32)
        u_ = [vel[t, i, x].astype(jnp.float32) for i in range(3)]
        for h in range(H):
            cut = slice(8 * h, 8 * h + 8)
            level, density, u = level_[cut], density_[cut], [v[cut] for v in u_]
            one = 1.0 + level
            sink = solute_omega - langmuir_rate / (one * one)
            factor = (0.5 * solute_omega) * level * (1.0 / density)
            speed = u[0] * u[0] + u[1] * u[1] + u[2] * u[2]
            yield sink, factor, u, 1.0 + 1.5 * speed

    def prepare(x, carry, *trip):
        for h, (sink, factor, u, stretch) in enumerate(saved_tiles(steps - 1, x)):
            for i, v in zip((0, 3, 4, 5, 6, 7), [sink, factor] + u + [stretch]):
                PU[i, x, pl.ds(8 * h, 8), :] = v
        return carry

    def solute_step(j, slot):
        t = steps - 1 - j
        cur = slot
        nxt = 1 - slot
        wait_sol(slot)
        for s in (0, 1):
            B[cur][1 + s, WX + 1 if s == 0 else 0, pl.ds(Y0, WY), :] = ux[slot, s]
            y = Y0 + WY if s == 0 else Y0 - 1
            for half in range(WX // 8):
                value = uy[slot, s, pl.ds(8 * half, 8), :]
                for i in range(8):
                    B[cur][3 + s, 1 + 8 * half + i, pl.ds(y, 1), :] = value[i : i + 1]
        halo = []
        for s in (0, 1):
            for h in range(H):
                face = uz[slot, s, pl.ds(8 * h, 8), :]
                halo.append(pltpu.roll(face, top - 1 if s == 0 else D - 1, 1))

        def body(x, carry, *trip):
            halo, packed = list(carry[0]), list(carry[1])
            if j:
                saved = list(saved_tiles(t, x))
            else:
                parts = [pl.ds(8 * h, 8) for h in range(H)]
                saved = [
                    (PU[0, x, r, :], PU[3, x, r, :], [PU[4 + i, x, r, :] for i in range(3)], None)
                    for r in parts
                ]
            for h, (sink, factor, u, stretch) in enumerate(saved):
                start = Y0 + 8 * h
                here = pl.ds(start, 8)
                hs = [B[cur][0, x + 1, here, :]]
                for p in range(1, 7):
                    c = FLOW_DIRS[p]
                    rows = pl.ds(start + c[1], 8)
                    value = B[cur][p, x + 1 + c[0], rows, :]
                    if c[2]:
                        s = side(c[2])
                        value = pltpu.roll(value, D - 1 if s == 0 else 1, 1)
                        value = jnp.where(edge[s], halo[s * H + h], value)
                        flag = S[1 + s, x + 1, here, :]
                    else:
                        flag = S[0, x + 1 + c[0], rows, :]
                    hs.append(jnp.where(flag > 0.5, B[cur][OPP[p], x + 1, here, :], value))
                mx, my, mz = hs[1] - hs[2], hs[3] - hs[4], hs[5] - hs[6]
                m0 = 0.25 * hs[0] + 0.125 * ((hs[1] + hs[2]) + (hs[3] + hs[4]) + (hs[5] + hs[6]))
                along = mx * u[0] + my * u[1] + mz * u[2]
                common = sink * m0 + (solute_omega * 0.5) * along
                new = [(1.0 - solute_omega) * v + common for v in hs]
                for p in range(7):
                    B[nxt][p, x + 1, here, :] = new[p]
                stage_sol_tile(nxt, x, h, new, packed, trip)
                out = [factor * mx, factor * my, factor * mz, factor * along]
                for i, v in enumerate(out + u + [stretch] if j else out):
                    PU[i, x, pl.ds(8 * h, 8), :] = v
            return tuple(pltpu.roll(v, D - 1, 1) for v in halo), tuple(packed)

        _, packed = over_x(body, (tuple(halo), blank), U_SOL)
        stage_sol(nxt, nxt, packed)

    over_x(prepare, 0, 4)
    own = [(x + 1, Y0 + 8 * h) for x in range(WX) for h in range(H)]
    for x, t in own:
        part = pl.ds(t, 8)
        for s in (0, 1):
            S[1 + s, x, part, :] = pltpu.roll(S[0, x, part, :], D - 1 if s == 0 else 1, 1)
    wait_flow(0, True, 0, whole, range(WX))
    for x in range(WX + 2):
        for t in range(0, WY + 16, 8):
            part = pl.ds(t, 8)
            flag = S[0, x, part, :]
            for s in (0, 1):
                halo = pltpu.roll(Zf[s, part, :], D - (NQ * SPAN + x), 1)
                if (x, t) in own:
                    moved = S[1 + s, x, part, :]
                else:
                    moved = pltpu.roll(flag, D - 1 if s == 0 else 1, 1)
                S[1 + s, x, part, :] = jnp.where(edge[s], halo, moved)

    def flow_tile(cur, x, h, sign=1.0):
        start = Y0 + 8 * h

        def read(p):
            c = FLOW_DIRS[p]
            rows = pl.ds(start + c[1], 8)
            here = A[cur][p, x + 1 + c[0], rows, :]
            if c == (0, 0, 0):
                return here
            if c[2]:
                s = side(c[2])
                here = pltpu.roll(here, D - 1 if s == 0 else 1, 1)
                lift = FACE[2][s].index(p) * SPAN + 1 + c[0]
                halo = ZR[s, x, pl.ds(8 * h + 1 + c[1], 8), :]
                halo = pltpu.roll(halo, D - lift, 1) if lift else halo
                here = jnp.where(edge[s], halo, here)
                flag = S[1 + s, x + 1 + c[0], rows, :]
            else:
                flag = S[0, x + 1 + c[0], rows, :]
            back = A[cur][OPP[p], x + 1, pl.ds(start, 8), :]
            return jnp.where(flag > 0.5, back, here)

        part = pl.ds(8 * h, 8)
        px, py, pz, along, ux, uy, uz, stretch = [PU[i, x, part, :] for i in range(8)]
        g = [read(p) for p in range(NF)]
        a = [g[p] + g[p + 1] for p in range(1, NF, 2)]
        d = [g[p] - g[p + 1] for p in range(1, NF, 2)]
        ax, ay, az = 2.0 * a[0], 2.0 * a[1], 2.0 * a[2]
        sxy_, sxz_, syz_ = a[3] + a[4], a[5] + a[6], a[7] + a[8]
        qxy, qxz, qyz = a[3] - a[4], a[5] - a[6], a[7] - a[8]
        qxx, qyy, qzz = ax + sxy_ + sxz_, ay + sxy_ + syz_, az + sxz_ + syz_
        total = 12.0 * g[0] + (qxx + ay + az) + syz_
        jx = 2.0 * d[0] + (d[3] + d[4]) + (d[5] + d[6])
        jy = 2.0 * d[1] + (d[3] - d[4]) + (d[7] + d[8])
        jz = 2.0 * d[2] + (d[5] - d[6]) + (d[7] - d[8])
        vx = qxx * ux + qxy * uy + qxz * uz
        vy = qxy * ux + qyy * uy + qyz * uz
        vz = qxz * ux + qyz * uy + qzz * uz
        quad = vx * ux + vy * uy + vz * uz
        w = sign * flow_omega / 36.0
        if sign < 0:
            px, py, pz, along = -px, -py, -pz, -along
        scalar = w * (total * stretch - 4.5 * quad) - along
        tx_ = (3.0 * w) * (jx + 3.0 * vx - ux * total) + px
        ty_ = (3.0 * w) * (jy + 3.0 * vy - uy * total) + py
        tz_ = (3.0 * w) * (jz + 3.0 * vz - uz * total) + pz
        rest = sign * (1.0 - flow_omega)
        new = [rest * g[0] + scalar]
        pairs = [tx_, ty_, tz_, tx_ + ty_, tx_ - ty_, tx_ + tz_, tx_ - tz_, ty_ + tz_, ty_ - tz_]
        for i, v in enumerate(pairs):
            p = 1 + 2 * i
            new.append(rest * g[p] + (scalar + v))
            new.append(rest * g[p + 1] + (scalar - v))
        return new

    solute_step(0, 0)
    send_sol(1)

    def outer_slabs(k):
        return [x for x in range(WX) if x < OUTER[k] or x >= WX - OUTER[k]]

    def flow_phase(k, phase):
        cur = k % 2
        nxt = 1 - cur
        span = (OUTER[k], WX // 2) if phase else (0, OUTER[k])

        def body(i, packed):
            packed = list(packed)
            for b in (0, 1):
                x = WX - 1 - i if b else i
                for h in range(H):
                    if k < steps - 1:
                        new = flow_tile(cur, x, h)
                        for p in range(NF):
                            A[nxt][p, x + 1, pl.ds(Y0 + 8 * h, 8), :] = new[p]
                        stage_tile(nxt, i, b, h, new, packed, span[1])
                    else:
                        new = flow_tile(cur, x, h, -1.0)
                        part = pl.ds(8 * h, 8)
                        here = pl.ds(Y0 + 8 * h, 8)
                        keep = (S[0, x + 1, here, :] < 0.5) & (lane <= top)
                        for p in range(NF):
                            oflow[p, x, part, :] = jnp.where(keep, new[p], 0.0)
                        for p in range(NP - NF):
                            osol[p, x, part, :] = jnp.where(
                                keep, -B[steps % 2][p, x + 1, here, :], 0.0
                            )
            return tuple(packed)

        if k == steps - 1:
            lax.fori_loop(span[0], span[1], lambda i, c: (body(i, ()), c)[1], 0)
            return
        packed = lax.fori_loop(span[0], span[1], body, blank * 2)
        stage_flow(nxt, False, nxt, packed, phase)
        send_flow(nxt, False, phase, span)

    for k in range(steps):
        slot = k % 2
        outer = outer_slabs(k)
        if k:
            wait_flow(slot, False, 0, (0, OUTER[k - 1]), outer)
        flow_phase(k, 0)
        if k:
            inner = [x for x in range(WX) if x not in outer]
            wait_flow(slot, False, 1, (OUTER[k - 1], WX // 2), inner)
        flow_phase(k, 1)
        if k < steps - 1:
            solute_step(k + 1, 1 - slot)
            if k < steps - 2:
                send_sol(slot)


def solution(mesh):
    names = ("gx", "gy", "gz")
    sizes = tuple(mesh.shape[a] for a in names)

    def per_device(flow, solute, rho, vel, lev, solid, owner):
        WX, WY, D = solid.shape
        steps = rho.shape[0]
        f32 = jnp.float32
        V = pltpu.VMEM
        DMA = pltpu.SemaphoreType.DMA
        hbm = pl.BlockSpec(memory_space=pltpu.HBM)
        n = len(NBR) + len(INNER) + len(FACES)
        faces = [
            V((2, 2, NQ + 1, WY, D), f32),
            V((2, 2, NQ + 1, WX, 1, D), f32),
            V((2, 2, 2, WY, D), f32),
            V((2, 4, 2, 1, D), f32),
            V((2, 4, 1, D), f32),
            V((2, 2, 4, 1, D), f32),
        ]
        sides = [V((2, 2, WY, D), f32), V((2, 2, WX, D), f32), V((2, 2, WY, D), f32)]
        minus_flow, minus_sol = pl.pallas_call(
            functools.partial(kernel, sizes, steps),
            out_shape=(
                pltpu.VMEM(flow.shape, f32),
                pltpu.VMEM(solute.shape, f32),
            ),
            in_specs=[pl.BlockSpec(memory_space=pltpu.SMEM)] + [hbm] * 6,
            out_specs=(pl.BlockSpec(memory_space=pltpu.VMEM),) * 2,
            scratch_shapes=[
                V((NF, WX + 2, WY + 16, D), f32),
                V((NF, WX + 2, WY + 16, D), f32),
                V((NP - NF, WX + 2, WY + 16, D), f32),
                V((NP - NF, WX + 2, WY + 16, D), f32),
                V((3, WX + 2, WY + 16, D), f32),
                V((2, WY + 16, D), f32),
                V((2, WX, WY + 8, D), f32),
                V((8, WX, WY, D), f32),
                V(rho.shape, rho.dtype),
                V(vel.shape, vel.dtype),
                V(lev.shape, lev.dtype),
                V(solid.shape, solid.dtype),
            ]
            + (faces + sides) * 2
            + [DMA((9,)), DMA((n,)), DMA((2, n))],
            compiler_params=pltpu.CompilerParams(
                collective_id=0, has_side_effects=True, vmem_limit_bytes=60 * 2**20
            ),
        )(owner, flow, solute, rho, vel, lev, solid)
        return -minus_flow, -minus_sol

    field = P(None, "gx", "gy", "gz")
    return jax.shard_map(
        per_device,
        mesh=mesh,
        in_specs=(field, field, field, P(None, None, "gx", "gy", "gz"), field, P("gx", "gy", "gz"), P()),
        out_specs=(field, field),
        check_vma=False,
    )
```
